32 devices in a mesh: slides: 2 (over y), tiles: 8 (over z, x), sub: 2 (over core).
Axes of the slice: x: 2, y: 2, z: 4, core: 2. Of those that a mesh axis runs over, the one named last changes fastest.
Arguments:
- tile_data: bfloat16 [96, 12, 12, 192], P(('slides', 'tiles'), None, None, 'sub'), parts along dimension 0, may hold values from -64 to 64
- cotangent: bfloat16 [96, 12, 12, 192], P(('slides', 'tiles'), None, None, 'sub'), parts along dimension 0, may hold values from -6 to 6
- neighbour: int32 [96, 8], P(('slides', 'tiles')), parts along dimension 0, may hold values from 0 to 47, as said below
- tissue: int32 [96, 8], P(('slides', 'tiles')), parts along dimension 0, may hold values from 0 to 1, as said below
- kernel: float32 [7, 7, 192], P(None, None, 'sub'), may hold values from -0.875 to 0.875
- conv_bias: float32 [192], P('sub'), may hold values from -3 to 3
- layer_norm_gain: float32 [192], P('sub'), may hold values from 0.5 to 2
- layer_norm_bias: float32 [192], P('sub'), may hold values from -3 to 3
- w_in: float32 [192, 768], P(None, 'sub'), may hold values from -0.4375 to 0.4375
- b_in: float32 [768], P('sub'), may hold values from -3 to 3
- w_out: float32 [768, 192], P('sub'), may hold values from -0.21875 to 0.21875
- b_out: float32 [192], P('sub'), may hold values from -3 to 3
- layer_scale: float32 [192], P('sub'), may hold values from 0.3 to 1
Outputs:
- block_out: bfloat16 [96, 12, 12, 192], P(('slides', 'tiles'), None, None, 'sub'), parts along dimension 0
- tile_grad: bfloat16 [96, 12, 12, 192], P(('slides', 'tiles'), None, None, 'sub'), parts along dimension 0
- grad_w_in: float32 [384, 768], P('slides', 'sub'), parts along dimension 0
- grad_w_out: float32 [1536, 192], P(('slides', 'sub')), parts along dimension 0
- grad_kernel: float32 [14, 7, 192], P('slides', None, 'sub'), parts along dimension 0
The draws below stay inside these ranges and needn't reach their ends.
There are 2 independent parts, one for each index of `slides`. The reference program is written for one: setup_inputs(seed, part) draws one part's arguments, and reference() takes and returns one part's arrays. A program takes and returns all parts, laid end to end along the dimension named above; an argument that names none is the same for every part. Nothing has to cross between parts.
Inputs may be any that keep to these rules, and one draw needn't show every extreme that they name: Tile t is held by index t // 6 of tiles. If neighbour[t, d] = u then neighbour[u, e] = t for the opposite side e (north and south, west and east, north-west and south-east, north-east and south-west). The index of tiles that holds neighbour[t, d] is (t // 6 + an offset that depends only on d and t % 6) % 8. Over all eight sides, the tiles of one index of tiles name tiles of any one index at most 6 times, and every index reaches 6. tissue[t, d] = tissue[neighbour[t, d], e] for the opposite side e.
All inputs are finite; a program needn't handle non-finite values.
Results may differ from the reference program's by a relative error of at most 0.0079.
Values may be sent and summed in bfloat16 or wider, within the bound.
No kernel may reach another device: no remote copies, remote signals or barrier semaphores. Data moves between devices by JAX's collectives and lax.ppermute only.
A program may use at most 64 MiB of HBM per device.

```python
import math
import jax
import jax.numpy as jnp
from jax import lax

C = 192
HID = 768
SIDE = 12
TILE_DEV = 6
OWNERS = 8
TILES = 48


def draw_tile_data(key, part):
    key_chan, key_tile, key_draw = jax.random.split(key, 3)
    channel_scale = 10.0 ** jax.random.uniform(key_chan, (C,), jnp.float32, -0.5, 0.5)
    tile_scale = 10.0 ** jax.random.uniform(key_tile, (TILES, 1, 1, 1), jnp.float32, -0.5, 0.5)
    draw_base = jnp.clip(jax.random.normal(key_draw, (TILES, SIDE, SIDE, C), jnp.float32), -6.0, 6.0)
    return (draw_base * channel_scale * tile_scale).astype(jnp.bfloat16)


def neighbour_tables(key):
    key_shift, key_slots, key_bits = jax.random.split(jax.random.fold_in(key, 11), 3)
    ordering = jax.random.permutation(key_shift, 4 * TILE_DEV).astype(jnp.int32)
    offset = ((ordering - ordering[0]) % OWNERS).reshape(4, TILE_DEV)
    slot_keys = jax.random.split(key_slots, 4)
    moved = jnp.stack([jax.random.permutation(slot_keys[pair_index], TILE_DEV).astype(jnp.int32) for pair_index in range(4)])
    reverted = jnp.argsort(moved, axis=1).astype(jnp.int32)
    device = jnp.arange(OWNERS, dtype=jnp.int32)[:, None]
    onward = []
    backward = []
    for pair_index in range(4):
        ahead = (device + offset[pair_index][None, :]) % OWNERS * TILE_DEV + moved[pair_index][None, :]
        onward.append(ahead.reshape(-1))
        back_slot = reverted[pair_index]
        behind = (device - offset[pair_index][back_slot][None, :]) % OWNERS * TILE_DEV + back_slot[None, :]
        backward.append(behind.reshape(-1))
    links_table = jnp.stack([onward[0], backward[0], onward[1], backward[1], onward[2], onward[3], backward[3], backward[2]], axis=1)
    tissue_bits = (jax.random.randint(key_bits, (4, TILES), 0, 4) > 0).astype(jnp.int32)
    tissue_table = jnp.stack([tissue_bits[0], tissue_bits[0][backward[0]], tissue_bits[1], tissue_bits[1][backward[1]], tissue_bits[2], tissue_bits[3], tissue_bits[3][backward[3]], tissue_bits[2][backward[2]]], axis=1)
    return (links_table.astype(jnp.int32), tissue_table)


def draw_neighbour(key, part):
    return neighbour_tables(key)[0]


def draw_tissue(key, part):
    return neighbour_tables(key)[1]


def levels(own_key, shape, cuts, smallest, high):
    factor_of = 1.0
    for position, parts in cuts:
        steps = jax.random.uniform(jax.random.fold_in(jax.random.fold_in(own_key, 6), position), (parts,), jnp.float32, smallest / len(cuts), high / len(cuts))
        factor_of = factor_of * jnp.repeat(jnp.exp(steps), shape[position] // parts).reshape((-1,) + (1,) * (len(shape) - 1 - position))
    return factor_of


def normal_values(stream_key, dims, scale, reach, cuts=(), kind=jnp.bfloat16):
    values = scale * jax.random.normal(stream_key, dims, jnp.float32)
    if cuts:
        values = values * levels(stream_key, dims, cuts, -0.22, 0.18)
    return jnp.clip(values, -reach, reach).astype(kind)


def setup_inputs(seed: int = 0, part: int = 0) -> dict:
    key_of = jax.random.split(jax.random.key(seed), 14)
    own_keys = jax.random.split(jax.random.fold_in(key_of[13], part), 14)
    return {
        "tile_data": draw_tile_data(jax.random.fold_in(jax.random.fold_in(key_of[13], part), 71), part),
        "cotangent": normal_values(own_keys[1], (TILES, SIDE, SIDE, C), 1.0, 6.0, ((0, 8), (3, 2))),
        "neighbour": draw_neighbour(jax.random.fold_in(jax.random.fold_in(key_of[13], part), 71), part),
        "tissue": draw_tissue(jax.random.fold_in(jax.random.fold_in(key_of[13], part), 71), part),
        "kernel": normal_values(key_of[4], (7, 7, C), 49 ** -0.5, 0.875, ((2, 2),), jnp.float32),
        "conv_bias": normal_values(key_of[5], (C,), 0.5, 3.0, ((0, 2),), jnp.float32),
        "layer_norm_gain": jnp.clip(jnp.exp(math.log(2.0) - 1.3862944 * jax.random.uniform(key_of[6], (C,), jnp.float32) ** levels(key_of[6], (C,), ((0, 2),), -0.2, 0.2)), 0.5, 2.0),
        "layer_norm_bias": normal_values(key_of[7], (C,), 0.5, 3.0, ((0, 2),), jnp.float32),
        "w_in": normal_values(key_of[8], (C, HID), C ** -0.5, 0.4375, ((1, 2),), jnp.float32),
        "b_in": normal_values(key_of[9], (HID,), 0.5, 3.0, ((0, 2),), jnp.float32),
        "w_out": normal_values(key_of[10], (HID, C), HID ** -0.5, 0.21875, ((0, 2),), jnp.float32),
        "b_out": normal_values(key_of[11], (C,), 0.5, 3.0, ((0, 2),), jnp.float32),
        "layer_scale": jnp.clip(jnp.exp(math.log(1.0) - 1.2039728 * jax.random.uniform(key_of[12], (C,), jnp.float32) ** levels(key_of[12], (C,), ((0, 2),), -0.2, 0.2)), 0.3, 1.0),
    }


eps_norm = 1e-06
root_half = 0.7071067811865476
inv_root_tau = 0.3989422804014327
side_kinds = (0, 1, 2, 3, 0, 0, 1, 1)

def edge_strip(block_data, kind_code):
    if kind_code == 0:
        return block_data[:, -3:]
    if kind_code == 1:
        return block_data[:, :3]
    if kind_code == 2:
        return jnp.swapaxes(block_data[:, :, -3:], 1, 2)
    return jnp.swapaxes(block_data[:, :, :3], 1, 2)

def assemble(inner, strips):
    top_band = jnp.concatenate([strips[:, 4][:, :, -3:], strips[:, 0], strips[:, 5][:, :, :3]], axis=2)
    low_band = jnp.concatenate([strips[:, 6][:, :, -3:], strips[:, 1], strips[:, 7][:, :, :3]], axis=2)
    mid_band = jnp.concatenate([jnp.swapaxes(strips[:, 2], 1, 2), inner, jnp.swapaxes(strips[:, 3], 1, 2)], axis=2)
    return jnp.concatenate([top_band, mid_band, low_band], axis=1)

def depthwise(field, weights):
    return lax.conv_general_dilated(field, weights[:, :, None, :], (1, 1), 'VALID', dimension_numbers=('NHWC', 'HWIO', 'NHWC'), feature_group_count=field.shape[3], precision=lax.Precision.HIGHEST)

def local_pass(grown, inner, cot_block, kernel, conv_bias, layer_norm_gain, layer_norm_bias, w_in16, b_in, w_out16, b_out, layer_scale):
    grown32 = grown.astype(jnp.float32)
    spatial = depthwise(grown32, kernel) + conv_bias
    channels = spatial.shape[3]
    flat = spatial.reshape(-1, channels)
    centre_pixel = flat - lax.optimization_barrier(jnp.mean(flat, axis=1, keepdims=True))
    spread_var = lax.optimization_barrier(jnp.mean(centre_pixel * centre_pixel, axis=1, keepdims=True))
    inverse_deviation = lax.rsqrt(spread_var + eps_norm)
    standardized_input = centre_pixel * inverse_deviation
    normed_rows = (standardized_input * layer_norm_gain + layer_norm_bias).astype(jnp.bfloat16)
    pre = jnp.dot(normed_rows, w_in16, preferred_element_type=jnp.float32) + b_in
    act = jax.nn.gelu(pre, approximate=False).astype(jnp.bfloat16)
    branch = jnp.dot(act, w_out16, preferred_element_type=jnp.float32) + b_out
    residual = inner.reshape(flat.shape).astype(jnp.float32)
    block_out = (residual + layer_scale * branch).astype(jnp.bfloat16).reshape(inner.shape)
    g_branch = (layer_scale * cot_block.reshape(flat.shape).astype(jnp.float32)).astype(jnp.bfloat16)
    g_act = jnp.dot(g_branch, w_out16.T, preferred_element_type=jnp.float32)
    slope = 0.5 * (1.0 + lax.erf(pre * root_half)) + pre * jnp.exp(-0.5 * pre * pre) * inv_root_tau
    g_pre = (g_act * slope).astype(jnp.bfloat16)
    part_out = jnp.dot(act.T, g_branch, preferred_element_type=jnp.float32)
    part_in = jnp.dot(normed_rows.T, g_pre, preferred_element_type=jnp.float32)
    g_normed = jnp.dot(g_pre, w_in16.T, preferred_element_type=jnp.float32)
    standardized_gradient = g_normed * layer_norm_gain
    flattened_gradient = inverse_deviation * (standardized_gradient - lax.optimization_barrier(jnp.mean(standardized_gradient, axis=1, keepdims=True)) - standardized_input * lax.optimization_barrier(jnp.mean(standardized_gradient * standardized_input, axis=1, keepdims=True)))
    g_conv = flattened_gradient.astype(jnp.bfloat16).reshape(spatial.shape)
    unused, pull_back = jax.vjp(lambda weights: depthwise(grown32, weights), kernel)
    part_kernel = pull_back(g_conv.astype(jnp.float32))[0]
    return (block_out, g_conv, part_in, part_out, part_kernel)

def gather_grown(field, inner, links, codes):
    pieces = []
    for direction in range(8):
        piece = edge_strip(field[links[:, direction]], side_kinds[direction])
        keep = (codes[:, direction] > 0)[:, None, None, None]
        pieces.append(jnp.where(keep, piece, jnp.zeros_like(piece)))
    return assemble(inner, jnp.stack(pieces, axis=1))

def reference(tile_data, cotangent, neighbour, tissue, kernel, conv_bias, layer_norm_gain, layer_norm_bias, w_in, b_in, w_out, b_out, layer_scale):
    w_in16 = w_in.astype(jnp.bfloat16)
    w_out16 = w_out.astype(jnp.bfloat16)
    tile_count = tile_data.shape[0]
    tile_side = tile_data.shape[1]
    channels = tile_data.shape[3]
    hidden_units = w_in.shape[1]
    block_len = math.gcd(tile_count, 32)
    step_count = tile_count // block_len
    flipped = kernel[::-1, ::-1]
    scale = 1.0 / math.sqrt(tile_count * tile_side * tile_side)

    def take(array, index):
        return lax.dynamic_slice_in_dim(array, (index * block_len).astype(jnp.int32), block_len, 0)

    def forward_step(carry, index):
        inner = take(tile_data, index)
        links = take(neighbour, index)
        codes = take(tissue, index)
        cot_block = take(cotangent, index)
        grown = gather_grown(tile_data, inner, links, codes)
        block_out, g_conv, part_in, part_out, part_kernel = local_pass(grown, inner, cot_block, kernel, conv_bias, layer_norm_gain, layer_norm_bias, w_in16, b_in, w_out16, b_out, layer_scale)
        return ((carry[0] + part_in, carry[1] + part_out, carry[2] + part_kernel), (block_out, g_conv))
    start_carry = (jnp.zeros((channels, hidden_units), jnp.float32), jnp.zeros((hidden_units, channels), jnp.float32), jnp.zeros((7, 7, channels), jnp.float32))
    indices = jnp.arange(step_count, dtype=jnp.int32)
    totals, stacked = lax.scan(forward_step, start_carry, indices)
    block_out = stacked[0].reshape(tile_data.shape)
    g_all = stacked[1].reshape(tile_data.shape)

    def backward_step(index):
        g_block = take(g_all, index)
        links = take(neighbour, index)
        codes = take(tissue, index)
        cot_block = take(cotangent, index)
        grown_grad = gather_grown(g_all, g_block, links, codes)
        total = cot_block.astype(jnp.float32) + depthwise(grown_grad.astype(jnp.float32), flipped)
        return total.astype(jnp.bfloat16)
    tile_grad = lax.map(backward_step, indices).reshape(tile_data.shape)
    return (block_out, tile_grad, totals[0] * scale, totals[1] * scale, totals[2] * scale)
```

```python
import math

import jax
import jax.numpy as jnp
from jax import lax
from jax.sharding import PartitionSpec as P

eps_norm = 1e-06
root_half = 0.7071067811865476
inv_root_tau = 0.3989422804014327


def edge_strip(block_data, kind_code):
    if kind_code == 0:
        return block_data[:, -3:]
    if kind_code == 1:
        return block_data[:, :3]
    if kind_code == 2:
        return jnp.swapaxes(block_data[:, :, -3:], 1, 2)
    return jnp.swapaxes(block_data[:, :, :3], 1, 2)


def all_strips(block_data):
    return jnp.stack([edge_strip(block_data, kind_code) for kind_code in range(4)], axis=1)


def assemble(inner, strips):
    top_band = jnp.concatenate(
        [strips[:, 4][:, :, -3:], strips[:, 0], strips[:, 5][:, :, :3]], axis=2
    )
    low_band = jnp.concatenate(
        [strips[:, 6][:, :, -3:], strips[:, 1], strips[:, 7][:, :, :3]], axis=2
    )
    mid_band = jnp.concatenate(
        [jnp.swapaxes(strips[:, 2], 1, 2), inner, jnp.swapaxes(strips[:, 3], 1, 2)], axis=2
    )
    return jnp.concatenate([top_band, mid_band, low_band], axis=1)


def depthwise(field, weights):
    return lax.conv_general_dilated(
        field,
        weights[:, :, None, :],
        (1, 1),
        "VALID",
        dimension_numbers=("NHWC", "HWIO", "NHWC"),
        feature_group_count=field.shape[3],
        precision=lax.Precision.HIGHEST,
    )


served_kind = (1, 0, 3, 2, 1, 1, 0, 0)
opposite = (1, 0, 3, 2, 7, 6, 5, 4)


def slots_of(neighbour, tile_dev, owners, capacity):
    links = neighbour.reshape(-1)
    count = links.shape[0]
    target = links // tile_dev
    offset = jnp.mod(target - lax.axis_index("tiles"), owners)
    order = jnp.arange(count, dtype=jnp.int32)
    same = offset[:, None] == offset[None, :]
    rank = jnp.sum((same & (order[None, :] < order[:, None])).astype(jnp.int32), axis=1)
    receive = target * capacity + rank
    facing = jnp.tile(jnp.array(opposite, jnp.int32), tile_dev)
    mirror = links % tile_dev * 8 + facing
    mirror_hot = mirror[:, None] == order[None, :]
    send = target * capacity + jnp.sum(jnp.where(mirror_hot, rank[None, :], 0), axis=1)
    slot = jnp.arange(owners * capacity, dtype=jnp.int32)
    fill = slot[:, None] == send[None, :]
    kinds = jnp.tile(jnp.array(served_kind, jnp.int32), tile_dev)
    which = order // 8 * 4 + kinds
    source = jnp.sum(jnp.where(fill, which[None, :], 0), axis=1)
    return receive, source


def exchange_tiles(box):
    return lax.all_to_all(box, "tiles", split_axis=0, concat_axis=0, tiled=True)


def swap_sub(piece):
    return lax.ppermute(piece, "sub", [(0, 1), (1, 0)])


def halo(block_data, receive, source, keep_side, owners, capacity):
    tile_dev, tile_side, unused, local_ch = block_data.shape
    strips = all_strips(block_data).reshape(tile_dev * 4, 3 * tile_side, local_ch)
    outbox = strips[source].reshape(owners, capacity * 3 * tile_side, local_ch)
    inbox = exchange_tiles(outbox).reshape(owners * capacity, 3, tile_side, local_ch)
    mine = inbox[receive].reshape(tile_dev, 8, 3, tile_side, local_ch)
    return assemble(block_data, jnp.where(keep_side, mine, jnp.zeros_like(mine)))


def local(
    tile_data,
    cotangent,
    neighbour,
    tissue,
    kernel,
    conv_bias,
    layer_norm_gain,
    layer_norm_bias,
    w_in,
    b_in,
    w_out,
    b_out,
    layer_scale,
):
    tile_dev, tile_side, unused, local_ch = tile_data.shape
    every_channel = w_in.shape[0]
    half_hidden = w_in.shape[1]
    owners = lax.axis_size("tiles")
    capacity = max(2, 8 * tile_dev // owners)
    half = tile_dev // 2
    scale = 1.0 / math.sqrt(owners * tile_dev * tile_side * tile_side)
    core = lax.axis_index("sub")
    first = core == 0

    def join(own, other, axis):
        return jnp.where(
            first,
            jnp.concatenate([own, other], axis=axis),
            jnp.concatenate([other, own], axis=axis),
        )

    def split(block):
        own = lax.dynamic_slice_in_dim(block, core * half, half, 0)
        other = lax.dynamic_slice_in_dim(block, (1 - core) * half, half, 0)
        return own.reshape(-1, block.shape[-1]), other.reshape(-1, block.shape[-1])

    receive, source = slots_of(neighbour, tile_dev, owners, capacity)
    keep_side = (tissue > 0)[:, :, None, None, None]
    grown = halo(tile_data, receive, source, keep_side, owners, capacity)

    w_in16 = w_in.astype(jnp.bfloat16)
    w_out16 = w_out.astype(jnp.bfloat16)
    w_in_all = jnp.concatenate([w_in16, swap_sub(w_in16)], axis=1)
    w_out_all = jnp.concatenate([w_out16, swap_sub(w_out16)], axis=0)
    b_in_all = jnp.concatenate([b_in, swap_sub(b_in)])
    vectors = jnp.stack([layer_norm_gain, layer_norm_bias, b_out, layer_scale])
    vectors = join(vectors, swap_sub(vectors), 1)
    gain, shift, b_out_all, branch_scale = vectors
    pair_own, pair_other = split(jnp.concatenate([tile_data, cotangent], axis=3))
    pair_other = swap_sub(pair_other)
    inner_rows = join(pair_own[:, :local_ch], pair_other[:, :local_ch], 1)
    cot_rows = join(pair_own[:, local_ch:], pair_other[:, local_ch:], 1)
    g_branch = (branch_scale * cot_rows.astype(jnp.float32)).astype(jnp.bfloat16)

    grown32 = grown.astype(jnp.float32)
    spatial = depthwise(grown32, kernel) + conv_bias
    spatial_own, spatial_other = split(spatial)
    flat = join(spatial_own, swap_sub(spatial_other), 1)
    centre_pixel = flat - jnp.mean(flat, axis=1, keepdims=True)
    spread_var = jnp.mean(centre_pixel * centre_pixel, axis=1, keepdims=True)
    inverse_deviation = lax.rsqrt(spread_var + eps_norm)
    standardized_input = centre_pixel * inverse_deviation
    normed = (standardized_input * gain + shift).astype(jnp.bfloat16)
    pre = jnp.dot(normed, w_in_all, preferred_element_type=jnp.float32) + b_in_all
    cdf = 0.5 * (1.0 + lax.erf(pre * root_half))
    act = (pre * cdf).astype(jnp.bfloat16)
    branch = jnp.dot(act, w_out_all, preferred_element_type=jnp.float32) + b_out_all
    block_rows = (inner_rows.astype(jnp.float32) + branch_scale * branch).astype(jnp.bfloat16)
    g_act = jnp.dot(g_branch, w_out_all.T, preferred_element_type=jnp.float32)
    slope = cdf + pre * jnp.exp(-0.5 * pre * pre) * inv_root_tau
    g_pre = (g_act * slope).astype(jnp.bfloat16)
    part_out = jnp.dot(act.T, g_branch, preferred_element_type=jnp.float32)
    part_in = jnp.dot(normed.T, g_pre, preferred_element_type=jnp.float32)
    g_normed = jnp.dot(g_pre, w_in_all.T, preferred_element_type=jnp.float32)
    standardized_gradient = g_normed * gain
    g_rows = (
        inverse_deviation
        * (
            standardized_gradient
            - jnp.mean(standardized_gradient, axis=1, keepdims=True)
            - standardized_input
            * jnp.mean(standardized_gradient * standardized_input, axis=1, keepdims=True)
        )
    ).astype(jnp.bfloat16)

    def back(rows):
        low, high = rows[:, :local_ch], rows[:, local_ch:]
        return jnp.where(first, low, high), jnp.where(first, high, low)

    g_own, g_other = back(g_rows)
    block_own, block_other = back(block_rows)
    g_other, block_other = swap_sub(g_other), swap_sub(block_other)
    tile_shape = (half,) + tile_data.shape[1:]
    g_conv = join(g_own.reshape(tile_shape), g_other.reshape(tile_shape), 0)
    block_out = join(block_own.reshape(tile_shape), block_other.reshape(tile_shape), 0)

    other_in = swap_sub(part_in[:, half_hidden:].astype(jnp.bfloat16))
    other_out = swap_sub(part_out[half_hidden:].astype(jnp.bfloat16))
    sum_in = part_in[:, :half_hidden] + other_in.astype(jnp.float32)
    sum_out = part_out[:half_hidden] + other_out.astype(jnp.float32)
    size = every_channel * half_hidden
    parts = jnp.concatenate([sum_in.reshape(owners, -1), sum_out.reshape(owners, -1)], axis=1)
    shares = exchange_tiles(parts.astype(jnp.bfloat16))
    share = jnp.sum(shares.astype(jnp.float32), axis=0).astype(jnp.bfloat16)

    g_grown = halo(g_conv, receive, source, keep_side, owners, capacity).astype(jnp.float32)
    unused, pull_back = jax.vjp(lambda weights: depthwise(grown32, weights), kernel)
    part_kernel = pull_back(g_conv.astype(jnp.float32))[0]
    message = jnp.concatenate([share, part_kernel.astype(jnp.bfloat16).reshape(-1)])
    everyone = exchange_tiles(jnp.broadcast_to(message[None], (owners,) + message.shape))
    each = size // owners
    grad_in = everyone[:, :each].reshape(w_in.shape).astype(jnp.float32) * scale
    grad_out = everyone[:, each : 2 * each].reshape(w_out.shape).astype(jnp.float32) * scale
    grad_kernel = jnp.sum(everyone[:, 2 * each :].astype(jnp.float32), axis=0) * scale
    tile_grad = cotangent.astype(jnp.float32) + depthwise(g_grown, kernel[::-1, ::-1])
    return (
        block_out,
        tile_grad.astype(jnp.bfloat16),
        grad_in,
        grad_out,
        grad_kernel.reshape(kernel.shape),
    )


def solution(mesh):
    placed = (
        P(("slides", "tiles"), None, None, "sub"),
        P(("slides", "tiles"), None, None, "sub"),
        P(("slides", "tiles"), None),
        P(("slides", "tiles"), None),
        P(None, None, "sub"),
        P("sub"),
        P("sub"),
        P("sub"),
        P(None, "sub"),
        P("sub"),
        P("sub", None),
        P("sub"),
        P("sub"),
    )
    return jax.shard_map(
        local,
        mesh=mesh,
        in_specs=placed,
        out_specs=(
            P(("slides", "tiles"), None, None, "sub"),
            P(("slides", "tiles"), None, None, "sub"),
            P("slides", "sub"),
            P(("slides", "sub"), None),
            P("slides", None, "sub"),
        ),
        check_vma=False,
    )
```

```python
import math

import jax
import jax.numpy as jnp
from jax import lax
from jax.experimental import pallas as pl
from jax.experimental.pallas import tpu as pltpu
from jax.sharding import PartitionSpec as P

eps_norm = 1e-06
root_half = 0.7071067811865476
inv_root_tau = 0.3989422804014327
served_kind = (1, 0, 3, 2, 1, 1, 0, 0)
opposite = (1, 0, 3, 2, 7, 6, 5, 4)
LANES = 128
F32 = jnp.float32
BF16 = jnp.bfloat16


def round_up(value, step):
    return -(-value // step) * step


def call(body, outs, operands, scalars=0, scratch=(), flops=0):
    spaces = [pltpu.SMEM] * scalars + [pltpu.VMEM] * (len(operands) - scalars)
    return pl.pallas_call(
        body,
        out_shape=outs,
        in_specs=[pl.BlockSpec(memory_space=space) for space in spaces],
        scratch_shapes=list(scratch),
        compiler_params=pltpu.CompilerParams(vmem_limit_bytes=48 << 20),
        cost_estimate=pl.CostEstimate(
            flops=flops,
            transcendentals=0,
            bytes_accessed=sum(o.size * o.dtype.itemsize for o in operands),
        ),
    )(*operands)


def shaped(shape, dtype):
    return jax.ShapeDtypeStruct(shape, dtype)


class Sizes:
    def __init__(self, tile_shape, hidden, owners):
        self.tiles, self.side, _, self.ch = tile_shape
        self.hidden = hidden
        self.owners = owners
        self.capacity = max(2, 8 * self.tiles // owners)
        self.pixels = self.side * self.side
        self.rows = self.pixels * self.tiles
        self.half = self.rows // 2
        self.extra = LANES - self.ch
        self.groups = self.ch // self.extra
        self.strip = 3 * self.side * self.ch // LANES
        self.tail = 3 * self.side - self.strip
        self.wide = self.side + 6
        self.box1 = round_up(self.capacity * self.strip, 16)
        self.weight_rows = 2 * (2 * self.ch) * hidden // LANES
        self.share = self.weight_rows // owners
        self.halo_at = round_up(self.share, 16)
        self.box2 = round_up(self.halo_at + self.capacity * self.strip, 16)
        self.taps_at = round_up(self.share, 16)
        self.box3 = round_up(self.taps_at + 49, 16)


def rank_links(z, neighbour, counts, ranks):
    @pl.loop(0, z.owners)
    def _(owner):
        counts[owner] = 0

    for tile in range(z.tiles):
        for side in range(8):
            target = neighbour[tile, side] // z.tiles
            rank = counts[target]
            counts[target] = rank + 1
            ranks[tile * 8 + side] = jnp.minimum(rank, z.capacity - 1)


def pack_strips(z, load_row, load_col, neighbour, ranks, strips, outbox, box, offset):
    direct = z.strip - 2 * z.side
    for tile in range(z.tiles):
        for kind in range(4):
            base = (tile * 4 + kind) * 32
            for line in range(3):
                place = z.side - 3 + line if kind in (0, 2) else line
                value = load_row(tile, place) if kind < 2 else load_col(tile, place)
                start = base + line * z.side
                if line < 2:
                    strips[start : start + z.side, 0 : z.ch] = value
                    continue
                strips[start : start + direct, 0 : z.ch] = value[0:direct]
                for group in range(z.groups):
                    low = base + group * z.tail
                    strips[low : low + z.tail, z.ch : LANES] = value[
                        direct:, group * z.extra : (group + 1) * z.extra
                    ]
    for tile in range(z.tiles):
        for side in range(8):
            link = neighbour[tile, side]
            target = link // z.tiles
            rank = ranks[(link - target * z.tiles) * 8 + opposite[side]]
            base = (tile * 4 + served_kind[side]) * 32
            outbox[pl.ds(target * box + offset + rank * z.strip, z.strip), :] = strips[
                base : base + z.strip, :
            ]


def assemble(z, inbox, box, offset, neighbour, tissue, ranks, flat, grown):
    pitch = z.wide * 8
    for tile in range(z.tiles):
        for side in range(8):
            target = neighbour[tile, side] // z.tiles
            rank = ranks[tile * 8 + side]
            value = inbox[pl.ds(target * box + offset + rank * z.strip, z.strip), :]
            value = jnp.where(tissue[tile, side] > 0, value, 0.0)
            base = (tile * 8 + side) * 40
            flat[base : base + z.strip, :] = value[:, 0 : z.ch]
            low = base + z.strip
            for group in range(z.groups):
                flat[low : low + z.tail, group * z.extra : (group + 1) * z.extra] = value[
                    group * z.tail : (group + 1) * z.tail, z.ch : LANES
                ]
    far = z.side + 3
    for tile in range(z.tiles):
        for side in range(8):
            base = (tile * 8 + side) * 40
            for line in range(3):
                start = base + line * z.side
                if side in (0, 1):
                    row = line if side == 0 else far + line
                    spot = pl.ds((row * z.wide + 3) * 8 + tile, z.side, stride=8)
                    grown[spot, :] = flat[start : start + z.side, :]
                elif side in (2, 3):
                    col = line if side == 2 else far + line
                    spot = pl.ds((3 * z.wide + col) * 8 + tile, z.side, stride=pitch)
                    grown[spot, :] = flat[start : start + z.side, :]
                else:
                    row = line if side in (4, 5) else far + line
                    col = 0 if side in (4, 6) else far
                    start += z.side - 3 if side in (4, 6) else 0
                    spot = pl.ds((row * z.wide + col) * 8 + tile, 3, stride=8)
                    grown[spot, :] = flat[start : start + 3, :]


def inner_spot(z, tile, row):
    return pl.ds(((row + 3) * z.wide + 3) * 8 + tile, z.side, stride=8)


def conv_row(z, grown, taps, row, start, flipped):
    line = z.wide * 8
    total = start
    for a in range(7):
        band = grown[pl.ds(pl.multiple_of((row + a) * line, 8), line), :]
        for b in range(7):
            tap = 48 - (a * 7 + b) if flipped else a * 7 + b
            total = total + band[b * 8 : (b + z.side) * 8] * taps[tap : tap + 1, :]
    return total


def tiny(z):
    return [pltpu.SMEM((z.owners,), jnp.int32), pltpu.SMEM((8 * z.tiles,), jnp.int32)]


def field(z):
    return pltpu.VMEM((z.wide * z.wide * 8, z.ch), F32)


def first_strips(z, neighbour, tile_data):
    def body(neighbour, tile_data, out, counts, ranks, plain, strips, box):
        rank_links(z, neighbour, counts, ranks)
        for tile in range(z.tiles):
            for row in range(z.side):
                at = (tile * z.side + row) * z.side
                plain[at : at + z.side, :] = tile_data[tile, row].astype(F32)

        def load_row(tile, row):
            return plain[pl.ds((tile * z.side + row) * z.side, z.side), :]

        def load_col(tile, col):
            return plain[pl.ds(tile * z.pixels + col, z.side, stride=z.side), :]

        pack_strips(z, load_row, load_col, neighbour, ranks, strips, box, z.box1, 0)
        out[...] = box[...].astype(BF16)

    rows = z.owners * z.box1
    return call(
        body,
        shaped((rows, LANES), BF16),
        [neighbour, tile_data],
        1,
        tiny(z)
        + [
            pltpu.VMEM((z.rows, z.ch), F32),
            pltpu.VMEM((z.tiles * 4 * 32, LANES), F32),
            pltpu.VMEM((rows, LANES), F32),
        ],
    )


def pixel_rows(z, tile_data, cotangent):
    def body(tile_data, cotangent, keep, send, work):
        core = lax.axis_index("sub")
        for which, block in enumerate((tile_data, cotangent)):
            for tile in range(z.tiles):
                for row in range(z.side):
                    spot = pl.ds(row * z.side * z.tiles + tile, z.side, stride=z.tiles)
                    work[spot, :] = block[tile, row].astype(F32)
            at = which * z.half
            own = pl.multiple_of(core * z.half, 16)
            far = pl.multiple_of((1 - core) * z.half, 16)
            keep[at : at + z.half, :] = work[pl.ds(own, z.half), :].astype(BF16)
            send[at : at + z.half, :] = work[pl.ds(far, z.half), :].astype(BF16)

    out = shaped((2 * z.half, z.ch), BF16)
    return call(
        body, (out, out), [tile_data, cotangent], 0, [pltpu.VMEM((z.rows, z.ch), F32)]
    )


def first_conv(z, neighbour, tissue, inbox, tile_data, taps, conv_bias):
    def body(neighbour, tissue, inbox, tile_data, taps, bias, own, far, counts, ranks, box, flat, grown):
        core = lax.axis_index("sub")
        rank_links(z, neighbour, counts, ranks)
        box[...] = inbox[...].astype(F32)
        assemble(z, box, z.box1, 0, neighbour, tissue, ranks, flat, grown)
        for tile in range(z.tiles):
            for row in range(z.side):
                grown[inner_spot(z, tile, row), :] = tile_data[tile, row].astype(F32)
        start = jnp.broadcast_to(bias[...], (z.side * 8, z.ch))
        half_side = z.side // 2

        def fill(out, first_row):
            @pl.loop(0, half_side)
            def _(step):
                total = conv_row(z, grown, taps, first_row + step, start, False)
                for col in range(z.side):
                    at = step * (z.side * z.tiles) + col * z.tiles
                    out[pl.ds(at, z.tiles), :] = total[col * 8 : col * 8 + z.tiles]

        fill(far, (1 - core) * half_side)
        fill(own, core * half_side)

    out = shaped((z.half, z.ch), F32)
    return call(
        body,
        (out, out),
        [neighbour, tissue, inbox, tile_data, taps, conv_bias],
        2,
        tiny(z)
        + [
            pltpu.VMEM((z.owners * z.box1, LANES), F32),
            pltpu.VMEM((z.tiles * 8 * 40, z.ch), F32),
            field(z),
        ],
    )


def block_pass(z, spatial, rows, w_in, w_out, vectors):
    hid = z.hidden
    wide = 2 * z.ch

    def body(sp_own, sp_far, row_own, row_far, wi_own, wi_far, wo_own, wo_far, v_own, v_far,
             g_own, block_own, keep, send, normed_s, branch_s, pre_s, gact_s, act_s, gpre_s,
             xhat_s, inv_s):
        first = lax.axis_index("sub") == 0

        def join(own, far):
            return jnp.where(
                first,
                jnp.concatenate([own, far], axis=1),
                jnp.concatenate([far, own], axis=1),
            )

        def vector(index):
            at = index * z.ch
            return join(v_own[:, at : at + z.ch], v_far[:, at : at + z.ch])

        gain, shift, b_out, layer_scale = [vector(index) for index in range(4)]
        flat = join(sp_own[...], sp_far[...])
        centre = flat - jnp.sum(flat, axis=1, keepdims=True) * (1.0 / wide)
        var = jnp.sum(centre * centre, axis=1, keepdims=True) * (1.0 / wide)
        inverse = lax.rsqrt(var + eps_norm)
        xhat = centre * inverse
        xhat_s[...] = xhat
        inv_s[...] = inverse
        normed_s[...] = (xhat * gain + shift).astype(BF16)
        cot = join(row_own[z.half :, :].astype(F32), row_far[z.half :, :].astype(F32))
        branch_s[...] = (layer_scale * cot).astype(BF16)
        normed = normed_s[...]
        g_branch = branch_s[...]
        across = (((1,), (1,)), ((), ()))
        down = (((0,), (0,)), ((), ()))
        for side, (wi, wo, vec) in enumerate(((wi_own, wo_own, v_own), (wi_far, wo_far, v_far))):
            at = side * hid
            b_in = vec[:, 4 * z.ch : 4 * z.ch + hid]
            pre_s[:, at : at + hid] = jnp.dot(normed, wi[...], preferred_element_type=F32) + b_in
            gact_s[:, at : at + hid] = lax.dot_general(
                g_branch, wo[...], across, preferred_element_type=F32
            )

        @pl.loop(0, z.half // 16)
        def _(step):
            spot = pl.ds(pl.multiple_of(step * 16, 16), 16)
            pre = pre_s[spot, :]
            cdf = 0.5 * (1.0 + lax.erf(pre * root_half))
            act_s[spot, :] = (pre * cdf).astype(BF16)
            slope = cdf + pre * jnp.exp(-0.5 * pre * pre) * inv_root_tau
            gpre_s[spot, :] = (gact_s[spot, :] * slope).astype(BF16)

        g_normed = lax.dot_general(
            gpre_s[:, 0:hid], wi_own[...], across, preferred_element_type=F32
        ) + lax.dot_general(gpre_s[:, hid:], wi_far[...], across, preferred_element_type=F32)
        xhat = xhat_s[...]
        leading = g_normed * gain
        mean_h = jnp.sum(leading, axis=1, keepdims=True) * (1.0 / wide)
        mean_hx = jnp.sum(leading * xhat, axis=1, keepdims=True) * (1.0 / wide)
        g_rows = inv_s[...] * (leading - mean_h - xhat * mean_hx)
        branch = (
            jnp.dot(act_s[:, 0:hid], wo_own[...], preferred_element_type=F32)
            + jnp.dot(act_s[:, hid:], wo_far[...], preferred_element_type=F32)
            + b_out
        )
        inner = join(row_own[0 : z.half, :].astype(F32), row_far[0 : z.half, :].astype(F32))
        block = inner + layer_scale * branch

        def part(value, mine):
            low, high = value[:, 0 : z.ch], value[:, z.ch :]
            return jnp.where(first == mine, low, high).astype(BF16)

        g_own[...] = part(g_rows, True)
        block_own[...] = part(block, True)
        send[0 : z.half, 0 : z.ch] = part(g_rows, False)
        send[z.half : 2 * z.half, 0 : z.ch] = part(block, False)
        for side in range(2):
            at = side * hid
            part_in = lax.dot_general(
                normed, gpre_s[:, at : at + hid], down, preferred_element_type=F32
            )
            part_out = lax.dot_general(
                act_s[:, at : at + hid], g_branch, down, preferred_element_type=F32
            )
            ref, base = (keep, 0) if side == 0 else (send, 2 * z.half)
            for group in range(hid // LANES):
                low = base + group * wide
                ref[low : low + wide, :] = part_in[
                    :, group * LANES : (group + 1) * LANES
                ].astype(ref.dtype)
            low = base + hid // LANES * wide
            ref[low : low + hid, :] = part_out[:, 0:LANES].astype(ref.dtype)
            low += hid
            ref[low : low + hid // 2, :] = jnp.concatenate(
                [part_out[0 : hid // 2, LANES:], part_out[hid // 2 :, LANES:]], axis=1
            ).astype(ref.dtype)

    rows_out = shaped((z.half, z.ch), BF16)
    return call(
        body,
        (
            rows_out,
            rows_out,
            shaped((z.weight_rows, LANES), F32),
            shaped((2 * z.half + z.weight_rows, LANES), BF16),
        ),
        [*spatial, *rows, *w_in, *w_out, *vectors],
        0,
        [
            pltpu.VMEM((z.half, wide), BF16),
            pltpu.VMEM((z.half, wide), BF16),
            pltpu.VMEM((z.half, 2 * hid), F32),
            pltpu.VMEM((z.half, 2 * hid), F32),
            pltpu.VMEM((z.half, 2 * hid), BF16),
            pltpu.VMEM((z.half, 2 * hid), BF16),
            pltpu.VMEM((z.half, wide), F32),
            pltpu.VMEM((z.half, 1), F32),
        ],
        flops=12 * z.half * wide * 2 * hid,
    )


def both_halves(z, work, own, far):
    core = lax.axis_index("sub")
    work[pl.ds(pl.multiple_of(core * z.half, 16), z.half), :] = own.astype(F32)
    work[pl.ds(pl.multiple_of((1 - core) * z.half, 16), z.half), :] = far.astype(F32)


def second_strips(z, neighbour, g_own, keep, received):
    def body(neighbour, g_own, keep, received, out, counts, ranks, plain, strips, box):
        rank_links(z, neighbour, counts, ranks)
        both_halves(z, plain, g_own[...], received[0 : z.half, 0 : z.ch])
        for owner in range(z.owners):
            at = owner * z.share
            low = 2 * z.half + at
            box[owner * z.box2 : owner * z.box2 + z.share, :] = keep[
                at : at + z.share, :
            ] + received[low : low + z.share, :].astype(F32)

        def load_row(tile, row):
            return plain[pl.ds(row * z.side * z.tiles + tile, z.side, stride=z.tiles), :]

        def load_col(tile, col):
            return plain[pl.ds(col * z.tiles + tile, z.side, stride=z.side * z.tiles), :]

        pack_strips(z, load_row, load_col, neighbour, ranks, strips, box, z.box2, z.halo_at)
        out[...] = box[...].astype(BF16)

    rows = z.owners * z.box2
    return call(
        body,
        shaped((rows, LANES), BF16),
        [neighbour, g_own, keep, received],
        1,
        tiny(z)
        + [
            pltpu.VMEM((z.rows, z.ch), F32),
            pltpu.VMEM((z.tiles * 4 * 32, LANES), F32),
            pltpu.VMEM((rows, LANES), F32),
        ],
    )


def filter_gradient(z, neighbour, tissue, inbox, tile_data, g_own, block_own, received):
    def body(neighbour, tissue, inbox, tile_data, g_own, block_own, received, taps, block_out,
             counts, ranks, box, flat, grown, plain, g_field, sums):
        rank_links(z, neighbour, counts, ranks)
        box[...] = inbox[...].astype(F32)
        assemble(z, box, z.box1, 0, neighbour, tissue, ranks, flat, grown)
        for tile in range(z.tiles):
            for row in range(z.side):
                grown[inner_spot(z, tile, row), :] = tile_data[tile, row].astype(F32)
        empty = jnp.zeros((z.wide * z.wide, z.ch), F32)
        for tile in range(z.tiles, 8):
            grown[pl.ds(tile, z.wide * z.wide, stride=8), :] = empty
        both_halves(z, plain, block_own[...], received[z.half : 2 * z.half, 0 : z.ch])
        for tile in range(z.tiles):
            for row in range(z.side):
                spot = pl.ds(row * z.side * z.tiles + tile, z.side, stride=z.tiles)
                block_out[tile, row] = plain[spot, :].astype(BF16)
        both_halves(z, plain, g_own[...], received[0 : z.half, 0 : z.ch])
        g_field[...] = jnp.zeros_like(g_field)
        for tile in range(z.tiles):
            g_field[pl.ds(tile, z.pixels, stride=8), :] = plain[
                pl.ds(tile, z.pixels, stride=z.tiles), :
            ]
        sums[...] = jnp.zeros_like(sums)
        line = z.wide * 8

        @pl.loop(0, z.side)
        def _(row):
            g_row = g_field[pl.ds(pl.multiple_of(row * z.side * 8, 8), z.side * 8), :]
            for a in range(7):
                band = grown[pl.ds(pl.multiple_of((row + a) * line, 8), line), :]
                for b in range(7):
                    product = band[b * 8 : (b + z.side) * 8] * g_row
                    total = product[0:8]
                    for col in range(1, z.side):
                        total = total + product[col * 8 : (col + 1) * 8]
                    at = (a * 7 + b) * 8
                    sums[at : at + 8, :] += total

        taps[...] = jnp.sum(sums[...].reshape(49, 8, z.ch), axis=1)

    return call(
        body,
        (shaped((49, z.ch), F32), shaped((z.tiles, z.side, z.side, z.ch), BF16)),
        [neighbour, tissue, inbox, tile_data, g_own, block_own, received],
        2,
        tiny(z)
        + [
            pltpu.VMEM((z.owners * z.box1, LANES), F32),
            pltpu.VMEM((z.tiles * 8 * 40, z.ch), F32),
            field(z),
            pltpu.VMEM((z.rows, z.ch), F32),
            pltpu.VMEM((z.pixels * 8, z.ch), F32),
            pltpu.VMEM((49 * 8, z.ch), F32),
        ],
    )


def sum_shares(z, inbox, taps):
    def body(inbox, taps, out):
        total = inbox[0 : z.share, :].astype(F32)
        for owner in range(1, z.owners):
            at = owner * z.box2
            total = total + inbox[at : at + z.share, :].astype(F32)
        share = total.astype(BF16)
        taps16 = taps[...].astype(BF16)
        for owner in range(z.owners):
            at = owner * z.box3
            out[at : at + z.share, :] = share
            at += z.taps_at
            out[at : at + 49, 0 : z.ch] = taps16

    return call(body, shaped((z.owners * z.box3, LANES), BF16), [inbox, taps])


def second_conv(z, neighbour, tissue, inbox, g_own, received, cotangent, taps):
    def body(neighbour, tissue, inbox, g_own, received, cotangent, taps, out,
             counts, ranks, box, flat, grown, plain, totals):
        rank_links(z, neighbour, counts, ranks)
        box[...] = inbox[...].astype(F32)
        assemble(z, box, z.box2, z.halo_at, neighbour, tissue, ranks, flat, grown)
        both_halves(z, plain, g_own[...], received[0 : z.half, 0 : z.ch])
        for tile in range(z.tiles):
            for row in range(z.side):
                spot = pl.ds(row * z.side * z.tiles + tile, z.side, stride=z.tiles)
                grown[inner_spot(z, tile, row), :] = plain[spot, :]
        start = jnp.zeros((z.side * 8, z.ch), F32)

        @pl.loop(0, z.side)
        def _(row):
            total = conv_row(z, grown, taps, row, start, True)
            totals[pl.ds(pl.multiple_of(row * z.side * 8, 8), z.side * 8), :] = total

        for tile in range(z.tiles):
            for row in range(z.side):
                spot = pl.ds(row * z.side * 8 + tile, z.side, stride=8)
                out[tile, row] = (totals[spot, :] + cotangent[tile, row].astype(F32)).astype(BF16)

    return call(
        body,
        shaped((z.tiles, z.side, z.side, z.ch), BF16),
        [neighbour, tissue, inbox, g_own, received, cotangent, taps],
        2,
        tiny(z)
        + [
            pltpu.VMEM((z.owners * z.box2, LANES), F32),
            pltpu.VMEM((z.tiles * 8 * 40, z.ch), F32),
            field(z),
            pltpu.VMEM((z.rows, z.ch), F32),
            pltpu.VMEM((z.pixels * 8, z.ch), F32),
        ],
    )


def finish(z, inbox, scale):
    hid = z.hidden
    wide = 2 * z.ch

    def body(inbox, grad_in, grad_out, grad_taps, work):
        total = jnp.zeros((49, z.ch), F32)
        for owner in range(z.owners):
            at = owner * z.box3
            work[owner * z.share : (owner + 1) * z.share, :] = (
                inbox[at : at + z.share, :].astype(F32) * scale
            )
            at += z.taps_at
            total = total + inbox[at : at + 49, 0 : z.ch].astype(F32)
        grad_taps[...] = total * scale
        for group in range(hid // LANES):
            low = group * wide
            grad_in[:, group * LANES : (group + 1) * LANES] = work[low : low + wide, :]
        low = hid // LANES * wide
        grad_out[:, 0:LANES] = work[low : low + hid, :]
        low += hid
        mid = hid // 2
        grad_out[0:mid, LANES:] = work[low : low + mid, 0 : wide - LANES]
        grad_out[mid:, LANES:] = work[low : low + mid, wide - LANES :]

    return call(
        body,
        (shaped((wide, hid), F32), shaped((hid, wide), F32), shaped((49, z.ch), F32)),
        [inbox],
        0,
        [pltpu.VMEM((z.weight_rows, LANES), F32)],
    )


def exchange_tiles(z, box):
    boxes = box.reshape(z.owners, -1, LANES)
    return lax.all_to_all(boxes, "tiles", split_axis=0, concat_axis=0, tiled=True).reshape(box.shape)


def swap_sub(piece):
    return lax.ppermute(piece, "sub", [(0, 1), (1, 0)])


def local(
    tile_data,
    cotangent,
    neighbour,
    tissue,
    kernel,
    conv_bias,
    layer_norm_gain,
    layer_norm_bias,
    w_in,
    b_in,
    w_out,
    b_out,
    layer_scale,
):
    z = Sizes(tile_data.shape, w_in.shape[1], lax.axis_size("tiles"))
    scale = 1.0 / math.sqrt(z.owners * z.rows)
    taps = kernel.reshape(49, z.ch)

    outbox = first_strips(z, neighbour, tile_data)
    inbox = exchange_tiles(z, outbox)

    w_in16 = w_in.astype(BF16)
    w_out16 = w_out.astype(BF16)
    vectors = jnp.concatenate([layer_norm_gain, layer_norm_bias, b_out, layer_scale, b_in])
    vectors = vectors.reshape(1, -1)
    rows_keep, rows_send = pixel_rows(z, tile_data, cotangent)

    sp_own, sp_far = first_conv(
        z, neighbour, tissue, inbox, tile_data, taps, conv_bias.reshape(1, z.ch)
    )
    g_own, block_own, keep, send = block_pass(
        z,
        (sp_own, swap_sub(sp_far)),
        (rows_keep, swap_sub(rows_send)),
        (w_in16, swap_sub(w_in16)),
        (w_out16, swap_sub(w_out16)),
        (vectors, swap_sub(vectors)),
    )
    received = swap_sub(send)
    inbox2 = exchange_tiles(z, second_strips(z, neighbour, g_own, keep, received))
    grad_taps, block_out = filter_gradient(
        z, neighbour, tissue, inbox, tile_data, g_own, block_own, received
    )
    inbox3 = exchange_tiles(z, sum_shares(z, inbox2, grad_taps))
    tile_grad = second_conv(z, neighbour, tissue, inbox2, g_own, received, cotangent, taps)
    grad_in, grad_out, grad_taps = finish(z, inbox3, scale)
    return block_out, tile_grad, grad_in, grad_out, grad_taps.reshape(kernel.shape)


def solution(mesh):
    placed = (
        P(("slides", "tiles"), None, None, "sub"),
        P(("slides", "tiles"), None, None, "sub"),
        P(("slides", "tiles"), None),
        P(("slides", "tiles"), None),
        P(None, None, "sub"),
        P("sub"),
        P("sub"),
        P("sub"),
        P(None, "sub"),
        P("sub"),
        P("sub", None),
        P("sub"),
        P("sub"),
    )
    return jax.shard_map(
        local,
        mesh=mesh,
        in_specs=placed,
        out_specs=(
            P(("slides", "tiles"), None, None, "sub"),
            P(("slides", "tiles"), None, None, "sub"),
            P("slides", "sub"),
            P(("slides", "sub"), None),
            P("slides", None, "sub"),
        ),
        check_vma=False,
    )
```

```python
import math

import jax
import jax.numpy as jnp
from jax import lax
from jax.experimental import pallas as pl
from jax.experimental.pallas import tpu as pltpu
from jax.sharding import PartitionSpec as P

eps_norm = 1e-06
root_half = 0.7071067811865476
inv_root_tau = 0.3989422804014327
served_kind = (1, 0, 3, 2, 1, 1, 0, 0)
opposite = (1, 0, 3, 2, 7, 6, 5, 4)
LANES = 128
FIRST_VMEM = 60
F32 = jnp.float32
BF16 = jnp.bfloat16


def round_up(value, step):
    return -(-value // step) * step


def call(body, outs, operands, scalars=0, scratch=(), flops=0, vmem=16, after=(), **specs):
    spaces = specs.pop("spaces", None)
    if spaces is None:
        spaces = [pltpu.SMEM] * scalars + [pltpu.VMEM] * (len(operands) - scalars)
    count = len(operands)
    stop = count + len(after)

    def run(*refs):
        body(*refs[:count], *refs[stop:])

    return pl.pallas_call(
        run,
        out_shape=outs,
        in_specs=[pl.BlockSpec(memory_space=space) for space in [*spaces, *[pl.ANY] * len(after)]],
        scratch_shapes=list(scratch),
        compiler_params=pltpu.CompilerParams(vmem_limit_bytes=vmem << 20),
        cost_estimate=pl.CostEstimate(
            flops=flops,
            transcendentals=0,
            bytes_accessed=sum(o.size * o.dtype.itemsize for o in operands),
        ),
        **specs,
    )(*operands, *after)


def shaped(shape, dtype):
    return jax.ShapeDtypeStruct(shape, dtype)


class Sizes:
    def __init__(self, tile_shape, hidden, owners):
        self.tiles, self.side, _, self.ch = tile_shape
        self.hidden = hidden
        self.owners = owners
        self.capacity = max(2, 8 * self.tiles // owners)
        self.links = 8 * self.tiles
        self.pixels = self.side * self.side
        self.rows = self.pixels * self.tiles
        self.half = self.rows // 2
        self.extra = LANES - self.ch
        self.groups = self.ch // self.extra
        self.strip = 3 * self.side * self.ch // LANES
        self.tail = 3 * self.side - self.strip
        self.far = self.side + 3
        self.wide = self.side + 6
        self.box1 = round_up(self.capacity * self.strip, 8)
        self.weight_rows = 2 * (2 * self.ch) * hidden // LANES
        self.share = self.weight_rows // owners
        self.halo_at = round_up(self.share, 8)
        self.box2 = round_up(self.halo_at + self.capacity * self.strip, 8)
        self.box3 = round_up(self.share, 8)

    def owner_of(self, link):
        factor = -(-65536 // self.tiles)
        assert self.owners * self.tiles * (factor * self.tiles - 65536) < 65536
        return (link * factor) >> 16


def rank_links(z, neighbour, counts, slots):
    @pl.loop(0, z.owners)
    def _(owner):
        counts[owner] = 0

    for link in range(z.links):
        owner = z.owner_of(neighbour[link // 8, link % 8])
        rank = counts[owner]
        counts[owner] = rank + 1
        slots[link] = owner
        slots[z.links + link] = jnp.minimum(rank, z.capacity - 1)
    for link in range(z.links):
        slot = neighbour[link // 8, link % 8] - slots[link] * z.tiles
        slots[2 * z.links + link] = slots[z.links + slot * 8 + opposite[link % 8]]


def pack_strips(z, load_row, load_col, slots, strips, outbox, box, offset):
    direct = z.strip - 2 * z.side
    for tile in range(z.tiles):
        for kind in range(4):
            base = (tile * 4 + kind) * 32
            for line in range(3):
                place = z.side - 3 + line if kind in (0, 2) else line
                value = load_row(tile, place) if kind < 2 else load_col(tile, place)
                start = base + line * z.side
                if line < 2:
                    strips[start : start + z.side, 0 : z.ch] = value
                    continue
                strips[start : start + direct, 0 : z.ch] = value[0:direct]
                for group in range(z.groups):
                    low = base + group * z.tail
                    strips[low : low + z.tail, z.ch : LANES] = value[
                        direct:, group * z.extra : (group + 1) * z.extra
                    ]
    for link in range(z.links):
        base = (link // 8 * 4 + served_kind[link % 8]) * 32
        low = slots[link] * box + offset + slots[2 * z.links + link] * z.strip
        outbox[pl.ds(low, z.strip), :] = strips[base : base + z.strip, :]


def assemble(z, inbox, box, offset, slots, tissue, flat, grown):
    pitch = z.wide * 8
    for link in range(z.links):
        low = slots[link] * box + offset + slots[z.links + link] * z.strip
        value = inbox[pl.ds(low, z.strip), :]
        value = jnp.where(tissue[link // 8, link % 8] > 0, value, 0.0)
        base = link * 40
        flat[base : base + z.strip, :] = value[:, 0 : z.ch]
        low = base + z.strip
        for group in range(z.groups):
            flat[low : low + z.tail, group * z.extra : (group + 1) * z.extra] = value[
                group * z.tail : (group + 1) * z.tail, z.ch : LANES
            ]
    far = z.far
    for tile in range(z.tiles):
        for side in range(8):
            base = (tile * 8 + side) * 40
            for line in range(3):
                start = base + line * z.side
                if side in (0, 1):
                    row = line if side == 0 else far + line
                    spot = pl.ds((row * z.wide + 3) * 8 + tile, z.side, stride=8)
                    grown[spot, :] = flat[start : start + z.side, :]
                elif side in (2, 3):
                    col = line if side == 2 else far + line
                    spot = pl.ds((3 * z.wide + col) * 8 + tile, z.side, stride=pitch)
                    grown[spot, :] = flat[start : start + z.side, :]
                else:
                    row = line if side in (4, 5) else far + line
                    col = 0 if side in (4, 6) else far
                    start += z.side - 3 if side in (4, 6) else 0
                    spot = pl.ds((row * z.wide + col) * 8 + tile, 3, stride=8)
                    grown[spot, :] = flat[start : start + 3, :]


def inner_spot(z, tile, row):
    return pl.ds(((row + 3) * z.wide + 3) * 8 + tile, z.side, stride=8)


def fill_inner(z, grown, tile_data):
    for tile in range(z.tiles):
        for row in range(z.side):
            grown[inner_spot(z, tile, row), :] = tile_data[tile, row].astype(F32)


def conv_row(z, grown, taps, row, start, flipped):
    line = z.wide * 8
    total = start
    for a in range(7):
        band = grown[pl.ds(pl.multiple_of((row + a) * line, 8), line), :]
        for b in range(7):
            tap = taps[6 - a, 6 - b : 7 - b, :] if flipped else taps[a, b : b + 1, :]
            total = total + band[b * 8 : (b + z.side) * 8] * tap
    return total


def rim_row(z, grown, taps, row, start):
    total = start
    inner = []
    for a in range(7):
        at = (row + a) * z.wide * 8
        if 3 <= row + a < z.far:
            inner.append((a, at))
            continue
        for b in range(7):
            low = at + b * 8
            total = total + grown[low : low + z.side * 8, :] * taps[a, b : b + 1, :]
    pieces = [total[col * 8 : (col + 1) * 8] for col in range(z.side)]
    for a, at in inner:
        for col in range(z.side):
            for b in range(7):
                if col + b < 3 or col + b >= z.far:
                    low = at + (col + b) * 8
                    pieces[col] = pieces[col] + grown[low : low + 8, :] * taps[a, b : b + 1, :]
    return pieces


def field(z):
    return pltpu.VMEM((z.wide * z.wide * 8, z.ch), F32)


def boxes(z, box):
    return pltpu.VMEM((z.owners * box, LANES), F32)


def flat_strips(z):
    return pltpu.VMEM((z.links * 40, z.ch), F32)


def packed_strips(z):
    return pltpu.VMEM((z.tiles * 4 * 32, LANES), F32)


def pixel_major(z):
    return pltpu.VMEM((z.rows, z.ch), F32)


def first_strips(z, neighbour, tile_data):
    def body(neighbour_hbm, tile_hbm, out, slots, neighbour, tile_data, sems, counts, plain, strips, box):
        fetch_links = pltpu.make_async_copy(neighbour_hbm, neighbour, sems.at[0])
        fetch_tiles = pltpu.make_async_copy(tile_hbm, tile_data, sems.at[1])
        fetch_links.start()
        fetch_tiles.start()
        fetch_links.wait()
        rank_links(z, neighbour, counts, slots)
        fetch_tiles.wait()
        for tile in range(z.tiles):
            for row in range(z.side):
                at = (tile * z.side + row) * z.side
                plain[at : at + z.side, :] = tile_data[tile, row].astype(F32)

        def load_row(tile, row):
            return plain[pl.ds((tile * z.side + row) * z.side, z.side), :]

        def load_col(tile, col):
            return plain[pl.ds(tile * z.pixels + col, z.side, stride=z.side), :]

        pack_strips(z, load_row, load_col, slots, strips, box, z.box1, 0)
        out[...] = box[...].astype(BF16)

    rows = z.owners * z.box1
    return call(
        body,
        (shaped((rows, LANES), BF16), shaped((3 * z.links,), jnp.int32)),
        [neighbour, tile_data],
        spaces=[pl.ANY, pl.ANY],
        vmem=FIRST_VMEM,
        out_specs=(
            pl.BlockSpec(memory_space=pltpu.VMEM),
            pl.BlockSpec(memory_space=pltpu.SMEM),
        ),
        scratch=[
            pltpu.SMEM(neighbour.shape, jnp.int32),
            pltpu.VMEM(tile_data.shape, BF16),
            pltpu.SemaphoreType.DMA((2,)),
            pltpu.SMEM((z.owners,), jnp.int32),
            pixel_major(z),
            packed_strips(z),
            boxes(z, z.box1),
        ],
    )


def local_part(z, tile_data, cotangent, taps, conv_bias):
    def body(tile_data, cotangent, taps, bias, keep, send, out, work, grown):
        core = lax.axis_index("sub")
        for which, block in enumerate((tile_data, cotangent)):
            for tile in range(z.tiles):
                for row in range(z.side):
                    spot = pl.ds(row * z.side * z.tiles + tile, z.side, stride=z.tiles)
                    work[spot, :] = block[tile, row].astype(F32)
            at = which * z.half
            own = pl.multiple_of(core * z.half, 16)
            far = pl.multiple_of((1 - core) * z.half, 16)
            keep[at : at + z.half, :] = work[pl.ds(own, z.half), :].astype(BF16)
            send[at : at + z.half, :] = work[pl.ds(far, z.half), :].astype(BF16)
        grown[...] = jnp.zeros_like(grown)
        fill_inner(z, grown, tile_data)
        start = jnp.broadcast_to(bias[...], (z.side * 8, z.ch))

        @pl.loop(0, z.side)
        def _(row):
            total = conv_row(z, grown, taps, row, start, False)
            out[pl.ds(pl.multiple_of(row * z.side * 8, 8), z.side * 8), :] = total

    rows = shaped((2 * z.half, z.ch), BF16)
    return call(
        body,
        (rows, rows, shaped((z.pixels * 8, z.ch), F32)),
        [tile_data, cotangent, taps, conv_bias],
        scratch=[pixel_major(z), field(z)],
        flops=2 * 49 * z.rows * z.ch,
    )


def rim_conv(z, slots, tissue, inbox, inner, taps, after):
    def body(slots, tissue, inbox, inner, taps, own, far, box, flat, grown, whole):
        core = lax.axis_index("sub")
        box[...] = inbox[...].astype(F32)
        assemble(z, box, z.box1, 0, slots, tissue, flat, grown)
        for row in range(z.side):
            start = inner[row * z.side * 8 : (row + 1) * z.side * 8, :]
            for col, piece in enumerate(rim_row(z, grown, taps, row, start)):
                at = (row * z.side + col) * z.tiles
                whole[at : at + z.tiles, :] = piece[0 : z.tiles]
        own[...] = whole[pl.ds(pl.multiple_of(core * z.half, 8), z.half), :]
        far[...] = whole[pl.ds(pl.multiple_of((1 - core) * z.half, 8), z.half), :]

    out = shaped((z.half, z.ch), F32)
    return call(
        body,
        (out, out),
        [slots, tissue, inbox, inner, taps],
        2,
        [boxes(z, z.box1), flat_strips(z), field(z), pixel_major(z)],
        after=after,
    )


ACROSS = (((1,), (1,)), ((), ()))
DOWN = (((0,), (0,)), ((), ()))


def join(first, own, far):
    return jnp.where(
        first, jnp.concatenate([own, far], axis=1), jnp.concatenate([far, own], axis=1)
    )


def both_vectors(z, first, v_own, v_far, index):
    at = index * z.ch
    return join(first, v_own[:, at : at + z.ch], v_far[:, at : at + z.ch])


def block_pass(z, spatial, rows, w_in, w_out, vectors):
    hid = z.hidden
    wide = 2 * z.ch

    def body(sp_own, sp_far, row_own, row_far, wi_own, wi_far, wo_own, wo_far, v_own,
             v_far, g_own, block_own, block_far, keep, send, normed_s, branch_s, pre_s, gact_s, act_s, gpre_s, xhat_s, inv_s):
        first = lax.axis_index("sub") == 0
        gain, shift, b_out, layer_scale = [
            both_vectors(z, first, v_own, v_far, index) for index in range(4)
        ]
        flat = join(first, sp_own[...], sp_far[...])
        centre = flat - jnp.sum(flat, axis=1, keepdims=True) * (1.0 / wide)
        var = jnp.sum(centre * centre, axis=1, keepdims=True) * (1.0 / wide)
        inverse = lax.rsqrt(var + eps_norm)
        xhat = centre * inverse
        xhat_s[...] = xhat
        inv_s[...] = inverse
        normed_s[...] = (xhat * gain + shift).astype(BF16)
        normed = normed_s[...]
        cot = join(first, row_own[z.half :, :].astype(F32), row_far[z.half :, :].astype(F32))
        branch_s[...] = (layer_scale * cot).astype(BF16)
        g_branch = branch_s[...]
        for side, (wi, wo, vec) in enumerate(((wi_own, wo_own, v_own), (wi_far, wo_far, v_far))):
            at = side * hid
            b_in = vec[:, 4 * z.ch : 4 * z.ch + hid]
            pre_s[:, at : at + hid] = jnp.dot(normed, wi[...], preferred_element_type=F32) + b_in
            gact_s[:, at : at + hid] = jnp.dot(g_branch, wo[...], preferred_element_type=F32)

        @pl.loop(0, z.half // 16)
        def _(step):
            spot = pl.ds(pl.multiple_of(step * 16, 16), 16)
            pre = pre_s[spot, :]
            cdf = 0.5 * (1.0 + lax.erf(pre * root_half))
            act_s[spot, :] = (pre * cdf).astype(BF16)
            slope = cdf + pre * jnp.exp(-0.5 * pre * pre) * inv_root_tau
            gpre_s[spot, :] = (gact_s[spot, :] * slope).astype(BF16)

        g_normed = lax.dot_general(
            gpre_s[:, 0:hid], wi_own[...], ACROSS, preferred_element_type=F32
        ) + lax.dot_general(gpre_s[:, hid:], wi_far[...], ACROSS, preferred_element_type=F32)
        xhat = xhat_s[...]
        leading = g_normed * gain
        mean_h = jnp.sum(leading, axis=1, keepdims=True) * (1.0 / wide)
        mean_hx = jnp.sum(leading * xhat, axis=1, keepdims=True) * (1.0 / wide)
        g_rows = inv_s[...] * (leading - mean_h - xhat * mean_hx)
        branch = (
            lax.dot_general(act_s[:, 0:hid], wo_own[...], ACROSS, preferred_element_type=F32)
            + lax.dot_general(act_s[:, hid:], wo_far[...], ACROSS, preferred_element_type=F32)
            + b_out
        )
        inner = join(
            first, row_own[0 : z.half, :].astype(F32), row_far[0 : z.half, :].astype(F32)
        )
        block = inner + layer_scale * branch

        def part(value, mine):
            low, high = value[:, 0 : z.ch], value[:, z.ch :]
            return jnp.where(first == mine, low, high).astype(BF16)

        g_own[...] = part(g_rows, True)
        block_own[...] = part(block, True)
        send[0 : z.half, 0 : z.ch] = part(g_rows, False)
        block_far[...] = part(block, False)
        for side in range(2):
            at = side * hid
            ref, low = (keep, 0) if side == 0 else (send, z.half)
            for left, right in ((normed, gpre_s), (g_branch, act_s)):
                grad = lax.dot_general(
                    left, right[:, at : at + hid], DOWN, preferred_element_type=F32
                )
                for group in range(hid // LANES):
                    lanes = slice(group * LANES, (group + 1) * LANES)
                    ref[low : low + wide, :] = grad[:, lanes].astype(ref.dtype)
                    low += wide

    rows_out = shaped((z.half, z.ch), BF16)
    return call(
        body,
        (
            rows_out,
            rows_out,
            rows_out,
            shaped((z.weight_rows, LANES), F32),
            shaped((z.half + z.weight_rows, LANES), BF16),
        ),
        [*spatial, *rows, *w_in, *w_out, *vectors],
        0,
        [
            pltpu.VMEM((z.half, wide), BF16),
            pltpu.VMEM((z.half, wide), BF16),
            pltpu.VMEM((z.half, 2 * hid), F32),
            pltpu.VMEM((z.half, 2 * hid), F32),
            pltpu.VMEM((z.half, 2 * hid), BF16),
            pltpu.VMEM((z.half, 2 * hid), BF16),
            pltpu.VMEM((z.half, wide), F32),
            pltpu.VMEM((z.half, 1), F32),
        ],
        flops=12 * z.half * wide * 2 * hid,
    )


def both_halves(z, work, own, far):
    core = lax.axis_index("sub")
    work[pl.ds(pl.multiple_of(core * z.half, 16), z.half), :] = own.astype(F32)
    work[pl.ds(pl.multiple_of((1 - core) * z.half, 16), z.half), :] = far.astype(F32)


def second_strips(z, slots, g_own, keep, received):
    def body(slots, g_own, keep, received, out, plain, strips, box):
        both_halves(z, plain, g_own[...], received[0 : z.half, 0 : z.ch])
        for owner in range(z.owners):
            at = owner * z.share
            low = z.half + at
            box[owner * z.box2 : owner * z.box2 + z.share, :] = keep[
                at : at + z.share, :
            ] + received[low : low + z.share, :].astype(F32)

        def load_row(tile, row):
            return plain[pl.ds(row * z.side * z.tiles + tile, z.side, stride=z.tiles), :]

        def load_col(tile, col):
            return plain[pl.ds(col * z.tiles + tile, z.side, stride=z.side * z.tiles), :]

        pack_strips(z, load_row, load_col, slots, strips, box, z.box2, z.halo_at)
        out[...] = box[...].astype(BF16)

    return call(
        body,
        shaped((z.owners * z.box2, LANES), BF16),
        [slots, g_own, keep, received],
        1,
        [pixel_major(z), packed_strips(z), boxes(z, z.box2)],
    )


def filter_gradient(z, slots, tissue, inbox, tile_data, g_own, received, scale):
    def body(slots, tissue, inbox, tile_data, g_own, received, taps, box, flat, grown, plain,
             g_field, sums):
        box[...] = inbox[...].astype(F32)
        assemble(z, box, z.box1, 0, slots, tissue, flat, grown)
        fill_inner(z, grown, tile_data)
        empty = jnp.zeros((z.wide * z.wide, z.ch), F32)
        for tile in range(z.tiles, 8):
            grown[pl.ds(tile, z.wide * z.wide, stride=8), :] = empty
        both_halves(z, plain, g_own[...], received[0 : z.half, 0 : z.ch])
        g_field[...] = jnp.zeros_like(g_field)
        for tile in range(z.tiles):
            g_field[pl.ds(tile, z.pixels, stride=8), :] = plain[
                pl.ds(tile, z.pixels, stride=z.tiles), :
            ]
        sums[...] = jnp.zeros_like(sums)
        line = z.wide * 8

        @pl.loop(0, z.side)
        def _(row):
            g_row = g_field[pl.ds(pl.multiple_of(row * z.side * 8, 8), z.side * 8), :]
            for a in range(7):
                band = grown[pl.ds(pl.multiple_of((row + a) * line, 8), line), :]
                for b in range(7):
                    product = band[b * 8 : (b + z.side) * 8] * g_row
                    total = product[0:8]
                    for col in range(1, z.side):
                        total = total + product[col * 8 : (col + 1) * 8]
                    at = (a * 7 + b) * 8
                    sums[at : at + 8, :] += total

        for a in range(7):
            rows = sums[a * 56 : (a + 1) * 56, :].reshape(7, 8, z.ch)
            taps[a] = jnp.sum(rows, axis=1) * scale

    return call(
        body,
        shaped((7, 7, z.ch), F32),
        [slots, tissue, inbox, tile_data, g_own, received],
        2,
        [
            boxes(z, z.box1),
            flat_strips(z),
            field(z),
            pixel_major(z),
            pltpu.VMEM((z.pixels * 8, z.ch), F32),
            pltpu.VMEM((49 * 8, z.ch), F32),
        ],
        flops=2 * 49 * z.rows * z.ch,
    )


def sum_shares(z, inbox, after):
    def body(inbox, out):
        total = inbox[0 : z.share, :].astype(F32)
        for owner in range(1, z.owners):
            at = owner * z.box2
            total = total + inbox[at : at + z.share, :].astype(F32)
        share = total.astype(BF16)
        for owner in range(z.owners):
            at = owner * z.box3
            out[at : at + z.share, :] = share

    return call(body, shaped((z.owners * z.box3, LANES), BF16), [inbox], after=after)


def second_conv(z, slots, tissue, inbox, g_own, received, block, cotangent, taps):
    def body(slots, tissue, inbox, g_own, received, block_own, block_far, cotangent, taps, out,
             block_out, box, flat, grown, plain, totals):
        box[...] = inbox[...].astype(F32)
        assemble(z, box, z.box2, z.halo_at, slots, tissue, flat, grown)
        both_halves(z, plain, g_own[...], received[0 : z.half, 0 : z.ch])
        for tile in range(z.tiles):
            for row in range(z.side):
                spot = pl.ds(row * z.side * z.tiles + tile, z.side, stride=z.tiles)
                grown[inner_spot(z, tile, row), :] = plain[spot, :]
        start = jnp.zeros((z.side * 8, z.ch), F32)

        @pl.loop(0, z.side)
        def _(row):
            total = conv_row(z, grown, taps, row, start, True)
            totals[pl.ds(pl.multiple_of(row * z.side * 8, 8), z.side * 8), :] = total

        for tile in range(z.tiles):
            for row in range(z.side):
                spot = pl.ds(row * z.side * 8 + tile, z.side, stride=8)
                out[tile, row] = (totals[spot, :] + cotangent[tile, row].astype(F32)).astype(BF16)

        both_halves(z, plain, block_own[...], block_far[...])
        for tile in range(z.tiles):
            for row in range(z.side):
                spot = pl.ds(row * z.side * z.tiles + tile, z.side, stride=z.tiles)
                block_out[tile, row] = plain[spot, :].astype(BF16)

    out = shaped((z.tiles, z.side, z.side, z.ch), BF16)
    return call(
        body,
        (out, out),
        [slots, tissue, inbox, g_own, received, *block, cotangent, taps],
        2,
        [
            boxes(z, z.box2),
            flat_strips(z),
            field(z),
            pixel_major(z),
            pltpu.VMEM((z.pixels * 8, z.ch), F32),
        ],
        flops=2 * 49 * z.rows * z.ch,
    )


def finish(z, inbox, taps, scale):
    hid = z.hidden
    wide = 2 * z.ch
    groups = hid // LANES

    def body(inbox, taps_own, taps_far, grad_in, grad_out, grad_taps):
        grad_taps[...] = taps_own[...] + taps_far[...]
        for owner in range(z.owners):
            row = owner * z.share
            stop = row + z.share
            while row < stop:
                group, place = divmod(row, wide)
                count = min(stop - row, wide - place)
                at = owner * z.box3 + row - owner * z.share
                out = grad_in if group < groups else grad_out
                low = group % groups * LANES
                out[place : place + count, low : low + LANES] = (
                    inbox[at : at + count, :].astype(F32) * scale
                )
                row += count

    out = shaped((wide, hid), F32)
    return call(body, (out, out, shaped((7, 7, z.ch), F32)), [inbox, *taps])


def exchange_tiles(z, box):
    boxes = box.reshape(z.owners, -1, LANES)
    return lax.all_to_all(boxes, "tiles", split_axis=0, concat_axis=0, tiled=True).reshape(box.shape)


def swap_sub(piece):
    return lax.ppermute(piece, "sub", [(0, 1), (1, 0)])


def sum_tiles(z, part):
    step = 1
    while True:
        pairs = [(owner, owner ^ step) for owner in range(z.owners)]
        other = lax.ppermute(part, "tiles", pairs)
        step *= 2
        if step == z.owners:
            return part, other
        part = part + other


def local(
    tile_data,
    cotangent,
    neighbour,
    tissue,
    kernel,
    conv_bias,
    layer_norm_gain,
    layer_norm_bias,
    w_in,
    b_in,
    w_out,
    b_out,
    layer_scale,
):
    z = Sizes(tile_data.shape, w_in.shape[1], lax.axis_size("tiles"))
    scale = 1.0 / math.sqrt(z.owners * z.rows)

    outbox, slots = first_strips(z, neighbour, tile_data)
    inbox = exchange_tiles(z, outbox)

    w_in16 = w_in.astype(BF16)
    w_out16 = w_out.T.astype(BF16)
    vectors = jnp.concatenate([layer_norm_gain, layer_norm_bias, b_out, layer_scale, b_in])
    vectors = vectors.reshape(1, -1)
    rows_keep, rows_send, inner = local_part(
        z, tile_data, cotangent, kernel, conv_bias.reshape(1, z.ch)
    )
    w_in_both = (w_in16, swap_sub(w_in16))
    w_out_both = (w_out16, swap_sub(w_out16))
    v_both = (vectors, swap_sub(vectors))
    rows_both = (rows_keep, swap_sub(rows_send))
    ready = (rows_both[1], w_in_both[1], w_out_both[1], v_both[1])
    sp_own, sp_far = rim_conv(z, slots, tissue, inbox, inner, kernel, ready)
    g_own, block_own, block_far, keep, send = block_pass(
        z, (sp_own, swap_sub(sp_far)), rows_both, w_in_both, w_out_both, v_both
    )
    received = swap_sub(send)
    inbox2 = exchange_tiles(z, second_strips(z, slots, g_own, keep, received))
    taps = filter_gradient(z, slots, tissue, inbox, tile_data, g_own, received, scale)
    taps_own, taps_far = sum_tiles(z, taps)
    inbox3 = exchange_tiles(z, sum_shares(z, inbox2, (taps_own,)))
    tile_grad, block_out = second_conv(
        z, slots, tissue, inbox2, g_own, received, (block_own, swap_sub(block_far)), cotangent, kernel
    )
    grad_in, grad_out, grad_kernel = finish(z, inbox3, (taps_own, taps_far), scale)
    return block_out, tile_grad, grad_in, grad_out.T, grad_kernel


def solution(mesh):
    placed = (
        P(("slides", "tiles"), None, None, "sub"),
        P(("slides", "tiles"), None, None, "sub"),
        P(("slides", "tiles"), None),
        P(("slides", "tiles"), None),
        P(None, None, "sub"),
        P("sub"),
        P("sub"),
        P("sub"),
        P(None, "sub"),
        P("sub"),
        P("sub", None),
        P("sub"),
        P("sub"),
    )
    return jax.shard_map(
        local,
        mesh=mesh,
        in_specs=placed,
        out_specs=(
            P(("slides", "tiles"), None, None, "sub"),
            P(("slides", "tiles"), None, None, "sub"),
            P("slides", "sub"),
            P(("slides", "sub"), None),
            P("slides", None, "sub"),
        ),
        check_vma=False,
    )
```

```python
import math

import jax
import jax.numpy as jnp
from jax import lax
from jax.experimental import pallas as pl
from jax.experimental.pallas import tpu as pltpu
from jax.sharding import PartitionSpec as P

eps_norm = 1e-06
root_half = 0.7071067811865476
inv_root_tau = 0.3989422804014327
served_kind = (1, 0, 3, 2, 1, 1, 0, 0)
opposite = (1, 0, 3, 2, 7, 6, 5, 4)
LANES = 128
FIRST_VMEM = 60
F32 = jnp.float32
BF16 = jnp.bfloat16


def round_up(value, step):
    return -(-value // step) * step


def call(body, outs, operands, scalars=0, scratch=(), flops=0, vmem=16, after=(), **specs):
    spaces = specs.pop("spaces", None)
    if spaces is None:
        spaces = [pltpu.SMEM] * scalars + [pltpu.VMEM] * (len(operands) - scalars)
    count = len(operands)
    stop = count + len(after)

    def run(*refs):
        body(*refs[:count], *refs[stop:])

    return pl.pallas_call(
        run,
        out_shape=outs,
        in_specs=[pl.BlockSpec(memory_space=space) for space in [*spaces, *[pl.ANY] * len(after)]],
        scratch_shapes=list(scratch),
        compiler_params=pltpu.CompilerParams(vmem_limit_bytes=vmem << 20),
        cost_estimate=pl.CostEstimate(
            flops=flops,
            transcendentals=0,
            bytes_accessed=sum(o.size * o.dtype.itemsize for o in operands),
        ),
        **specs,
    )(*operands, *after)


def shaped(shape, dtype):
    return jax.ShapeDtypeStruct(shape, dtype)


class Sizes:
    def __init__(self, tile_shape, hidden, owners):
        self.tiles, self.side, _, self.ch = tile_shape
        self.hidden = hidden
        self.owners = owners
        self.capacity = max(2, 8 * self.tiles // owners)
        self.links = 8 * self.tiles
        self.pixels = self.side * self.side
        self.rows = self.pixels * self.tiles
        self.half = self.rows // 2
        self.extra = LANES - self.ch
        self.groups = self.ch // self.extra
        self.strip = 3 * self.side * self.ch // LANES
        self.tail = 3 * self.side - self.strip
        self.far = self.side + 3
        self.wide = self.side + 6
        self.box1 = round_up(self.capacity * self.strip, 8)
        self.weight_rows = 2 * (2 * self.ch) * hidden // LANES
        self.share = self.weight_rows // owners
        self.halo_at = round_up(self.share, 8)
        self.box2 = round_up(self.halo_at + self.capacity * self.strip, 8)
        self.box3 = round_up(self.share, 8)
        self.taps_at = round_up(self.share, 16)
        self.message = round_up(self.taps_at + 49, 16)
        self.paired = owners in (4, 8)

    def owner_of(self, link):
        factor = -(-65536 // self.tiles)
        assert self.owners * self.tiles * (factor * self.tiles - 65536) < 65536
        return (link * factor) >> 16


def rank_links(z, neighbour, counts, slots):
    @pl.loop(0, z.owners)
    def _(owner):
        counts[owner] = 0

    for link in range(z.links):
        owner = z.owner_of(neighbour[link // 8, link % 8])
        rank = counts[owner]
        counts[owner] = rank + 1
        slots[link] = owner
        slots[z.links + link] = jnp.minimum(rank, z.capacity - 1)
    for link in range(z.links):
        slot = neighbour[link // 8, link % 8] - slots[link] * z.tiles
        slots[2 * z.links + link] = slots[z.links + slot * 8 + opposite[link % 8]]


def pack_strips(z, load_row, load_col, slots, strips, outbox, box, offset):
    direct = z.strip - 2 * z.side
    for tile in range(z.tiles):
        for kind in range(4):
            base = (tile * 4 + kind) * 32
            for line in range(3):
                place = z.side - 3 + line if kind in (0, 2) else line
                value = load_row(tile, place) if kind < 2 else load_col(tile, place)
                start = base + line * z.side
                if line < 2:
                    strips[start : start + z.side, 0 : z.ch] = value
                    continue
                strips[start : start + direct, 0 : z.ch] = value[0:direct]
                for group in range(z.groups):
                    low = base + group * z.tail
                    strips[low : low + z.tail, z.ch : LANES] = value[
                        direct:, group * z.extra : (group + 1) * z.extra
                    ]
    for link in range(z.links):
        base = (link // 8 * 4 + served_kind[link % 8]) * 32
        low = slots[link] * box + offset + slots[2 * z.links + link] * z.strip
        outbox[pl.ds(low, z.strip), :] = strips[base : base + z.strip, :]


def assemble(z, inbox, box, offset, slots, tissue, flat, grown):
    pitch = z.wide * 8
    for link in range(z.links):
        low = slots[link] * box + offset + slots[z.links + link] * z.strip
        value = inbox[pl.ds(low, z.strip), :]
        value = jnp.where(tissue[link // 8, link % 8] > 0, value, 0.0)
        base = link * 40
        flat[base : base + z.strip, :] = value[:, 0 : z.ch]
        low = base + z.strip
        for group in range(z.groups):
            flat[low : low + z.tail, group * z.extra : (group + 1) * z.extra] = value[
                group * z.tail : (group + 1) * z.tail, z.ch : LANES
            ]
    far = z.far
    for tile in range(z.tiles):
        for side in range(8):
            base = (tile * 8 + side) * 40
            for line in range(3):
                start = base + line * z.side
                if side in (0, 1):
                    row = line if side == 0 else far + line
                    spot = pl.ds((row * z.wide + 3) * 8 + tile, z.side, stride=8)
                    grown[spot, :] = flat[start : start + z.side, :]
                elif side in (2, 3):
                    col = line if side == 2 else far + line
                    spot = pl.ds((3 * z.wide + col) * 8 + tile, z.side, stride=pitch)
                    grown[spot, :] = flat[start : start + z.side, :]
                else:
                    row = line if side in (4, 5) else far + line
                    col = 0 if side in (4, 6) else far
                    start += z.side - 3 if side in (4, 6) else 0
                    spot = pl.ds((row * z.wide + col) * 8 + tile, 3, stride=8)
                    grown[spot, :] = flat[start : start + 3, :]


def inner_spot(z, tile, row):
    return pl.ds(((row + 3) * z.wide + 3) * 8 + tile, z.side, stride=8)


def fill_inner(z, grown, tile_data):
    for tile in range(z.tiles):
        for row in range(z.side):
            grown[inner_spot(z, tile, row), :] = tile_data[tile, row].astype(F32)


def conv_row(z, grown, taps, row, start, flipped):
    line = z.wide * 8
    total = start
    for a in range(7):
        band = grown[pl.ds(pl.multiple_of((row + a) * line, 8), line), :]
        for b in range(7):
            tap = taps[6 - a, 6 - b : 7 - b, :] if flipped else taps[a, b : b + 1, :]
            total = total + band[b * 8 : (b + z.side) * 8] * tap
    return total


def rim_row(z, grown, taps, row, start, flipped):
    total = start
    inner = []

    def tap(a, b):
        return taps[6 - a, 6 - b : 7 - b, :] if flipped else taps[a, b : b + 1, :]

    for a in range(7):
        at = (row + a) * z.wide * 8
        if 3 <= row + a < z.far:
            inner.append((a, at))
            continue
        for b in range(7):
            low = at + b * 8
            total = total + grown[low : low + z.side * 8, :] * tap(a, b)
    pieces = [total[col * 8 : (col + 1) * 8] for col in range(z.side)]
    for a, at in inner:
        for col in range(z.side):
            for b in range(7):
                if col + b < 3 or col + b >= z.far:
                    low = at + (col + b) * 8
                    pieces[col] = pieces[col] + grown[low : low + 8, :] * tap(a, b)
    return pieces


def field(z):
    return pltpu.VMEM((z.wide * z.wide * 8, z.ch), F32)


def boxes(z, box):
    return pltpu.VMEM((z.owners * box, LANES), F32)


def flat_strips(z):
    return pltpu.VMEM((z.links * 40, z.ch), F32)


def packed_strips(z):
    return pltpu.VMEM((z.tiles * 4 * 32, LANES), F32)


def pixel_major(z):
    return pltpu.VMEM((z.rows, z.ch), F32)


def first_strips(z, neighbour, tile_data):
    def body(neighbour_hbm, tile_hbm, out, slots, neighbour, tile_data, sems, counts, plain, strips, box):
        fetch_links = pltpu.make_async_copy(neighbour_hbm, neighbour, sems.at[0])
        fetch_tiles = pltpu.make_async_copy(tile_hbm, tile_data, sems.at[1])
        fetch_links.start()
        fetch_tiles.start()
        fetch_links.wait()
        rank_links(z, neighbour, counts, slots)
        fetch_tiles.wait()
        for tile in range(z.tiles):
            for row in range(z.side):
                at = (tile * z.side + row) * z.side
                plain[at : at + z.side, :] = tile_data[tile, row].astype(F32)

        def load_row(tile, row):
            return plain[pl.ds((tile * z.side + row) * z.side, z.side), :]

        def load_col(tile, col):
            return plain[pl.ds(tile * z.pixels + col, z.side, stride=z.side), :]

        pack_strips(z, load_row, load_col, slots, strips, box, z.box1, 0)
        out[...] = box[...].astype(BF16)

    rows = z.owners * z.box1
    return call(
        body,
        (shaped((rows, LANES), BF16), shaped((3 * z.links,), jnp.int32)),
        [neighbour, tile_data],
        spaces=[pl.ANY, pl.ANY],
        vmem=FIRST_VMEM,
        out_specs=(
            pl.BlockSpec(memory_space=pltpu.VMEM),
            pl.BlockSpec(memory_space=pltpu.SMEM),
        ),
        scratch=[
            pltpu.SMEM(neighbour.shape, jnp.int32),
            pltpu.VMEM(tile_data.shape, BF16),
            pltpu.SemaphoreType.DMA((2,)),
            pltpu.SMEM((z.owners,), jnp.int32),
            pixel_major(z),
            packed_strips(z),
            boxes(z, z.box1),
        ],
    )


def local_part(z, slots, tile_data, cotangent, taps, conv_bias):
    def body(slots, tile_data, cotangent, taps, bias, keep, send, out, links, work, grown):
        for place in range(3 * z.links):
            links[place] = slots[place]
        core = lax.axis_index("sub")
        for which, block in enumerate((tile_data, cotangent)):
            for tile in range(z.tiles):
                for row in range(z.side):
                    spot = pl.ds(row * z.side * z.tiles + tile, z.side, stride=z.tiles)
                    work[spot, :] = block[tile, row].astype(F32)
            at = which * z.half
            own = pl.multiple_of(core * z.half, 16)
            far = pl.multiple_of((1 - core) * z.half, 16)
            keep[at : at + z.half, :] = work[pl.ds(own, z.half), :].astype(BF16)
            send[at : at + z.half, :] = work[pl.ds(far, z.half), :].astype(BF16)
        grown[...] = jnp.zeros_like(grown)
        fill_inner(z, grown, tile_data)
        start = jnp.broadcast_to(bias[...], (z.side * 8, z.ch))

        @pl.loop(0, z.side)
        def _(row):
            total = conv_row(z, grown, taps, row, start, False)
            out[pl.ds(pl.multiple_of(row * z.side * 8, 8), z.side * 8), :] = total

    rows = shaped((2 * z.half, z.ch), BF16)
    return call(
        body,
        (rows, rows, shaped((z.pixels * 8, z.ch), F32), shaped(slots.shape, jnp.int32)),
        [slots, tile_data, cotangent, taps, conv_bias],
        1,
        scratch=[pixel_major(z), field(z)],
        out_specs=tuple(
            pl.BlockSpec(memory_space=space) for space in [pltpu.VMEM] * 3 + [pltpu.SMEM]
        ),
        flops=2 * 49 * z.rows * z.ch,
    )


def rim_conv(z, slots, tissue, inbox, inner, taps, after):
    def body(slots, tissue, inbox, inner, taps, own, far, box, flat, grown, whole):
        core = lax.axis_index("sub")
        box[...] = inbox[...].astype(F32)
        assemble(z, box, z.box1, 0, slots, tissue, flat, grown)
        for row in range(z.side):
            start = inner[row * z.side * 8 : (row + 1) * z.side * 8, :]
            for col, piece in enumerate(rim_row(z, grown, taps, row, start, False)):
                at = (row * z.side + col) * z.tiles
                whole[at : at + z.tiles, :] = piece[0 : z.tiles]
        own[...] = whole[pl.ds(pl.multiple_of(core * z.half, 8), z.half), :]
        far[...] = whole[pl.ds(pl.multiple_of((1 - core) * z.half, 8), z.half), :]

    out = shaped((z.half, z.ch), F32)
    return call(
        body,
        (out, out),
        [slots, tissue, inbox, inner, taps],
        2,
        [boxes(z, z.box1), flat_strips(z), field(z), pixel_major(z)],
        after=after,
    )


ACROSS = (((1,), (1,)), ((), ()))
DOWN = (((0,), (0,)), ((), ()))


def join(first, own, far):
    return jnp.where(
        first, jnp.concatenate([own, far], axis=1), jnp.concatenate([far, own], axis=1)
    )


def both_vectors(z, first, v_own, v_far, index):
    at = index * z.ch
    return join(first, v_own[:, at : at + z.ch], v_far[:, at : at + z.ch])


def block_pass(z, spatial, rows, w_in, w_out, vectors):
    hid = z.hidden
    wide = 2 * z.ch

    def body(sp_own, sp_far, row_own, row_far, wi_own, wi_far, wo_own, wo_far, v_own,
             v_far, g_own, block_own, block_far, keep, send, normed_s, branch_s, pre_s, gact_s, act_s, gpre_s, xhat_s, inv_s):
        first = lax.axis_index("sub") == 0
        gain, shift, b_out, layer_scale = [
            both_vectors(z, first, v_own, v_far, index) for index in range(4)
        ]
        flat = join(first, sp_own[...], sp_far[...])
        centre = flat - jnp.sum(flat, axis=1, keepdims=True) * (1.0 / wide)
        var = jnp.sum(centre * centre, axis=1, keepdims=True) * (1.0 / wide)
        inverse = lax.rsqrt(var + eps_norm)
        xhat = centre * inverse
        xhat_s[...] = xhat
        inv_s[...] = inverse
        normed_s[...] = (xhat * gain + shift).astype(BF16)
        normed = normed_s[...]
        cot = join(first, row_own[z.half :, :].astype(F32), row_far[z.half :, :].astype(F32))
        branch_s[...] = (layer_scale * cot).astype(BF16)
        g_branch = branch_s[...]
        for side, (wi, wo, vec) in enumerate(((wi_own, wo_own, v_own), (wi_far, wo_far, v_far))):
            at = side * hid
            b_in = vec[:, 4 * z.ch : 4 * z.ch + hid]
            pre_s[:, at : at + hid] = jnp.dot(normed, wi[...], preferred_element_type=F32) + b_in
            gact_s[:, at : at + hid] = jnp.dot(g_branch, wo[...], preferred_element_type=F32)

        @pl.loop(0, z.half // 16)
        def _(step):
            spot = pl.ds(pl.multiple_of(step * 16, 16), 16)
            pre = pre_s[spot, :]
            cdf = 0.5 * (1.0 + lax.erf(pre * root_half))
            act_s[spot, :] = (pre * cdf).astype(BF16)
            slope = cdf + pre * jnp.exp(-0.5 * pre * pre) * inv_root_tau
            gpre_s[spot, :] = (gact_s[spot, :] * slope).astype(BF16)

        g_normed = lax.dot_general(
            gpre_s[:, 0:hid], wi_own[...], ACROSS, preferred_element_type=F32
        ) + lax.dot_general(gpre_s[:, hid:], wi_far[...], ACROSS, preferred_element_type=F32)
        xhat = xhat_s[...]
        leading = g_normed * gain
        mean_h = jnp.sum(leading, axis=1, keepdims=True) * (1.0 / wide)
        mean_hx = jnp.sum(leading * xhat, axis=1, keepdims=True) * (1.0 / wide)
        g_rows = inv_s[...] * (leading - mean_h - xhat * mean_hx)
        branch = (
            lax.dot_general(act_s[:, 0:hid], wo_own[...], ACROSS, preferred_element_type=F32)
            + lax.dot_general(act_s[:, hid:], wo_far[...], ACROSS, preferred_element_type=F32)
            + b_out
        )
        inner = join(
            first, row_own[0 : z.half, :].astype(F32), row_far[0 : z.half, :].astype(F32)
        )
        block = inner + layer_scale * branch

        def part(value, mine):
            low, high = value[:, 0 : z.ch], value[:, z.ch :]
            return jnp.where(first == mine, low, high).astype(BF16)

        g_own[...] = part(g_rows, True)
        block_own[...] = part(block, True)
        send[0 : z.half, 0 : z.ch] = part(g_rows, False)
        block_far[...] = part(block, False)
        for side in range(2):
            at = side * hid
            ref, low = (keep, 0) if side == 0 else (send, z.half)
            for left, right in ((normed, gpre_s), (g_branch, act_s)):
                grad = lax.dot_general(
                    left, right[:, at : at + hid], DOWN, preferred_element_type=F32
                )
                for group in range(hid // LANES):
                    lanes = slice(group * LANES, (group + 1) * LANES)
                    ref[low : low + wide, :] = grad[:, lanes].astype(ref.dtype)
                    low += wide

    rows_out = shaped((z.half, z.ch), BF16)
    return call(
        body,
        (
            rows_out,
            rows_out,
            rows_out,
            shaped((z.weight_rows, LANES), F32),
            shaped((z.half + z.weight_rows, LANES), BF16),
        ),
        [*spatial, *rows, *w_in, *w_out, *vectors],
        0,
        [
            pltpu.VMEM((z.half, wide), BF16),
            pltpu.VMEM((z.half, wide), BF16),
            pltpu.VMEM((z.half, 2 * hid), F32),
            pltpu.VMEM((z.half, 2 * hid), F32),
            pltpu.VMEM((z.half, 2 * hid), BF16),
            pltpu.VMEM((z.half, 2 * hid), BF16),
            pltpu.VMEM((z.half, wide), F32),
            pltpu.VMEM((z.half, 1), F32),
        ],
        flops=12 * z.half * wide * 2 * hid,
    )


def both_halves(z, work, own, far):
    core = lax.axis_index("sub")
    work[pl.ds(pl.multiple_of(core * z.half, 16), z.half), :] = own.astype(F32)
    work[pl.ds(pl.multiple_of((1 - core) * z.half, 16), z.half), :] = far.astype(F32)


def second_strips(z, slots, g_own, keep, received):
    def body(slots, g_own, keep, received, out, plain, strips, box):
        both_halves(z, plain, g_own[...], received[0 : z.half, 0 : z.ch])
        for owner in range(z.owners):
            at = owner * z.share
            low = z.half + at
            box[owner * z.box2 : owner * z.box2 + z.share, :] = keep[
                at : at + z.share, :
            ] + received[low : low + z.share, :].astype(F32)

        def load_row(tile, row):
            return plain[pl.ds(row * z.side * z.tiles + tile, z.side, stride=z.tiles), :]

        def load_col(tile, col):
            return plain[pl.ds(col * z.tiles + tile, z.side, stride=z.side * z.tiles), :]

        pack_strips(z, load_row, load_col, slots, strips, box, z.box2, z.halo_at)
        out[...] = box[...].astype(BF16)

    return call(
        body,
        shaped((z.owners * z.box2, LANES), BF16),
        [slots, g_own, keep, received],
        1,
        [pixel_major(z), packed_strips(z), boxes(z, z.box2)],
    )


def filter_gradient(z, slots, tissue, inbox, tile_data, g_own, received, scale):
    def body(slots, tissue, inbox, tile_data, g_own, received, taps, box, flat, grown, plain,
             g_field, sums):
        box[...] = inbox[...].astype(F32)
        assemble(z, box, z.box1, 0, slots, tissue, flat, grown)
        fill_inner(z, grown, tile_data)
        empty = jnp.zeros((z.wide * z.wide, z.ch), F32)
        for tile in range(z.tiles, 8):
            grown[pl.ds(tile, z.wide * z.wide, stride=8), :] = empty
        both_halves(z, plain, g_own[...], received[0 : z.half, 0 : z.ch])
        g_field[...] = jnp.zeros_like(g_field)
        for tile in range(z.tiles):
            g_field[pl.ds(tile, z.pixels, stride=8), :] = plain[
                pl.ds(tile, z.pixels, stride=z.tiles), :
            ]
        sums[...] = jnp.zeros_like(sums)
        line = z.wide * 8

        @pl.loop(0, z.side)
        def _(row):
            g_row = g_field[pl.ds(pl.multiple_of(row * z.side * 8, 8), z.side * 8), :]
            for a in range(7):
                band = grown[pl.ds(pl.multiple_of((row + a) * line, 8), line), :]
                for b in range(7):
                    product = band[b * 8 : (b + z.side) * 8] * g_row
                    total = product[0:8]
                    for col in range(1, z.side):
                        total = total + product[col * 8 : (col + 1) * 8]
                    at = (a * 7 + b) * 8
                    sums[at : at + 8, :] += total

        for a in range(7):
            rows = sums[a * 56 : (a + 1) * 56, :].reshape(7, 8, z.ch)
            taps[a] = jnp.sum(rows, axis=1) * scale

    return call(
        body,
        shaped((7, 7, z.ch), F32),
        [slots, tissue, inbox, tile_data, g_own, received],
        2,
        [
            boxes(z, z.box1),
            flat_strips(z),
            field(z),
            pixel_major(z),
            pltpu.VMEM((z.pixels * 8, z.ch), F32),
            pltpu.VMEM((49 * 8, z.ch), F32),
        ],
        flops=2 * 49 * z.rows * z.ch,
    )


def sum_shares(z, inbox, after):
    def body(inbox, out):
        total = inbox[0 : z.share, :].astype(F32)
        for owner in range(1, z.owners):
            at = owner * z.box2
            total = total + inbox[at : at + z.share, :].astype(F32)
        share = total.astype(BF16)
        for owner in range(z.owners):
            at = owner * z.box3
            out[at : at + z.share, :] = share

    return call(body, shaped((z.owners * z.box3, LANES), BF16), [inbox], after=after)


def second_inner(z, g_own, received, block, cotangent, taps):
    def body(g_own, received, block_own, block_far, cotangent, taps, out, block_out, plain, grown, cot):
        both_halves(z, plain, block_own[...], block_far[...])
        for tile in range(z.tiles):
            for row in range(z.side):
                spot = pl.ds(row * z.side * z.tiles + tile, z.side, stride=z.tiles)
                block_out[tile, row] = plain[spot, :].astype(BF16)
        both_halves(z, plain, g_own[...], received[0 : z.half, 0 : z.ch])
        grown[...] = jnp.zeros_like(grown)
        for tile in range(z.tiles):
            for row in range(z.side):
                spot = pl.ds(row * z.side * z.tiles + tile, z.side, stride=z.tiles)
                grown[inner_spot(z, tile, row), :] = plain[spot, :]
                spot = pl.ds(row * z.side * 8 + tile, z.side, stride=8)
                cot[spot, :] = cotangent[tile, row].astype(F32)

        @pl.loop(0, z.side)
        def _(row):
            spot = pl.ds(pl.multiple_of(row * z.side * 8, 8), z.side * 8)
            out[spot, :] = conv_row(z, grown, taps, row, cot[spot, :], True)

    return call(
        body,
        (
            shaped((z.pixels * 8, z.ch), F32),
            shaped((z.tiles, z.side, z.side, z.ch), BF16),
        ),
        [g_own, received, *block, cotangent, taps],
        0,
        [pixel_major(z), field(z), pltpu.VMEM((z.pixels * 8, z.ch), F32)],
        flops=2 * 49 * z.rows * z.ch,
    )


def second_rim(z, slots, tissue, inbox, inner, taps, after):
    def body(slots, tissue, inbox, inner, taps, out, box, flat, grown, totals):
        box[...] = inbox[...].astype(F32)
        assemble(z, box, z.box2, z.halo_at, slots, tissue, flat, grown)
        for row in range(z.side):
            start = inner[row * z.side * 8 : (row + 1) * z.side * 8, :]
            for col, piece in enumerate(rim_row(z, grown, taps, row, start, True)):
                at = (row * z.side + col) * 8
                totals[at : at + 8, :] = piece
            for tile in range(z.tiles):
                spot = pl.ds(row * z.side * 8 + tile, z.side, stride=8)
                out[tile, row] = totals[spot, :].astype(BF16)

    return call(
        body,
        shaped((z.tiles, z.side, z.side, z.ch), BF16),
        [slots, tissue, inbox, inner, taps],
        2,
        [
            boxes(z, z.box2),
            flat_strips(z),
            field(z),
            pltpu.VMEM((z.pixels * 8, z.ch), F32),
        ],
        after=after,
    )


def share_message(z, inbox, taps, after):
    def body(inbox, taps_own, taps_far, out):
        total = inbox[0 : z.share, :].astype(F32)
        for owner in range(1, z.owners):
            at = owner * z.box2
            total = total + inbox[at : at + z.share, :].astype(F32)
        out[0 : z.share, :] = total.astype(BF16)
        rows = [taps_own[a] + taps_far[a] for a in range(7)]
        low = z.taps_at
        out[low : low + 49, 0 : z.ch] = jnp.concatenate(rows, axis=0).astype(BF16)

    return call(body, shaped((z.message, LANES), BF16), [inbox, *taps], after=after)


def column(z, messages):
    count = len(messages)

    def body(*refs):
        messages, (out, taps, work) = refs[:count], refs[count:]
        line = lax.axis_index("tiles") // 2
        for step, message in enumerate(messages):
            place = jnp.bitwise_xor(line, step)
            at = pl.multiple_of(place * z.share, 16)
            out[pl.ds(at, z.share), :] = message[0 : z.share, :]
            at = pl.multiple_of(place * 56, 8)
            work[pl.ds(at, 49), :] = message[z.taps_at : z.taps_at + 49, 0 : z.ch].astype(F32)
        for a in range(7):
            total = work[a * 7 : a * 7 + 7, :]
            for place in range(1, count):
                low = place * 56 + a * 7
                total = total + work[low : low + 7, :]
            taps[a] = total

    return call(
        body,
        (shaped((count * z.share, LANES), BF16), shaped((7, 7, z.ch), F32)),
        messages,
        scratch=[pltpu.VMEM((count * 56, z.ch), F32)],
    )


def finish_columns(z, own, far, scale):
    hid = z.hidden
    wide = 2 * z.ch
    groups = hid // LANES

    def body(own, far, grad_in, grad_out):
        first = lax.axis_index("tiles") % 2 == 0
        for owner in range(z.owners):
            row = owner * z.share
            stop = row + z.share
            while row < stop:
                group, place = divmod(row, wide)
                count = min(stop - row, wide - place)
                at = owner // 2 * z.share + row - owner * z.share
                out = grad_in if group < groups else grad_out
                low = group % groups * LANES
                mine, other = own[at : at + count, :], far[at : at + count, :]
                value = jnp.where(first == (owner % 2 == 0), mine.astype(F32), other.astype(F32))
                out[place : place + count, low : low + LANES] = value * scale
                row += count

    out = shaped((wide, hid), F32)
    return call(body, (out, out), [own, far])


def finish(z, inbox, taps, scale):
    hid = z.hidden
    wide = 2 * z.ch
    groups = hid // LANES

    def body(inbox, taps_own, taps_far, grad_in, grad_out, grad_taps):
        grad_taps[...] = taps_own[...] + taps_far[...]
        for owner in range(z.owners):
            row = owner * z.share
            stop = row + z.share
            while row < stop:
                group, place = divmod(row, wide)
                count = min(stop - row, wide - place)
                at = owner * z.box3 + row - owner * z.share
                out = grad_in if group < groups else grad_out
                low = group % groups * LANES
                out[place : place + count, low : low + LANES] = (
                    inbox[at : at + count, :].astype(F32) * scale
                )
                row += count

    out = shaped((wide, hid), F32)
    return call(body, (out, out, shaped((7, 7, z.ch), F32)), [inbox, *taps])


def exchange_tiles(z, box):
    boxes = box.reshape(z.owners, -1, LANES)
    return lax.all_to_all(boxes, "tiles", split_axis=0, concat_axis=0, tiled=True).reshape(box.shape)


def swap_sub(piece):
    return lax.ppermute(piece, "sub", [(0, 1), (1, 0)])


def swap_tiles(z, piece, step):
    pairs = [(owner, owner ^ step) for owner in range(z.owners)]
    return lax.ppermute(piece, "tiles", pairs)


def sum_tiles(z, part):
    step = 1
    while True:
        other = swap_tiles(z, part, step)
        step *= 2
        if step == z.owners:
            return part, other
        part = part + other


def local(
    tile_data,
    cotangent,
    neighbour,
    tissue,
    kernel,
    conv_bias,
    layer_norm_gain,
    layer_norm_bias,
    w_in,
    b_in,
    w_out,
    b_out,
    layer_scale,
):
    z = Sizes(tile_data.shape, w_in.shape[1], lax.axis_size("tiles"))
    scale = 1.0 / math.sqrt(z.owners * z.rows)

    outbox, slots = first_strips(z, neighbour, tile_data)
    inbox = exchange_tiles(z, outbox)

    w_in16 = w_in.astype(BF16)
    w_out16 = w_out.T.astype(BF16)
    vectors = jnp.concatenate([layer_norm_gain, layer_norm_bias, b_out, layer_scale, b_in])
    vectors = vectors.reshape(1, -1)
    rows_keep, rows_send, inner, slots = local_part(
        z, slots, tile_data, cotangent, kernel, conv_bias.reshape(1, z.ch)
    )
    w_in_both = (w_in16, swap_sub(w_in16))
    w_out_both = (w_out16, swap_sub(w_out16))
    v_both = (vectors, swap_sub(vectors))
    rows_both = (rows_keep, swap_sub(rows_send))
    ready = (rows_both[1], w_in_both[1], w_out_both[1], v_both[1])
    sp_own, sp_far = rim_conv(z, slots, tissue, inbox, inner, kernel, ready)
    g_own, block_own, block_far, keep, send = block_pass(
        z, (sp_own, swap_sub(sp_far)), rows_both, w_in_both, w_out_both, v_both
    )
    received = swap_sub(send)
    inbox2 = exchange_tiles(z, second_strips(z, slots, g_own, keep, received))
    taps = filter_gradient(z, slots, tissue, inbox, tile_data, g_own, received, scale)
    inner2, block_out = second_inner(
        z, g_own, received, (block_own, swap_sub(block_far)), cotangent, kernel
    )
    if z.paired:
        taps_both = (taps, swap_tiles(z, taps, 1))
        message = share_message(z, inbox2, taps_both, (inner2,))
        steps = range(2, z.owners, 2)
        messages = [message] + [swap_tiles(z, message, step) for step in steps]
        own, grad_kernel = column(z, messages)
        far = swap_tiles(z, own, 1)
        tile_grad = second_rim(z, slots, tissue, inbox2, inner2, kernel, (own,))
        grad_in, grad_out = finish_columns(z, own, far, scale)
    else:
        taps_own, taps_far = sum_tiles(z, taps)
        inbox3 = exchange_tiles(z, sum_shares(z, inbox2, (taps_own, inner2)))
        tile_grad = second_rim(z, slots, tissue, inbox2, inner2, kernel, ())
        grad_in, grad_out, grad_kernel = finish(z, inbox3, (taps_own, taps_far), scale)
    return block_out, tile_grad, grad_in, grad_out.T, grad_kernel


def solution(mesh):
    placed = (
        P(("slides", "tiles"), None, None, "sub"),
        P(("slides", "tiles"), None, None, "sub"),
        P(("slides", "tiles"), None),
        P(("slides", "tiles"), None),
        P(None, None, "sub"),
        P("sub"),
        P("sub"),
        P("sub"),
        P(None, "sub"),
        P("sub"),
        P("sub", None),
        P("sub"),
        P("sub"),
    )
    return jax.shard_map(
        local,
        mesh=mesh,
        in_specs=placed,
        out_specs=(
            P(("slides", "tiles"), None, None, "sub"),
            P(("slides", "tiles"), None, None, "sub"),
            P("slides", "sub"),
            P(("slides", "sub"), None),
            P("slides", None, "sub"),
        ),
        check_vma=False,
    )
```

```python
import math

import jax
import jax.numpy as jnp
from jax import lax
from jax.experimental import pallas as pl
from jax.experimental.pallas import tpu as pltpu
from jax.sharding import PartitionSpec as P

eps_norm = 1e-06
root_half = 0.7071067811865476
inv_root_tau = 0.3989422804014327
served_kind = (1, 0, 3, 2, 1, 1, 0, 0)
opposite = (1, 0, 3, 2, 7, 6, 5, 4)
LANES = 128
FIRST_VMEM = 60
F32 = jnp.float32
BF16 = jnp.bfloat16


def round_up(value, step):
    return -(-value // step) * step


def call(body, outs, operands, scalars=0, scratch=(), flops=0, vmem=16, after=(), **specs):
    spaces = specs.pop("spaces", None)
    if spaces is None:
        spaces = [pltpu.SMEM] * scalars + [pltpu.VMEM] * (len(operands) - scalars)
    count = len(operands)
    stop = count + len(after)

    def run(*refs):
        body(*refs[:count], *refs[stop:])

    return pl.pallas_call(
        run,
        out_shape=outs,
        in_specs=[pl.BlockSpec(memory_space=space) for space in [*spaces, *[pl.ANY] * len(after)]],
        scratch_shapes=list(scratch),
        compiler_params=pltpu.CompilerParams(vmem_limit_bytes=vmem << 20),
        cost_estimate=pl.CostEstimate(
            flops=flops,
            transcendentals=0,
            bytes_accessed=sum(o.size * o.dtype.itemsize for o in operands),
        ),
        **specs,
    )(*operands, *after)


def shaped(shape, dtype):
    return jax.ShapeDtypeStruct(shape, dtype)


class Sizes:
    def __init__(self, tile_shape, hidden, owners):
        self.tiles, self.side, _, self.ch = tile_shape
        self.hidden = hidden
        self.owners = owners
        self.capacity = max(2, 8 * self.tiles // owners)
        self.links = 8 * self.tiles
        self.pixels = self.side * self.side
        self.rows = self.pixels * self.tiles
        self.half = self.rows // 2
        self.extra = LANES - self.ch
        self.groups = self.ch // self.extra
        self.strip = 3 * self.side * self.ch // LANES
        self.tail = 3 * self.side - self.strip
        self.far = self.side + 3
        self.wide = self.side + 6
        self.box1 = round_up(self.capacity * self.strip, 8)
        self.weight_rows = 2 * (2 * self.ch) * hidden // LANES
        self.share = self.weight_rows // owners
        self.halo_at = round_up(self.share, 8)
        self.box2 = round_up(self.halo_at + self.capacity * self.strip, 8)
        self.box3 = round_up(self.share, 8)
        self.taps_at = round_up(self.share, 16)
        self.message = round_up(self.taps_at + 49, 16)
        self.paired = owners in (4, 8)

    def owner_of(self, link):
        factor = -(-65536 // self.tiles)
        assert self.owners * self.tiles * (factor * self.tiles - 65536) < 65536
        return (link * factor) >> 16


def rank_links(z, neighbour, counts, slots):
    @pl.loop(0, z.owners)
    def _(owner):
        counts[owner] = 0

    for link in range(z.links):
        owner = z.owner_of(neighbour[link // 8, link % 8])
        rank = counts[owner]
        counts[owner] = rank + 1
        slots[link] = owner
        slots[z.links + link] = jnp.minimum(rank, z.capacity - 1)
    for link in range(z.links):
        slot = neighbour[link // 8, link % 8] - slots[link] * z.tiles
        slots[2 * z.links + link] = slots[z.links + slot * 8 + opposite[link % 8]]


def pack_strips(z, load_row, load_col, slots, strips, outbox, box, offset):
    direct = z.strip - 2 * z.side
    for tile in range(z.tiles):
        for kind in range(4):
            base = (tile * 4 + kind) * 32
            for line in range(3):
                place = z.side - 3 + line if kind in (0, 2) else line
                value = load_row(tile, place) if kind < 2 else load_col(tile, place)
                start = base + line * z.side
                if line < 2:
                    strips[start : start + z.side, 0 : z.ch] = value
                    continue
                strips[start : start + direct, 0 : z.ch] = value[0:direct]
                for group in range(z.groups):
                    low = base + group * z.tail
                    strips[low : low + z.tail, z.ch : LANES] = value[
                        direct:, group * z.extra : (group + 1) * z.extra
                    ]
    for link in range(z.links):
        base = (link // 8 * 4 + served_kind[link % 8]) * 32
        low = slots[link] * box + offset + slots[2 * z.links + link] * z.strip
        outbox[pl.ds(low, z.strip), :] = strips[base : base + z.strip, :]


def assemble(z, inbox, box, offset, slots, tissue, flat, grown):
    pitch = z.wide * 8
    for link in range(z.links):
        low = slots[link] * box + offset + slots[z.links + link] * z.strip
        value = inbox[pl.ds(low, z.strip), :]
        value = jnp.where(tissue[link // 8, link % 8] > 0, value, 0.0)
        base = link * 40
        flat[base : base + z.strip, :] = value[:, 0 : z.ch]
        low = base + z.strip
        for group in range(z.groups):
            flat[low : low + z.tail, group * z.extra : (group + 1) * z.extra] = value[
                group * z.tail : (group + 1) * z.tail, z.ch : LANES
            ]
    far = z.far
    for tile in range(z.tiles):
        for side in range(8):
            base = (tile * 8 + side) * 40
            for line in range(3):
                start = base + line * z.side
                if side in (0, 1):
                    row = line if side == 0 else far + line
                    spot = pl.ds((row * z.wide + 3) * 8 + tile, z.side, stride=8)
                    grown[spot, :] = flat[start : start + z.side, :]
                elif side in (2, 3):
                    col = line if side == 2 else far + line
                    spot = pl.ds((3 * z.wide + col) * 8 + tile, z.side, stride=pitch)
                    grown[spot, :] = flat[start : start + z.side, :]
                else:
                    row = line if side in (4, 5) else far + line
                    col = 0 if side in (4, 6) else far
                    start += z.side - 3 if side in (4, 6) else 0
                    spot = pl.ds((row * z.wide + col) * 8 + tile, 3, stride=8)
                    grown[spot, :] = flat[start : start + 3, :]


def inner_spot(z, tile, row):
    return pl.ds(((row + 3) * z.wide + 3) * 8 + tile, z.side, stride=8)


def fill_inner(z, grown, tile_data):
    for tile in range(z.tiles):
        for row in range(z.side):
            grown[inner_spot(z, tile, row), :] = tile_data[tile, row].astype(F32)


def conv_row(z, grown, taps, row, start, flipped):
    line = z.wide * 8
    total = start
    for a in range(7):
        band = grown[pl.ds(pl.multiple_of((row + a) * line, 8), line), :]
        for b in range(7):
            tap = taps[6 - a, 6 - b : 7 - b, :] if flipped else taps[a, b : b + 1, :]
            total = total + band[b * 8 : (b + z.side) * 8] * tap
    return total


def rim_row(z, grown, taps, row, start, flipped):
    total = start
    inner = []

    def tap(a, b):
        return taps[6 - a, 6 - b : 7 - b, :] if flipped else taps[a, b : b + 1, :]

    for a in range(7):
        at = (row + a) * z.wide * 8
        if 3 <= row + a < z.far:
            inner.append((a, at))
            continue
        for b in range(7):
            low = at + b * 8
            total = total + grown[low : low + z.side * 8, :] * tap(a, b)
    pieces = [total[col * 8 : (col + 1) * 8] for col in range(z.side)]
    for a, at in inner:
        for col in range(z.side):
            for b in range(7):
                if col + b < 3 or col + b >= z.far:
                    low = at + (col + b) * 8
                    pieces[col] = pieces[col] + grown[low : low + 8, :] * tap(a, b)
    return pieces


def field(z):
    return pltpu.VMEM((z.wide * z.wide * 8, z.ch), F32)


def boxes(z, box):
    return pltpu.VMEM((z.owners * box, LANES), F32)


def flat_strips(z):
    return pltpu.VMEM((z.links * 40, z.ch), F32)


def packed_strips(z):
    return pltpu.VMEM((z.tiles * 4 * 32, LANES), F32)


def pixel_major(z):
    return pltpu.VMEM((z.rows, z.ch), F32)


def first_strips(z, neighbour, tile_data):
    def body(neighbour_hbm, tile_hbm, out, slots, neighbour, tile_data, sems, counts, plain, strips, box):
        fetch_links = pltpu.make_async_copy(neighbour_hbm, neighbour, sems.at[0])
        fetch_tiles = pltpu.make_async_copy(tile_hbm, tile_data, sems.at[1])
        fetch_links.start()
        fetch_tiles.start()
        fetch_links.wait()
        rank_links(z, neighbour, counts, slots)
        fetch_tiles.wait()
        for tile in range(z.tiles):
            for row in range(z.side):
                at = (tile * z.side + row) * z.side
                plain[at : at + z.side, :] = tile_data[tile, row].astype(F32)

        def load_row(tile, row):
            return plain[pl.ds((tile * z.side + row) * z.side, z.side), :]

        def load_col(tile, col):
            return plain[pl.ds(tile * z.pixels + col, z.side, stride=z.side), :]

        pack_strips(z, load_row, load_col, slots, strips, box, z.box1, 0)
        out[...] = box[...].astype(BF16)

    rows = z.owners * z.box1
    return call(
        body,
        (shaped((rows, LANES), BF16), shaped((3 * z.links,), jnp.int32)),
        [neighbour, tile_data],
        spaces=[pl.ANY, pl.ANY],
        vmem=FIRST_VMEM,
        out_specs=(
            pl.BlockSpec(memory_space=pltpu.VMEM),
            pl.BlockSpec(memory_space=pltpu.SMEM),
        ),
        scratch=[
            pltpu.SMEM(neighbour.shape, jnp.int32),
            pltpu.VMEM(tile_data.shape, BF16),
            pltpu.SemaphoreType.DMA((2,)),
            pltpu.SMEM((z.owners,), jnp.int32),
            pixel_major(z),
            packed_strips(z),
            boxes(z, z.box1),
        ],
    )


def local_part(z, slots, tile_data, cotangent, taps, conv_bias):
    def body(slots, tile_data, cotangent, taps, bias, keep, send, out, links, work, grown):
        for place in range(3 * z.links):
            links[place] = slots[place]
        core = lax.axis_index("sub")
        for which, block in enumerate((tile_data, cotangent)):
            for tile in range(z.tiles):
                for row in range(z.side):
                    spot = pl.ds(row * z.side * z.tiles + tile, z.side, stride=z.tiles)
                    work[spot, :] = block[tile, row].astype(F32)
            at = which * z.half
            own = pl.multiple_of(core * z.half, 16)
            far = pl.multiple_of((1 - core) * z.half, 16)
            for ref, half in ((keep, own), (send, far)):
                ref[at : at + z.half, 0 : z.ch] = work[pl.ds(half, z.half), :].astype(BF16)
                ref[at : at + z.half, z.ch : LANES] = jnp.zeros((z.half, z.extra), BF16)
        grown[...] = jnp.zeros_like(grown)
        fill_inner(z, grown, tile_data)
        start = jnp.broadcast_to(bias[...], (z.side * 8, z.ch))

        @pl.loop(0, z.side)
        def _(row):
            total = conv_row(z, grown, taps, row, start, False)
            out[pl.ds(pl.multiple_of(row * z.side * 8, 8), z.side * 8), :] = total

    rows = shaped((2 * z.half, LANES), BF16)
    return call(
        body,
        (rows, rows, shaped((z.pixels * 8, z.ch), F32), shaped(slots.shape, jnp.int32)),
        [slots, tile_data, cotangent, taps, conv_bias],
        1,
        scratch=[pixel_major(z), field(z)],
        out_specs=tuple(
            pl.BlockSpec(memory_space=space) for space in [pltpu.VMEM] * 3 + [pltpu.SMEM]
        ),
        flops=2 * 49 * z.rows * z.ch,
    )


def rim_conv(z, slots, tissue, inbox, inner, taps, after):
    def body(slots, tissue, inbox, inner, taps, own, far, box, flat, grown, whole):
        core = lax.axis_index("sub")
        box[...] = inbox[...].astype(F32)
        assemble(z, box, z.box1, 0, slots, tissue, flat, grown)
        for row in range(z.side):
            start = inner[row * z.side * 8 : (row + 1) * z.side * 8, :]
            for col, piece in enumerate(rim_row(z, grown, taps, row, start, False)):
                at = (row * z.side + col) * z.tiles
                whole[at : at + z.tiles, :] = piece[0 : z.tiles]
        for out, half in ((own, core), (far, 1 - core)):
            out[:, 0 : z.ch] = whole[pl.ds(pl.multiple_of(half * z.half, 8), z.half), :]
            out[:, z.ch : LANES] = jnp.zeros((z.half, z.extra), F32)

    out = shaped((z.half, LANES), F32)
    return call(
        body,
        (out, out),
        [slots, tissue, inbox, inner, taps],
        2,
        [boxes(z, z.box1), flat_strips(z), field(z), pixel_major(z)],
        after=after,
    )


ACROSS = (((1,), (1,)), ((), ()))
DOWN = (((0,), (0,)), ((), ()))


def arrange_weights(z, w_in, w_out):
    hid = z.hidden

    def body(w_in, w_out, in_mine, out_mine, in_theirs, out_theirs):
        first = lax.axis_index("sub") == 0
        for w, mine, theirs in ((w_in, in_mine, in_theirs), (w_out, out_mine, out_theirs)):
            low, high = w[0 : z.ch, :], w[z.ch : 2 * z.ch, :]
            own = jnp.where(first, low, high).astype(BF16)
            far = jnp.where(first, high, low).astype(BF16)
            empty = jnp.zeros((z.extra, hid), BF16)
            for out, blocks in ((mine, (own, far)), (theirs, (far, own))):
                for place, block in enumerate(blocks):
                    at = place * LANES
                    out[at : at + z.ch, :] = block
                    out[at + z.ch : at + LANES, :] = empty

    return call(body, (shaped((2 * LANES, hid), BF16),) * 4, [w_in, w_out])


def block_pass(z, spatial, rows, w_in, w_out, vectors):
    hid = z.hidden
    wide = 2 * LANES
    every = 2 * z.ch

    def body(sp_own, sp_far, row_own, row_far, wi_own, wi_far, wo_own, wo_far, v_own, v_far,
             g_own, block_own, block_far, keep, send, normed_s, branch_s, pre_s, gact_s, act_s,
             gpre_s, xhat_s, inv_s):
        def vector(index):
            at = index * z.ch
            empty = jnp.zeros((1, z.extra), F32)
            own, far = v_own[:, at : at + z.ch], v_far[:, at : at + z.ch]
            return jnp.concatenate([own, empty, far, empty], axis=1)

        gain, shift, b_out, layer_scale = [vector(index) for index in range(4)]
        lanes = lax.broadcasted_iota(jnp.int32, (1, wide), 1)
        flat = jnp.concatenate([sp_own[...], sp_far[...]], axis=1)
        centre = flat - jnp.sum(flat, axis=1, keepdims=True) * (1.0 / every)
        centre = jnp.where(lanes % LANES < z.ch, centre, 0.0)
        var = jnp.sum(centre * centre, axis=1, keepdims=True) * (1.0 / every)
        inverse = lax.rsqrt(var + eps_norm)
        xhat = centre * inverse
        xhat_s[...] = xhat
        inv_s[...] = inverse
        normed_s[...] = (xhat * gain + shift).astype(BF16)
        normed = normed_s[...]
        cot = jnp.concatenate([row_own[z.half :, :], row_far[z.half :, :]], axis=1)
        branch_s[...] = (layer_scale * cot.astype(F32)).astype(BF16)
        g_branch = branch_s[...]
        for side, (wi, wo, vec) in enumerate(((wi_own, wo_own, v_own), (wi_far, wo_far, v_far))):
            at = side * hid
            b_in = vec[:, 4 * z.ch : 4 * z.ch + hid]
            pre_s[:, at : at + hid] = jnp.dot(normed, wi[...], preferred_element_type=F32) + b_in
            gact_s[:, at : at + hid] = jnp.dot(g_branch, wo[...], preferred_element_type=F32)

        @pl.loop(0, z.half // 48, unroll=1)
        def _(step):
            spot = pl.ds(pl.multiple_of(step * 48, 48), 48)
            for low in range(0, 2 * hid, 256):
                part = slice(low, low + 256)
                pre = pre_s[spot, part]
                cdf = 0.5 * (1.0 + lax.erf(pre * root_half))
                act_s[spot, part] = (pre * cdf).astype(BF16)
                slope = cdf + pre * jnp.exp(-0.5 * pre * pre) * inv_root_tau
                gpre_s[spot, part] = (gact_s[spot, part] * slope).astype(BF16)

        g_normed = lax.dot_general(
            gpre_s[:, 0:hid], wi_own[...], ACROSS, preferred_element_type=F32
        ) + lax.dot_general(gpre_s[:, hid:], wi_far[...], ACROSS, preferred_element_type=F32)
        xhat = xhat_s[...]
        leading = g_normed * gain
        mean_h = jnp.sum(leading, axis=1, keepdims=True) * (1.0 / every)
        mean_hx = jnp.sum(leading * xhat, axis=1, keepdims=True) * (1.0 / every)
        g_rows = (inv_s[...] * (leading - mean_h - xhat * mean_hx)).astype(BF16)
        g_own[...] = g_rows[:, 0:LANES]
        send[0 : z.half, :] = g_rows[:, LANES:]
        branch = layer_scale * (
            lax.dot_general(act_s[:, 0:hid], wo_own[...], ACROSS, preferred_element_type=F32)
            + lax.dot_general(act_s[:, hid:], wo_far[...], ACROSS, preferred_element_type=F32)
            + b_out
        )
        block_own[...] = (row_own[0 : z.half, :].astype(F32) + branch[:, 0:LANES]).astype(BF16)
        block_far[...] = (row_far[0 : z.half, :].astype(F32) + branch[:, LANES:]).astype(BF16)
        for side in range(2):
            at = side * hid
            ref, low = (keep, 0) if side == 0 else (send, z.half)
            for left, right in ((normed, gpre_s), (g_branch, act_s)):
                grad = lax.dot_general(
                    left, right[:, at : at + hid], DOWN, preferred_element_type=F32
                )
                for group in range(hid // LANES):
                    part = slice(group * LANES, (group + 1) * LANES)
                    for place in (0, LANES) if side == 0 else (LANES, 0):
                        ref[low : low + z.ch, :] = grad[place : place + z.ch, part].astype(ref.dtype)
                        low += z.ch

    rows_out = shaped((z.half, LANES), BF16)
    return call(
        body,
        (
            rows_out,
            rows_out,
            rows_out,
            shaped((z.weight_rows, LANES), F32),
            shaped((z.half + z.weight_rows, LANES), BF16),
        ),
        [*spatial, *rows, *w_in, *w_out, *vectors],
        0,
        [
            pltpu.VMEM((z.half, wide), BF16),
            pltpu.VMEM((z.half, wide), BF16),
            pltpu.VMEM((z.half, 2 * hid), F32),
            pltpu.VMEM((z.half, 2 * hid), F32),
            pltpu.VMEM((z.half, 2 * hid), BF16),
            pltpu.VMEM((z.half, 2 * hid), BF16),
            pltpu.VMEM((z.half, wide), F32),
            pltpu.VMEM((z.half, 1), F32),
        ],
        flops=12 * z.half * wide * 2 * hid,
    )


def both_halves(z, work, own, far):
    core = lax.axis_index("sub")
    work[pl.ds(pl.multiple_of(core * z.half, 16), z.half), :] = own.astype(F32)
    work[pl.ds(pl.multiple_of((1 - core) * z.half, 16), z.half), :] = far.astype(F32)


def second_strips(z, slots, g_own, keep, received):
    def body(slots, g_own, keep, received, out, plain, strips, box):
        both_halves(z, plain, g_own[:, 0 : z.ch], received[0 : z.half, 0 : z.ch])
        for owner in range(z.owners):
            at = owner * z.share
            low = z.half + at
            box[owner * z.box2 : owner * z.box2 + z.share, :] = keep[
                at : at + z.share, :
            ] + received[low : low + z.share, :].astype(F32)

        def load_row(tile, row):
            return plain[pl.ds(row * z.side * z.tiles + tile, z.side, stride=z.tiles), :]

        def load_col(tile, col):
            return plain[pl.ds(col * z.tiles + tile, z.side, stride=z.side * z.tiles), :]

        pack_strips(z, load_row, load_col, slots, strips, box, z.box2, z.halo_at)
        out[...] = box[...].astype(BF16)

    return call(
        body,
        shaped((z.owners * z.box2, LANES), BF16),
        [slots, g_own, keep, received],
        1,
        [pixel_major(z), packed_strips(z), boxes(z, z.box2)],
    )


def filter_gradient(z, slots, tissue, inbox, tile_data, g_own, received, scale):
    def body(slots, tissue, inbox, tile_data, g_own, received, taps, box, flat, grown, plain,
             g_field, sums):
        box[...] = inbox[...].astype(F32)
        assemble(z, box, z.box1, 0, slots, tissue, flat, grown)
        fill_inner(z, grown, tile_data)
        empty = jnp.zeros((z.wide * z.wide, z.ch), F32)
        for tile in range(z.tiles, 8):
            grown[pl.ds(tile, z.wide * z.wide, stride=8), :] = empty
        both_halves(z, plain, g_own[:, 0 : z.ch], received[0 : z.half, 0 : z.ch])
        g_field[...] = jnp.zeros_like(g_field)
        for tile in range(z.tiles):
            g_field[pl.ds(tile, z.pixels, stride=8), :] = plain[
                pl.ds(tile, z.pixels, stride=z.tiles), :
            ]
        sums[...] = jnp.zeros_like(sums)
        line = z.wide * 8

        @pl.loop(0, z.side)
        def _(row):
            g_row = g_field[pl.ds(pl.multiple_of(row * z.side * 8, 8), z.side * 8), :]
            for a in range(7):
                band = grown[pl.ds(pl.multiple_of((row + a) * line, 8), line), :]
                for b in range(7):
                    product = band[b * 8 : (b + z.side) * 8] * g_row
                    total = product[0:8]
                    for col in range(1, z.side):
                        total = total + product[col * 8 : (col + 1) * 8]
                    at = (a * 7 + b) * 8
                    sums[at : at + 8, :] += total

        for a in range(7):
            rows = sums[a * 56 : (a + 1) * 56, :].reshape(7, 8, z.ch)
            taps[a] = jnp.sum(rows, axis=1) * scale

    return call(
        body,
        shaped((7, 7, z.ch), F32),
        [slots, tissue, inbox, tile_data, g_own, received],
        2,
        [
            boxes(z, z.box1),
            flat_strips(z),
            field(z),
            pixel_major(z),
            pltpu.VMEM((z.pixels * 8, z.ch), F32),
            pltpu.VMEM((49 * 8, z.ch), F32),
        ],
        flops=2 * 49 * z.rows * z.ch,
    )


def sum_shares(z, inbox, after):
    def body(inbox, out):
        total = inbox[0 : z.share, :].astype(F32)
        for owner in range(1, z.owners):
            at = owner * z.box2
            total = total + inbox[at : at + z.share, :].astype(F32)
        share = total.astype(BF16)
        for owner in range(z.owners):
            at = owner * z.box3
            out[at : at + z.share, :] = share

    return call(body, shaped((z.owners * z.box3, LANES), BF16), [inbox], after=after)


def second_inner(z, g_own, received, block, cotangent, taps):
    def body(g_own, received, block_own, block_far, cotangent, taps, out, block_out, plain, grown, cot):
        both_halves(z, plain, block_own[:, 0 : z.ch], block_far[:, 0 : z.ch])
        for tile in range(z.tiles):
            for row in range(z.side):
                spot = pl.ds(row * z.side * z.tiles + tile, z.side, stride=z.tiles)
                block_out[tile, row] = plain[spot, :].astype(BF16)
        both_halves(z, plain, g_own[:, 0 : z.ch], received[0 : z.half, 0 : z.ch])
        grown[...] = jnp.zeros_like(grown)
        for tile in range(z.tiles):
            for row in range(z.side):
                spot = pl.ds(row * z.side * z.tiles + tile, z.side, stride=z.tiles)
                grown[inner_spot(z, tile, row), :] = plain[spot, :]
                spot = pl.ds(row * z.side * 8 + tile, z.side, stride=8)
                cot[spot, :] = cotangent[tile, row].astype(F32)

        @pl.loop(0, z.side)
        def _(row):
            spot = pl.ds(pl.multiple_of(row * z.side * 8, 8), z.side * 8)
            out[spot, :] = conv_row(z, grown, taps, row, cot[spot, :], True)

    return call(
        body,
        (
            shaped((z.pixels * 8, z.ch), F32),
            shaped((z.tiles, z.side, z.side, z.ch), BF16),
        ),
        [g_own, received, *block, cotangent, taps],
        0,
        [pixel_major(z), field(z), pltpu.VMEM((z.pixels * 8, z.ch), F32)],
        flops=2 * 49 * z.rows * z.ch,
    )


def second_rim(z, slots, tissue, inbox, inner, taps, messages, after):
    count = len(messages)

    def body(slots, tissue, inbox, inner, taps, *refs):
        messages, (out, *refs) = refs[:count], refs[count:]
        if count:
            grad_taps, box, flat, grown, totals, work = refs
            line = lax.axis_index("tiles") // 2
            for step, message in enumerate(messages):
                at = pl.multiple_of(jnp.bitwise_xor(line, step) * 56, 8)
                work[pl.ds(at, 49), :] = message[z.taps_at : z.taps_at + 49, 0 : z.ch].astype(F32)
            for a in range(7):
                total = work[a * 7 : a * 7 + 7, :]
                for place in range(1, count):
                    low = place * 56 + a * 7
                    total = total + work[low : low + 7, :]
                grad_taps[a] = total
        else:
            box, flat, grown, totals = refs
        box[...] = inbox[...].astype(F32)
        assemble(z, box, z.box2, z.halo_at, slots, tissue, flat, grown)
        for row in range(z.side):
            start = inner[row * z.side * 8 : (row + 1) * z.side * 8, :]
            for col, piece in enumerate(rim_row(z, grown, taps, row, start, True)):
                at = (row * z.side + col) * 8
                totals[at : at + 8, :] = piece
            for tile in range(z.tiles):
                spot = pl.ds(row * z.side * 8 + tile, z.side, stride=8)
                out[tile, row] = totals[spot, :].astype(BF16)

    outs = (shaped((z.tiles, z.side, z.side, z.ch), BF16), shaped((7, 7, z.ch), F32))
    scratch = [
        boxes(z, z.box2),
        flat_strips(z),
        field(z),
        pltpu.VMEM((z.pixels * 8, z.ch), F32),
        pltpu.VMEM((count * 56, z.ch), F32),
    ]
    if not count:
        outs, scratch = outs[0], scratch[:-1]
    return call(
        body, outs, [slots, tissue, inbox, inner, taps, *messages], 2, scratch, after=after
    )


def share_message(z, inbox, taps, after):
    def body(inbox, taps_own, taps_far, out):
        total = inbox[0 : z.share, :].astype(F32)
        for owner in range(1, z.owners):
            at = owner * z.box2
            total = total + inbox[at : at + z.share, :].astype(F32)
        out[0 : z.share, :] = total.astype(BF16)
        rows = [taps_own[a] + taps_far[a] for a in range(7)]
        low = z.taps_at
        out[low : low + 49, 0 : z.ch] = jnp.concatenate(rows, axis=0).astype(BF16)

    return call(body, shaped((z.message, LANES), BF16), [inbox, *taps], after=after)


def column(z, messages):
    count = len(messages)

    def body(*refs):
        messages, (out,) = refs[:count], refs[count:]
        line = lax.axis_index("tiles") // 2
        for step, message in enumerate(messages):
            at = pl.multiple_of(jnp.bitwise_xor(line, step) * z.share, 16)
            out[pl.ds(at, z.share), :] = message[0 : z.share, :]

    return call(body, shaped((count * z.share, LANES), BF16), messages)


def finish_share(z, grads, owner, share):
    core = lax.axis_index("sub")
    wide = 2 * z.ch
    groups = z.hidden // LANES
    row, stop = owner * z.share, (owner + 1) * z.share
    while row < stop:
        group, place = divmod(row, wide)
        side, place = divmod(place, z.ch)
        count = min(stop - row, z.ch - place)
        at = row - owner * z.share
        block = core if side == 0 else 1 - core
        spot = pl.ds(pl.multiple_of(block * z.ch, 8) + place, count)
        low = group % groups * LANES
        grads[group // groups][spot, low : low + LANES] = share(at, count)
        row += count


def finish(z, inbox, taps, scale):
    groups = z.hidden // LANES

    def body(inbox, taps_own, taps_far, grad_in, grad_out, grad_taps, work):
        grad_taps[...] = taps_own[...] + taps_far[...]
        for owner in range(z.owners):
            at = owner * z.box3
            work[owner * z.share : (owner + 1) * z.share, :] = (
                inbox[at : at + z.share, :].astype(F32) * scale
            )
        core = lax.axis_index("sub")
        for index, grad in enumerate((grad_in, grad_out)):
            for group in range(groups):
                for side, block in enumerate((core, 1 - core)):
                    low = ((index * groups + group) * 2 + side) * z.ch
                    spot = pl.ds(pl.multiple_of(block * z.ch, 8), z.ch)
                    lanes = slice(group * LANES, (group + 1) * LANES)
                    grad[spot, lanes] = work[low : low + z.ch, :]

    out = shaped((2 * z.ch, z.hidden), F32)
    return call(
        body,
        (out, out, shaped((7, 7, z.ch), F32)),
        [inbox, *taps],
        scratch=[pltpu.VMEM((z.weight_rows, LANES), F32)],
    )


def finish_columns(z, own, far, scale):
    def body(own, far, grad_in, grad_out):
        first = lax.axis_index("tiles") % 2 == 0
        for owner in range(z.owners):

            def share(at, count, owner=owner):
                low = owner // 2 * z.share + at
                mine = own[low : low + count, :].astype(F32)
                other = far[low : low + count, :].astype(F32)
                pair = (mine, other) if owner % 2 == 0 else (other, mine)
                return jnp.where(first, *pair) * scale

            finish_share(z, (grad_in, grad_out), owner, share)

    out = shaped((2 * z.ch, z.hidden), F32)
    return call(body, (out, out), [own, far])


def exchange_tiles(z, box):
    boxes = box.reshape(z.owners, -1, LANES)
    return lax.all_to_all(boxes, "tiles", split_axis=0, concat_axis=0, tiled=True).reshape(box.shape)


def swap_sub(piece):
    return lax.ppermute(piece, "sub", [(0, 1), (1, 0)])


def swap_tiles(z, piece, step):
    pairs = [(owner, owner ^ step) for owner in range(z.owners)]
    return lax.ppermute(piece, "tiles", pairs)


def sum_tiles(z, part):
    step = 1
    while True:
        other = swap_tiles(z, part, step)
        step *= 2
        if step == z.owners:
            return part, other
        part = part + other


def local(
    tile_data,
    cotangent,
    neighbour,
    tissue,
    kernel,
    conv_bias,
    layer_norm_gain,
    layer_norm_bias,
    w_in,
    b_in,
    w_out,
    b_out,
    layer_scale,
):
    z = Sizes(tile_data.shape, w_in.shape[1], lax.axis_size("tiles"))
    scale = 1.0 / math.sqrt(z.owners * z.rows)

    outbox, slots = first_strips(z, neighbour, tile_data)
    inbox = exchange_tiles(z, outbox)

    in_mine, out_mine, in_theirs, out_theirs = arrange_weights(z, w_in, w_out.T)
    vectors = jnp.concatenate([layer_norm_gain, layer_norm_bias, b_out, layer_scale, b_in])
    vectors = vectors.reshape(1, -1)
    rows_keep, rows_send, inner, slots = local_part(
        z, slots, tile_data, cotangent, kernel, conv_bias.reshape(1, z.ch)
    )
    w_in_both = (in_mine, swap_sub(in_theirs))
    w_out_both = (out_mine, swap_sub(out_theirs))
    v_both = (vectors, swap_sub(vectors))
    rows_both = (rows_keep, swap_sub(rows_send))
    ready = (rows_both[1], w_in_both[1], w_out_both[1], v_both[1])
    sp_own, sp_far = rim_conv(z, slots, tissue, inbox, inner, kernel, ready)
    g_own, block_own, block_far, keep, send = block_pass(
        z, (sp_own, swap_sub(sp_far)), rows_both, w_in_both, w_out_both, v_both
    )
    received = swap_sub(send)
    inbox2 = exchange_tiles(z, second_strips(z, slots, g_own, keep, received))
    taps = filter_gradient(z, slots, tissue, inbox, tile_data, g_own, received, scale)
    inner2, block_out = second_inner(
        z, g_own, received, (block_own, swap_sub(block_far)), cotangent, kernel
    )
    if z.paired:
        taps_both = (taps, swap_tiles(z, taps, 1))
        message = share_message(z, inbox2, taps_both, (inner2,))
        steps = range(2, z.owners, 2)
        messages = [message] + [swap_tiles(z, message, step) for step in steps]
        own = column(z, messages)
        far = swap_tiles(z, own, 1)
        tile_grad, grad_kernel = second_rim(
            z, slots, tissue, inbox2, inner2, kernel, messages, (own,)
        )
        grad_in, grad_out = finish_columns(z, own, far, scale)
    else:
        taps_own, taps_far = sum_tiles(z, taps)
        inbox3 = exchange_tiles(z, sum_shares(z, inbox2, (taps_own, inner2)))
        tile_grad = second_rim(z, slots, tissue, inbox2, inner2, kernel, (), ())
        grad_in, grad_out, grad_kernel = finish(z, inbox3, (taps_own, taps_far), scale)
    return block_out, tile_grad, grad_in, grad_out.T, grad_kernel


def solution(mesh):
    placed = (
        P(("slides", "tiles"), None, None, "sub"),
        P(("slides", "tiles"), None, None, "sub"),
        P(("slides", "tiles"), None),
        P(("slides", "tiles"), None),
        P(None, None, "sub"),
        P("sub"),
        P("sub"),
        P("sub"),
        P(None, "sub"),
        P("sub"),
        P("sub", None),
        P("sub"),
        P("sub"),
    )
    return jax.shard_map(
        local,
        mesh=mesh,
        in_specs=placed,
        out_specs=(
            P(("slides", "tiles"), None, None, "sub"),
            P(("slides", "tiles"), None, None, "sub"),
            P("slides", "sub"),
            P(("slides", "sub"), None),
            P("slides", None, "sub"),
        ),
        check_vma=False,
    )
```

```python
import math

import jax
import jax.numpy as jnp
from jax import lax
from jax.experimental import pallas as pl
from jax.experimental.pallas import tpu as pltpu
from jax.sharding import PartitionSpec as P

eps_norm = 1e-06
root_half = 0.7071067811865476
inv_root_tau = 0.3989422804014327
served_kind = (1, 0, 3, 2, 1, 1, 0, 0)
opposite = (1, 0, 3, 2, 7, 6, 5, 4)
LANES = 128
FIRST_VMEM = 60
F32 = jnp.float32
BF16 = jnp.bfloat16


def round_up(value, step):
    return -(-value // step) * step


def call(body, outs, operands, scalars=0, scratch=(), flops=0, vmem=16, after=(), **specs):
    spaces = specs.pop("spaces", None)
    if spaces is None:
        spaces = [pltpu.SMEM] * scalars + [pltpu.VMEM] * (len(operands) - scalars)
    count = len(operands)
    stop = count + len(after)

    def run(*refs):
        body(*refs[:count], *refs[stop:])

    return pl.pallas_call(
        run,
        out_shape=outs,
        in_specs=[pl.BlockSpec(memory_space=space) for space in [*spaces, *[pl.ANY] * len(after)]],
        scratch_shapes=list(scratch),
        compiler_params=pltpu.CompilerParams(vmem_limit_bytes=vmem << 20),
        cost_estimate=pl.CostEstimate(
            flops=flops,
            transcendentals=0,
            bytes_accessed=sum(o.size * o.dtype.itemsize for o in operands),
        ),
        **specs,
    )(*operands, *after)


def shaped(shape, dtype):
    return jax.ShapeDtypeStruct(shape, dtype)


class Sizes:
    def __init__(self, tile_shape, hidden, owners):
        self.tiles, self.side, _, self.ch = tile_shape
        self.hidden = hidden
        self.owners = owners
        self.capacity = max(2, 8 * self.tiles // owners)
        self.links = 8 * self.tiles
        self.pixels = self.side * self.side
        self.rows = self.pixels * self.tiles
        self.half = self.rows // 2
        self.extra = LANES - self.ch
        self.groups = self.ch // self.extra
        self.strip = 3 * self.side * self.ch // LANES
        self.tail = 3 * self.side - self.strip
        self.far = self.side + 3
        self.wide = self.side + 6
        self.box1 = round_up(self.capacity * self.strip, 8)
        self.weight_rows = 2 * (2 * self.ch) * hidden // LANES
        self.share = self.weight_rows // owners
        self.halo_at = round_up(self.share, 8)
        self.box2 = round_up(self.halo_at + self.capacity * self.strip, 8)
        self.box3 = round_up(self.share, 8)
        self.taps_at = round_up(self.share, 16)
        self.message = round_up(self.taps_at + 49, 16)
        self.paired = owners == 8

    def owner_of(self, link):
        factor = -(-65536 // self.tiles)
        assert self.owners * self.tiles * (factor * self.tiles - 65536) < 65536
        return (link * factor) >> 16


def rank_links(z, neighbour, counts, slots):
    @pl.loop(0, z.owners)
    def _(owner):
        counts[owner] = 0

    for link in range(z.links):
        owner = z.owner_of(neighbour[link // 8, link % 8])
        rank = counts[owner]
        counts[owner] = rank + 1
        slots[link] = owner
        slots[z.links + link] = jnp.minimum(rank, z.capacity - 1)
    for link in range(z.links):
        slot = neighbour[link // 8, link % 8] - slots[link] * z.tiles
        slots[2 * z.links + link] = slots[z.links + slot * 8 + opposite[link % 8]]


def pack_strips(z, load_row, load_col, slots, strips, outbox, box, offset):
    direct = z.strip - 2 * z.side
    for tile in range(z.tiles):
        for kind in range(4):
            base = (tile * 4 + kind) * 32
            for line in range(3):
                place = z.side - 3 + line if kind in (0, 2) else line
                value = load_row(tile, place) if kind < 2 else load_col(tile, place)
                start = base + line * z.side
                if line < 2:
                    strips[start : start + z.side, 0 : z.ch] = value
                    continue
                strips[start : start + direct, 0 : z.ch] = value[0:direct]
                for group in range(z.groups):
                    low = base + group * z.tail
                    strips[low : low + z.tail, z.ch : LANES] = value[
                        direct:, group * z.extra : (group + 1) * z.extra
                    ]
    for link in range(z.links):
        base = (link // 8 * 4 + served_kind[link % 8]) * 32
        low = slots[link] * box + offset + slots[2 * z.links + link] * z.strip
        outbox[pl.ds(low, z.strip), :] = strips[base : base + z.strip, :]


def assemble(z, inbox, box, offset, slots, tissue, flat, grown):
    pitch = z.wide * 8
    for link in range(z.links):
        low = slots[link] * box + offset + slots[z.links + link] * z.strip
        value = inbox[pl.ds(low, z.strip), :]
        value = jnp.where(tissue[link // 8, link % 8] > 0, value, 0.0)
        base = link * 40
        flat[base : base + z.strip, :] = value[:, 0 : z.ch]
        low = base + z.strip
        for group in range(z.groups):
            flat[low : low + z.tail, group * z.extra : (group + 1) * z.extra] = value[
                group * z.tail : (group + 1) * z.tail, z.ch : LANES
            ]
    far = z.far
    for tile in range(z.tiles):
        for side in range(8):
            base = (tile * 8 + side) * 40
            for line in range(3):
                start = base + line * z.side
                if side in (0, 1):
                    row = line if side == 0 else far + line
                    spot = pl.ds((row * z.wide + 3) * 8 + tile, z.side, stride=8)
                    grown[spot, :] = flat[start : start + z.side, :]
                elif side in (2, 3):
                    col = line if side == 2 else far + line
                    spot = pl.ds((3 * z.wide + col) * 8 + tile, z.side, stride=pitch)
                    grown[spot, :] = flat[start : start + z.side, :]
                else:
                    row = line if side in (4, 5) else far + line
                    col = 0 if side in (4, 6) else far
                    start += z.side - 3 if side in (4, 6) else 0
                    spot = pl.ds((row * z.wide + col) * 8 + tile, 3, stride=8)
                    grown[spot, :] = flat[start : start + 3, :]


def inner_spot(z, tile, row):
    return pl.ds(((row + 3) * z.wide + 3) * 8 + tile, z.side, stride=8)


def fill_inner(z, grown, tile_data):
    for tile in range(z.tiles):
        for row in range(z.side):
            grown[inner_spot(z, tile, row), :] = tile_data[tile, row].astype(F32)


def conv_row(z, grown, taps, row, start, flipped):
    line = z.wide * 8
    total = start
    for a in range(7):
        band = grown[pl.ds(pl.multiple_of((row + a) * line, 8), line), :]
        for b in range(7):
            tap = taps[6 - a, 6 - b : 7 - b, :] if flipped else taps[a, b : b + 1, :]
            total = total + band[b * 8 : (b + z.side) * 8] * tap
    return total


def rim_row(z, grown, taps, row, start, flipped):
    total = start
    inner = []

    def tap(a, b):
        return taps[6 - a, 6 - b : 7 - b, :] if flipped else taps[a, b : b + 1, :]

    for a in range(7):
        at = (row + a) * z.wide * 8
        if 3 <= row + a < z.far:
            inner.append((a, at))
            continue
        for b in range(7):
            low = at + b * 8
            total = total + grown[low : low + z.side * 8, :] * tap(a, b)
    pieces = [total[col * 8 : (col + 1) * 8] for col in range(z.side)]
    for a, at in inner:
        for col in range(z.side):
            for b in range(7):
                if col + b < 3 or col + b >= z.far:
                    low = at + (col + b) * 8
                    pieces[col] = pieces[col] + grown[low : low + 8, :] * tap(a, b)
    return pieces


def field(z):
    return pltpu.VMEM((z.wide * z.wide * 8 + 256, z.ch), F32)


def boxes(z, box):
    return pltpu.VMEM((z.owners * box, LANES), F32)


def flat_strips(z):
    return pltpu.VMEM((z.links * 40 + 8, z.ch), F32)


def packed_strips(z):
    return pltpu.VMEM((z.tiles * 4 * 32 + 8, LANES), F32)


def pixel_major(z):
    return pltpu.VMEM((z.rows + 320, z.ch), F32)


def first_strips(z, neighbour, tile_data):
    def body(neighbour_hbm, tile_hbm, out, slots, neighbour, tile_data, sems, counts, plain, strips, box):
        fetch_links = pltpu.make_async_copy(neighbour_hbm, neighbour, sems.at[0])
        fetch_tiles = pltpu.make_async_copy(tile_hbm, tile_data, sems.at[1])
        fetch_links.start()
        fetch_tiles.start()
        fetch_links.wait()
        rank_links(z, neighbour, counts, slots)
        fetch_tiles.wait()
        for tile in range(z.tiles):
            for row in range(z.side):
                at = (tile * z.side + row) * z.side
                plain[at : at + z.side, :] = tile_data[tile, row].astype(F32)

        def load_row(tile, row):
            return plain[pl.ds((tile * z.side + row) * z.side, z.side), :]

        def load_col(tile, col):
            return plain[pl.ds(tile * z.pixels + col, z.side, stride=z.side), :]

        pack_strips(z, load_row, load_col, slots, strips, box, z.box1, 0)
        out[...] = box[...].astype(BF16)

    rows = z.owners * z.box1
    return call(
        body,
        (shaped((rows, LANES), BF16), shaped((3 * z.links,), jnp.int32)),
        [neighbour, tile_data],
        spaces=[pl.ANY, pl.ANY],
        vmem=FIRST_VMEM,
        out_specs=(
            pl.BlockSpec(memory_space=pltpu.VMEM),
            pl.BlockSpec(memory_space=pltpu.SMEM),
        ),
        scratch=[
            pltpu.SMEM(neighbour.shape, jnp.int32),
            pltpu.VMEM(tile_data.shape, BF16),
            pltpu.SemaphoreType.DMA((2,)),
            pltpu.SMEM((z.owners,), jnp.int32),
            pixel_major(z),
            packed_strips(z),
            boxes(z, z.box1),
        ],
    )


def local_part(z, slots, tile_data, cotangent, taps, conv_bias):
    def body(slots, tile_data, cotangent, taps, bias, keep, send, out, links, work, grown):
        for place in range(3 * z.links):
            links[place] = slots[place]
        core = lax.axis_index("sub")
        for which, block in enumerate((tile_data, cotangent)):
            for tile in range(z.tiles):
                for row in range(z.side):
                    spot = pl.ds(row * z.side * z.tiles + tile, z.side, stride=z.tiles)
                    work[spot, :] = block[tile, row].astype(F32)
            at = which * z.half
            own = pl.multiple_of(core * z.half, 16)
            far = pl.multiple_of((1 - core) * z.half, 16)
            for ref, half in ((keep, own), (send, far)):
                ref[at : at + z.half, 0 : z.ch] = work[pl.ds(half, z.half), :].astype(BF16)
                ref[at : at + z.half, z.ch : LANES] = jnp.zeros((z.half, z.extra), BF16)
        grown[...] = jnp.zeros_like(grown)
        fill_inner(z, grown, tile_data)
        start = jnp.broadcast_to(bias[...], (z.side * 8, z.ch))

        @pl.loop(0, z.side)
        def _(row):
            total = conv_row(z, grown, taps, row, start, False)
            out[pl.ds(pl.multiple_of(row * z.side * 8, 8), z.side * 8), :] = total

    rows = shaped((2 * z.half, LANES), BF16)
    return call(
        body,
        (rows, rows, shaped((z.pixels * 8, z.ch), F32), shaped(slots.shape, jnp.int32)),
        [slots, tile_data, cotangent, taps, conv_bias],
        1,
        scratch=[pixel_major(z), field(z)],
        out_specs=tuple(
            pl.BlockSpec(memory_space=space) for space in [pltpu.VMEM] * 3 + [pltpu.SMEM]
        ),
        flops=2 * 49 * z.rows * z.ch,
    )


def rim_conv(z, slots, tissue, inbox, inner, taps, after):
    def body(slots, tissue, inbox, inner, taps, own, far, box, flat, grown, whole):
        core = lax.axis_index("sub")
        box[...] = inbox[...].astype(F32)
        assemble(z, box, z.box1, 0, slots, tissue, flat, grown)
        for row in range(z.side):
            start = inner[row * z.side * 8 : (row + 1) * z.side * 8, :]
            for col, piece in enumerate(rim_row(z, grown, taps, row, start, False)):
                at = (row * z.side + col) * z.tiles
                whole[at : at + z.tiles, :] = piece[0 : z.tiles]
        for out, half in ((own, core), (far, 1 - core)):
            out[:, 0 : z.ch] = whole[pl.ds(pl.multiple_of(half * z.half, 8), z.half), :]
            out[:, z.ch : LANES] = jnp.zeros((z.half, z.extra), F32)

    out = shaped((z.half, LANES), F32)
    return call(
        body,
        (out, out),
        [slots, tissue, inbox, inner, taps],
        2,
        [boxes(z, z.box1), flat_strips(z), field(z), pixel_major(z)],
        after=after,
    )


ACROSS = (((1,), (1,)), ((), ()))
DOWN = (((0,), (0,)), ((), ()))


def arrange_weights(z, w_in, w_out):
    hid = z.hidden

    def body(w_in, w_out, in_mine, out_mine, in_theirs, out_theirs):
        first = lax.axis_index("sub") == 0
        for w, mine, theirs in ((w_in, in_mine, in_theirs), (w_out, out_mine, out_theirs)):
            low, high = w[0 : z.ch, :], w[z.ch : 2 * z.ch, :]
            own = jnp.where(first, low, high).astype(BF16)
            far = jnp.where(first, high, low).astype(BF16)
            empty = jnp.zeros((z.extra, hid), BF16)
            for out, blocks in ((mine, (own, far)), (theirs, (far, own))):
                for place, block in enumerate(blocks):
                    at = place * LANES
                    out[at : at + z.ch, :] = block
                    out[at + z.ch : at + LANES, :] = empty

    return call(body, (shaped((2 * LANES, hid), BF16),) * 4, [w_in, w_out])


def block_pass(z, spatial, rows, w_in, w_out, vectors):
    hid = z.hidden
    wide = 2 * LANES
    every = 2 * z.ch

    def body(sp_own, sp_far, row_own, row_far, wi_own, wi_far, wo_own, wo_far, v_own, v_far,
             g_own, block_own, block_far, keep, send, normed_s, branch_s, pre_s, gact_s, act_s,
             gpre_s, xhat_s, inv_s):
        def vector(index):
            at = index * z.ch
            empty = jnp.zeros((1, z.extra), F32)
            own, far = v_own[:, at : at + z.ch], v_far[:, at : at + z.ch]
            return jnp.concatenate([own, empty, far, empty], axis=1)

        gain, shift, b_out, layer_scale = [vector(index) for index in range(4)]
        lanes = lax.broadcasted_iota(jnp.int32, (1, wide), 1)
        flat = jnp.concatenate([sp_own[...], sp_far[...]], axis=1)
        centre = flat - jnp.sum(flat, axis=1, keepdims=True) * (1.0 / every)
        centre = jnp.where(lanes % LANES < z.ch, centre, 0.0)
        var = jnp.sum(centre * centre, axis=1, keepdims=True) * (1.0 / every)
        inverse = lax.rsqrt(var + eps_norm)
        xhat = centre * inverse
        xhat_s[...] = xhat
        inv_s[...] = inverse
        normed_s[...] = (xhat * gain + shift).astype(BF16)
        normed = normed_s[...]
        cot = jnp.concatenate([row_own[z.half :, :], row_far[z.half :, :]], axis=1)
        branch_s[...] = (layer_scale * cot.astype(F32)).astype(BF16)
        g_branch = branch_s[...]
        for side, (wi, wo, vec) in enumerate(((wi_own, wo_own, v_own), (wi_far, wo_far, v_far))):
            at = side * hid
            b_in = vec[:, 4 * z.ch : 4 * z.ch + hid]
            pre_s[:, at : at + hid] = jnp.dot(normed, wi[...], preferred_element_type=F32) + b_in
            gact_s[:, at : at + hid] = jnp.dot(g_branch, wo[...], preferred_element_type=F32)

        @pl.loop(0, z.half // 48, unroll=1)
        def _(step):
            spot = pl.ds(pl.multiple_of(step * 48, 48), 48)
            for low in range(0, 2 * hid, 256):
                part = slice(low, low + 256)
                pre = pre_s[spot, part]
                cdf = 0.5 * (1.0 + lax.erf(pre * root_half))
                act_s[spot, part] = (pre * cdf).astype(BF16)
                slope = cdf + pre * jnp.exp(-0.5 * pre * pre) * inv_root_tau
                gpre_s[spot, part] = (gact_s[spot, part] * slope).astype(BF16)

        g_normed = lax.dot_general(
            gpre_s[:, 0:hid], wi_own[...], ACROSS, preferred_element_type=F32
        ) + lax.dot_general(gpre_s[:, hid:], wi_far[...], ACROSS, preferred_element_type=F32)
        xhat = xhat_s[...]
        leading = g_normed * gain
        mean_h = jnp.sum(leading, axis=1, keepdims=True) * (1.0 / every)
        mean_hx = jnp.sum(leading * xhat, axis=1, keepdims=True) * (1.0 / every)
        g_rows = (inv_s[...] * (leading - mean_h - xhat * mean_hx)).astype(BF16)
        g_own[...] = g_rows[:, 0:LANES]
        send[0 : z.half, :] = g_rows[:, LANES:]
        branch = layer_scale * (
            lax.dot_general(act_s[:, 0:hid], wo_own[...], ACROSS, preferred_element_type=F32)
            + lax.dot_general(act_s[:, hid:], wo_far[...], ACROSS, preferred_element_type=F32)
            + b_out
        )
        block_own[...] = (row_own[0 : z.half, :].astype(F32) + branch[:, 0:LANES]).astype(BF16)
        block_far[...] = (row_far[0 : z.half, :].astype(F32) + branch[:, LANES:]).astype(BF16)
        for side in range(2):
            at = side * hid
            ref, low = (keep, 0) if side == 0 else (send, z.half)
            for left, right in ((normed, gpre_s), (g_branch, act_s)):
                grad = lax.dot_general(
                    left, right[:, at : at + hid], DOWN, preferred_element_type=F32
                )
                for group in range(hid // LANES):
                    part = slice(group * LANES, (group + 1) * LANES)
                    for place in (0, LANES) if side == 0 else (LANES, 0):
                        ref[low : low + z.ch, :] = grad[place : place + z.ch, part].astype(ref.dtype)
                        low += z.ch

    rows_out = shaped((z.half, LANES), BF16)
    return call(
        body,
        (
            rows_out,
            rows_out,
            rows_out,
            shaped((z.weight_rows, LANES), F32),
            shaped((z.half + z.weight_rows, LANES), BF16),
        ),
        [*spatial, *rows, *w_in, *w_out, *vectors],
        0,
        [
            pltpu.VMEM((z.half, wide), BF16),
            pltpu.VMEM((z.half, wide), BF16),
            pltpu.VMEM((z.half, 2 * hid), F32),
            pltpu.VMEM((z.half, 2 * hid), F32),
            pltpu.VMEM((z.half, 2 * hid), BF16),
            pltpu.VMEM((z.half, 2 * hid), BF16),
            pltpu.VMEM((z.half, wide), F32),
            pltpu.VMEM((z.half, 1), F32),
        ],
        flops=12 * z.half * wide * 2 * hid,
    )


def both_halves(z, work, own, far):
    core = lax.axis_index("sub")
    work[pl.ds(pl.multiple_of(core * z.half, 16), z.half), :] = own.astype(F32)
    work[pl.ds(pl.multiple_of((1 - core) * z.half, 16), z.half), :] = far.astype(F32)


def second_strips(z, slots, g_own, keep, received):
    def body(slots, g_own, keep, received, out, plain, strips, box):
        both_halves(z, plain, g_own[:, 0 : z.ch], received[0 : z.half, 0 : z.ch])
        for owner in range(z.owners):
            at = owner * z.share
            low = z.half + at
            box[owner * z.box2 : owner * z.box2 + z.share, :] = keep[
                at : at + z.share, :
            ] + received[low : low + z.share, :].astype(F32)

        def load_row(tile, row):
            return plain[pl.ds(row * z.side * z.tiles + tile, z.side, stride=z.tiles), :]

        def load_col(tile, col):
            return plain[pl.ds(col * z.tiles + tile, z.side, stride=z.side * z.tiles), :]

        pack_strips(z, load_row, load_col, slots, strips, box, z.box2, z.halo_at)
        out[...] = box[...].astype(BF16)

    return call(
        body,
        shaped((z.owners * z.box2, LANES), BF16),
        [slots, g_own, keep, received],
        1,
        [pixel_major(z), packed_strips(z), boxes(z, z.box2)],
    )


def filter_gradient(z, slots, tissue, inbox, tile_data, g_own, received, scale):
    def body(slots, tissue, inbox, tile_data, g_own, received, taps, box, flat, grown, plain,
             g_field, sums):
        box[...] = inbox[...].astype(F32)
        assemble(z, box, z.box1, 0, slots, tissue, flat, grown)
        fill_inner(z, grown, tile_data)
        empty = jnp.zeros((z.wide * z.wide, z.ch), F32)
        for tile in range(z.tiles, 8):
            grown[pl.ds(tile, z.wide * z.wide, stride=8), :] = empty
        both_halves(z, plain, g_own[:, 0 : z.ch], received[0 : z.half, 0 : z.ch])
        g_field[...] = jnp.zeros_like(g_field)
        for tile in range(z.tiles):
            g_field[pl.ds(tile, z.pixels, stride=8), :] = plain[
                pl.ds(tile, z.pixels, stride=z.tiles), :
            ]
        sums[...] = jnp.zeros_like(sums)
        line = z.wide * 8

        @pl.loop(0, z.side)
        def _(row):
            g_row = g_field[pl.ds(pl.multiple_of(row * z.side * 8, 8), z.side * 8), :]
            for a in range(7):
                band = grown[pl.ds(pl.multiple_of((row + a) * line, 8), line), :]
                for b in range(7):
                    product = band[b * 8 : (b + z.side) * 8] * g_row
                    total = product[0:8]
                    for col in range(1, z.side):
                        total = total + product[col * 8 : (col + 1) * 8]
                    at = (a * 7 + b) * 8
                    sums[at : at + 8, :] += total

        for a in range(7):
            rows = sums[a * 56 : (a + 1) * 56, :].reshape(7, 8, z.ch)
            taps[a] = jnp.sum(rows, axis=1) * scale

    return call(
        body,
        shaped((7, 7, z.ch), F32),
        [slots, tissue, inbox, tile_data, g_own, received],
        2,
        [
            boxes(z, z.box1),
            flat_strips(z),
            field(z),
            pixel_major(z),
            pltpu.VMEM((z.pixels * 8 + 64, z.ch), F32),
            pltpu.VMEM((49 * 8, z.ch), F32),
        ],
        flops=2 * 49 * z.rows * z.ch,
    )


def sum_shares(z, inbox, after):
    def body(inbox, out):
        total = inbox[0 : z.share, :].astype(F32)
        for owner in range(1, z.owners):
            at = owner * z.box2
            total = total + inbox[at : at + z.share, :].astype(F32)
        share = total.astype(BF16)
        for owner in range(z.owners):
            at = owner * z.box3
            out[at : at + z.share, :] = share

    return call(body, shaped((z.owners * z.box3, LANES), BF16), [inbox], after=after)


def second_inner(z, g_own, received, block, cotangent, taps):
    def body(g_own, received, block_own, block_far, cotangent, taps, out, block_out, plain, grown, cot):
        both_halves(z, plain, block_own[:, 0 : z.ch], block_far[:, 0 : z.ch])
        for tile in range(z.tiles):
            for row in range(z.side):
                spot = pl.ds(row * z.side * z.tiles + tile, z.side, stride=z.tiles)
                block_out[tile, row] = plain[spot, :].astype(BF16)
        both_halves(z, plain, g_own[:, 0 : z.ch], received[0 : z.half, 0 : z.ch])
        grown[...] = jnp.zeros_like(grown)
        for tile in range(z.tiles):
            for row in range(z.side):
                spot = pl.ds(row * z.side * z.tiles + tile, z.side, stride=z.tiles)
                grown[inner_spot(z, tile, row), :] = plain[spot, :]
                spot = pl.ds(row * z.side * 8 + tile, z.side, stride=8)
                cot[spot, :] = cotangent[tile, row].astype(F32)

        @pl.loop(0, z.side)
        def _(row):
            spot = pl.ds(pl.multiple_of(row * z.side * 8, 8), z.side * 8)
            out[spot, :] = conv_row(z, grown, taps, row, cot[spot, :], True)

    return call(
        body,
        (
            shaped((z.pixels * 8, z.ch), F32),
            shaped((z.tiles, z.side, z.side, z.ch), BF16),
        ),
        [g_own, received, *block, cotangent, taps],
        0,
        [pixel_major(z), field(z), pltpu.VMEM((z.pixels * 8 + 64, z.ch), F32)],
        flops=2 * 49 * z.rows * z.ch,
    )


def second_rim(z, slots, tissue, inbox, inner, taps, messages, after):
    count = len(messages)

    def body(slots, tissue, inbox, inner, taps, *refs):
        messages, (out, *refs) = refs[:count], refs[count:]
        if count:
            grad_taps, box, flat, grown, totals, work = refs
            line = lax.axis_index("tiles") // 2
            for step, message in enumerate(messages):
                at = pl.multiple_of(jnp.bitwise_xor(line, step) * 56, 8)
                work[pl.ds(at, 49), :] = message[z.taps_at : z.taps_at + 49, 0 : z.ch].astype(F32)
            for a in range(7):
                total = work[a * 7 : a * 7 + 7, :]
                for place in range(1, count):
                    low = place * 56 + a * 7
                    total = total + work[low : low + 7, :]
                grad_taps[a] = total
        else:
            box, flat, grown, totals = refs
        box[...] = inbox[...].astype(F32)
        assemble(z, box, z.box2, z.halo_at, slots, tissue, flat, grown)
        for row in range(z.side):
            start = inner[row * z.side * 8 : (row + 1) * z.side * 8, :]
            for col, piece in enumerate(rim_row(z, grown, taps, row, start, True)):
                at = (row * z.side + col) * 8
                totals[at : at + 8, :] = piece
            for tile in range(z.tiles):
                spot = pl.ds(row * z.side * 8 + tile, z.side, stride=8)
                out[tile, row] = totals[spot, :].astype(BF16)

    outs = (shaped((z.tiles, z.side, z.side, z.ch), BF16), shaped((7, 7, z.ch), F32))
    scratch = [
        boxes(z, z.box2),
        flat_strips(z),
        field(z),
        pltpu.VMEM((z.pixels * 8 + 64, z.ch), F32),
        pltpu.VMEM((count * 56, z.ch), F32),
    ]
    if not count:
        outs, scratch = outs[0], scratch[:-1]
    return call(
        body, outs, [slots, tissue, inbox, inner, taps, *messages], 2, scratch, after=after
    )


def share_message(z, inbox, taps, after):
    def body(inbox, taps_own, taps_far, out):
        total = inbox[0 : z.share, :].astype(F32)
        for owner in range(1, z.owners):
            at = owner * z.box2
            total = total + inbox[at : at + z.share, :].astype(F32)
        out[0 : z.share, :] = total.astype(BF16)
        rows = [taps_own[a] + taps_far[a] for a in range(7)]
        low = z.taps_at
        out[low : low + 49, 0 : z.ch] = jnp.concatenate(rows, axis=0).astype(BF16)

    return call(body, shaped((z.message, LANES), BF16), [inbox, *taps], after=after)


def column(z, messages):
    count = len(messages)

    def body(*refs):
        messages, (out,) = refs[:count], refs[count:]
        line = lax.axis_index("tiles") // 2
        for step, message in enumerate(messages):
            at = pl.multiple_of(jnp.bitwise_xor(line, step) * z.share, 16)
            out[pl.ds(at, z.share), :] = message[0 : z.share, :]

    return call(body, shaped((count * z.share, LANES), BF16), messages)


def finish_share(z, grads, owner, share):
    core = lax.axis_index("sub")
    wide = 2 * z.ch
    groups = z.hidden // LANES
    row, stop = owner * z.share, (owner + 1) * z.share
    while row < stop:
        group, place = divmod(row, wide)
        side, place = divmod(place, z.ch)
        count = min(stop - row, z.ch - place)
        at = row - owner * z.share
        block = core if side == 0 else 1 - core
        spot = pl.ds(pl.multiple_of(block * z.ch, 8) + place, count)
        low = group % groups * LANES
        grads[group // groups][spot, low : low + LANES] = share(at, count)
        row += count


def finish(z, inbox, taps, scale):
    groups = z.hidden // LANES

    def body(inbox, taps_own, taps_far, grad_in, grad_out, grad_taps, work):
        grad_taps[...] = taps_own[...] + taps_far[...]
        for owner in range(z.owners):
            at = owner * z.box3
            work[owner * z.share : (owner + 1) * z.share, :] = (
                inbox[at : at + z.share, :].astype(F32) * scale
            )
        core = lax.axis_index("sub")
        for index, grad in enumerate((grad_in, grad_out)):
            for group in range(groups):
                for side, block in enumerate((core, 1 - core)):
                    low = ((index * groups + group) * 2 + side) * z.ch
                    spot = pl.ds(pl.multiple_of(block * z.ch, 8), z.ch)
                    lanes = slice(group * LANES, (group + 1) * LANES)
                    grad[spot, lanes] = work[low : low + z.ch, :]

    out = shaped((2 * z.ch, z.hidden), F32)
    return call(
        body,
        (out, out, shaped((7, 7, z.ch), F32)),
        [inbox, *taps],
        scratch=[pltpu.VMEM((z.weight_rows, LANES), F32)],
    )


def finish_columns(z, own, far, scale):
    def body(own, far, grad_in, grad_out):
        first = lax.axis_index("tiles") % 2 == 0
        for owner in range(z.owners):

            def share(at, count, owner=owner):
                low = owner // 2 * z.share + at
                mine = own[low : low + count, :].astype(F32)
                other = far[low : low + count, :].astype(F32)
                pair = (mine, other) if owner % 2 == 0 else (other, mine)
                return jnp.where(first, *pair) * scale

            finish_share(z, (grad_in, grad_out), owner, share)

    out = shaped((2 * z.ch, z.hidden), F32)
    return call(body, (out, out), [own, far])


def exchange_tiles(z, box):
    boxes = box.reshape(z.owners, -1, LANES)
    return lax.all_to_all(boxes, "tiles", split_axis=0, concat_axis=0, tiled=True).reshape(box.shape)


def swap_sub(piece):
    return lax.ppermute(piece, "sub", [(0, 1), (1, 0)])


def swap_tiles(z, piece, step):
    pairs = [(owner, owner ^ step) for owner in range(z.owners)]
    return lax.ppermute(piece, "tiles", pairs)


def sum_tiles(z, part):
    step = 1
    while True:
        other = swap_tiles(z, part, step)
        step *= 2
        if step == z.owners:
            return part, other
        part = part + other


def local(
    tile_data,
    cotangent,
    neighbour,
    tissue,
    kernel,
    conv_bias,
    layer_norm_gain,
    layer_norm_bias,
    w_in,
    b_in,
    w_out,
    b_out,
    layer_scale,
):
    z = Sizes(tile_data.shape, w_in.shape[1], lax.axis_size("tiles"))
    scale = 1.0 / math.sqrt(z.owners * z.rows)

    outbox, slots = first_strips(z, neighbour, tile_data)
    inbox = exchange_tiles(z, outbox)

    in_mine, out_mine, in_theirs, out_theirs = arrange_weights(z, w_in, w_out.T)
    vectors = jnp.concatenate([layer_norm_gain, layer_norm_bias, b_out, layer_scale, b_in])
    vectors = vectors.reshape(1, -1)
    rows_keep, rows_send, inner, slots = local_part(
        z, slots, tile_data, cotangent, kernel, conv_bias.reshape(1, z.ch)
    )
    w_in_both = (in_mine, swap_sub(in_theirs))
    w_out_both = (out_mine, swap_sub(out_theirs))
    v_both = (vectors, swap_sub(vectors))
    rows_both = (rows_keep, swap_sub(rows_send))
    ready = (rows_both[1], w_in_both[1], w_out_both[1], v_both[1])
    sp_own, sp_far = rim_conv(z, slots, tissue, inbox, inner, kernel, ready)
    g_own, block_own, block_far, keep, send = block_pass(
        z, (sp_own, swap_sub(sp_far)), rows_both, w_in_both, w_out_both, v_both
    )
    received = swap_sub(send)
    inbox2 = exchange_tiles(z, second_strips(z, slots, g_own, keep, received))
    taps = filter_gradient(z, slots, tissue, inbox, tile_data, g_own, received, scale)
    inner2, block_out = second_inner(
        z, g_own, received, (block_own, swap_sub(block_far)), cotangent, kernel
    )
    if z.paired:
        taps_both = (taps, swap_tiles(z, taps, 1))
        message = share_message(z, inbox2, taps_both, (inner2,))
        steps = range(2, z.owners, 2)
        messages = [message] + [swap_tiles(z, message, step) for step in steps]
        own = column(z, messages)
        far = swap_tiles(z, own, 1)
        tile_grad, grad_kernel = second_rim(
            z, slots, tissue, inbox2, inner2, kernel, messages, (own,)
        )
        grad_in, grad_out = finish_columns(z, own, far, scale)
    else:
        taps_own, taps_far = sum_tiles(z, taps)
        inbox3 = exchange_tiles(z, sum_shares(z, inbox2, (taps_own, inner2)))
        tile_grad = second_rim(z, slots, tissue, inbox2, inner2, kernel, (), ())
        grad_in, grad_out, grad_kernel = finish(z, inbox3, (taps_own, taps_far), scale)
    return block_out, tile_grad, grad_in, grad_out.T, grad_kernel


def solution(mesh):
    placed = (
        P(("slides", "tiles"), None, None, "sub"),
        P(("slides", "tiles"), None, None, "sub"),
        P(("slides", "tiles"), None),
        P(("slides", "tiles"), None),
        P(None, None, "sub"),
        P("sub"),
        P("sub"),
        P("sub"),
        P(None, "sub"),
        P("sub"),
        P("sub", None),
        P("sub"),
        P("sub"),
    )
    return jax.shard_map(
        local,
        mesh=mesh,
        in_specs=placed,
        out_specs=(
            P(("slides", "tiles"), None, None, "sub"),
            P(("slides", "tiles"), None, None, "sub"),
            P("slides", "sub"),
            P(("slides", "sub"), None),
            P("slides", None, "sub"),
        ),
        check_vma=False,
    )
```

```python
import math

import jax
import jax.numpy as jnp
from jax import lax
from jax.experimental import pallas as pl
from jax.experimental.pallas import tpu as pltpu
from jax.sharding import PartitionSpec as P

eps_norm = 1e-06
root_half = 0.7071067811865476
inv_root_tau = 0.3989422804014327
served_kind = (1, 0, 3, 2, 1, 1, 0, 0)
opposite = (1, 0, 3, 2, 7, 6, 5, 4)
LANES = 128
FIRST_VMEM = 60
F32 = jnp.float32
BF16 = jnp.bfloat16


def round_up(value, step):
    return -(-value // step) * step


def call(body, outs, operands, scalars=0, scratch=(), flops=0, vmem=16, after=(), **specs):
    spaces = specs.pop("spaces", None)
    if spaces is None:
        spaces = [pltpu.SMEM] * scalars + [pltpu.VMEM] * (len(operands) - scalars)
    count = len(operands)
    stop = count + len(after)

    def run(*refs):
        body(*refs[:count], *refs[stop:])

    return pl.pallas_call(
        run,
        out_shape=outs,
        in_specs=[pl.BlockSpec(memory_space=space) for space in [*spaces, *[pl.ANY] * len(after)]],
        scratch_shapes=list(scratch),
        compiler_params=pltpu.CompilerParams(vmem_limit_bytes=vmem << 20),
        cost_estimate=pl.CostEstimate(
            flops=flops,
            transcendentals=0,
            bytes_accessed=sum(o.size * o.dtype.itemsize for o in operands),
        ),
        **specs,
    )(*operands, *after)


def shaped(shape, dtype):
    return jax.ShapeDtypeStruct(shape, dtype)


class Sizes:
    def __init__(self, tile_shape, hidden, owners):
        self.tiles, self.side, _, self.ch = tile_shape
        self.hidden = hidden
        self.owners = owners
        self.capacity = max(2, 8 * self.tiles // owners)
        self.links = 8 * self.tiles
        self.pixels = self.side * self.side
        self.rows = self.pixels * self.tiles
        self.half = self.rows // 2
        self.extra = LANES - self.ch
        self.groups = self.ch // self.extra
        self.strip = 3 * self.side * self.ch // LANES
        self.tail = 3 * self.side - self.strip
        self.far = self.side + 3
        self.wide = self.side + 6
        self.box1 = round_up(self.capacity * self.strip, 8)
        self.weight_rows = 2 * (2 * self.ch) * hidden // LANES
        self.share = self.weight_rows // owners
        self.halo_at = round_up(self.share, 8)
        self.box2 = round_up(self.halo_at + self.capacity * self.strip, 8)
        self.box3 = round_up(self.share, 8)
        self.taps_at = round_up(self.share, 16)
        self.message = self.taps_at + 40
        self.paired = owners == 8

    def owner_of(self, link):
        factor = -(-65536 // self.tiles)
        assert self.owners * self.tiles * (factor * self.tiles - 65536) < 65536
        return (link * factor) >> 16


def rank_links(z, neighbour, counts, slots):
    @pl.loop(0, z.owners)
    def _(owner):
        counts[owner] = 0

    for link in range(z.links):
        owner = z.owner_of(neighbour[link // 8, link % 8])
        rank = counts[owner]
        counts[owner] = rank + 1
        slots[link] = owner
        slots[z.links + link] = jnp.minimum(rank, z.capacity - 1)
    for link in range(z.links):
        slot = neighbour[link // 8, link % 8] - slots[link] * z.tiles
        slots[2 * z.links + link] = slots[z.links + slot * 8 + opposite[link % 8]]


def pack_strips(z, load_row, load_col, slots, strips, outbox, box, offset):
    direct = z.strip - 2 * z.side
    for tile in range(z.tiles):
        for kind in range(4):
            base = (tile * 4 + kind) * 32
            for line in range(3):
                place = z.side - 3 + line if kind in (0, 2) else line
                value = load_row(tile, place) if kind < 2 else load_col(tile, place)
                start = base + line * z.side
                if line < 2:
                    strips[start : start + z.side, 0 : z.ch] = value
                    continue
                strips[start : start + direct, 0 : z.ch] = value[0:direct]
                for group in range(z.groups):
                    low = base + group * z.tail
                    strips[low : low + z.tail, z.ch : LANES] = value[
                        direct:, group * z.extra : (group + 1) * z.extra
                    ]
    for link in range(z.links):
        base = (link // 8 * 4 + served_kind[link % 8]) * 32
        low = slots[link] * box + offset + slots[2 * z.links + link] * z.strip
        outbox[pl.ds(low, z.strip), :] = strips[base : base + z.strip, :]


def assemble(z, inbox, box, offset, slots, tissue, flat, grown):
    pitch = z.wide * 8
    for link in range(z.links):
        low = slots[link] * box + offset + slots[z.links + link] * z.strip
        value = inbox[pl.ds(low, z.strip), :]
        value = jnp.where(tissue[link // 8, link % 8] > 0, value, 0.0)
        base = link * 40
        flat[base : base + z.strip, :] = value[:, 0 : z.ch]
        low = base + z.strip
        for group in range(z.groups):
            flat[low : low + z.tail, group * z.extra : (group + 1) * z.extra] = value[
                group * z.tail : (group + 1) * z.tail, z.ch : LANES
            ]
    far = z.far
    for tile in range(z.tiles):
        for side in range(8):
            base = (tile * 8 + side) * 40
            for line in range(3):
                start = base + line * z.side
                if side in (0, 1):
                    row = line if side == 0 else far + line
                    spot = pl.ds((row * z.wide + 3) * 8 + tile, z.side, stride=8)
                    grown[spot, :] = flat[start : start + z.side, :]
                elif side in (2, 3):
                    col = line if side == 2 else far + line
                    spot = pl.ds((3 * z.wide + col) * 8 + tile, z.side, stride=pitch)
                    grown[spot, :] = flat[start : start + z.side, :]
                else:
                    row = line if side in (4, 5) else far + line
                    col = 0 if side in (4, 6) else far
                    start += z.side - 3 if side in (4, 6) else 0
                    spot = pl.ds((row * z.wide + col) * 8 + tile, 3, stride=8)
                    grown[spot, :] = flat[start : start + 3, :]


def inner_spot(z, tile, row):
    return pl.ds(((row + 3) * z.wide + 3) * 8 + tile, z.side, stride=8)


def fill_inner(z, grown, tile_data):
    for tile in range(z.tiles):
        for row in range(z.side):
            grown[inner_spot(z, tile, row), :] = tile_data[tile, row].astype(F32)


def conv_row(z, grown, taps, row, start, flipped):
    line = z.wide * 8
    total = start
    for a in range(7):
        band = grown[pl.ds(pl.multiple_of((row + a) * line, 8), line), :]
        for b in range(7):
            tap = taps[6 - a, 6 - b : 7 - b, :] if flipped else taps[a, b : b + 1, :]
            total = total + band[b * 8 : (b + z.side) * 8] * tap
    return total


def rim_row(z, grown, taps, row, start, flipped):
    total = start
    inner = []

    def tap(a, b):
        return taps[6 - a, 6 - b : 7 - b, :] if flipped else taps[a, b : b + 1, :]

    for a in range(7):
        at = (row + a) * z.wide * 8
        if 3 <= row + a < z.far:
            inner.append((a, at))
            continue
        for b in range(7):
            low = at + b * 8
            total = total + grown[low : low + z.side * 8, :] * tap(a, b)
    pieces = [total[col * 8 : (col + 1) * 8] for col in range(z.side)]
    for a, at in inner:
        for col in range(z.side):
            for b in range(7):
                if col + b < 3 or col + b >= z.far:
                    low = at + (col + b) * 8
                    pieces[col] = pieces[col] + grown[low : low + 8, :] * tap(a, b)
    return pieces


def field(z):
    return pltpu.VMEM((z.wide * z.wide * 8 + 256, z.ch), F32)


def boxes(z, box):
    return pltpu.VMEM((z.owners * box, LANES), F32)


def flat_strips(z):
    return pltpu.VMEM((z.links * 40 + 8, z.ch), F32)


def packed_strips(z):
    return pltpu.VMEM((z.tiles * 4 * 32 + 8, LANES), F32)


def pixel_major(z):
    return pltpu.VMEM((z.rows + 320, z.ch), F32)


def first_strips(z, neighbour, tile_data):
    def body(neighbour_hbm, tile_hbm, out, slots, neighbour, tile_data, sems, counts, plain, strips, box):
        fetch_links = pltpu.make_async_copy(neighbour_hbm, neighbour, sems.at[0])
        fetch_tiles = pltpu.make_async_copy(tile_hbm, tile_data, sems.at[1])
        fetch_links.start()
        fetch_tiles.start()
        fetch_links.wait()
        rank_links(z, neighbour, counts, slots)
        fetch_tiles.wait()
        for tile in range(z.tiles):
            for row in range(z.side):
                at = (tile * z.side + row) * z.side
                plain[at : at + z.side, :] = tile_data[tile, row].astype(F32)

        def load_row(tile, row):
            return plain[pl.ds((tile * z.side + row) * z.side, z.side), :]

        def load_col(tile, col):
            return plain[pl.ds(tile * z.pixels + col, z.side, stride=z.side), :]

        pack_strips(z, load_row, load_col, slots, strips, box, z.box1, 0)
        out[...] = box[...].astype(BF16)

    rows = z.owners * z.box1
    return call(
        body,
        (shaped((rows, LANES), BF16), shaped((3 * z.links,), jnp.int32)),
        [neighbour, tile_data],
        spaces=[pl.ANY, pl.ANY],
        vmem=FIRST_VMEM,
        out_specs=(
            pl.BlockSpec(memory_space=pltpu.VMEM),
            pl.BlockSpec(memory_space=pltpu.SMEM),
        ),
        scratch=[
            pltpu.SMEM(neighbour.shape, jnp.int32),
            pltpu.VMEM(tile_data.shape, BF16),
            pltpu.SemaphoreType.DMA((2,)),
            pltpu.SMEM((z.owners,), jnp.int32),
            pixel_major(z),
            packed_strips(z),
            boxes(z, z.box1),
        ],
    )


def local_part(z, slots, tile_data, cotangent, taps, conv_bias):
    def body(slots, tile_data, cotangent, taps, bias, keep, send, out, links, work, grown):
        for place in range(3 * z.links):
            links[place] = slots[place]
        core = lax.axis_index("sub")
        for which, block in enumerate((tile_data, cotangent)):
            for tile in range(z.tiles):
                for row in range(z.side):
                    spot = pl.ds(row * z.side * z.tiles + tile, z.side, stride=z.tiles)
                    work[spot, :] = block[tile, row].astype(F32)
            at = which * z.half
            own = pl.multiple_of(core * z.half, 16)
            far = pl.multiple_of((1 - core) * z.half, 16)
            for ref, half in ((keep, own), (send, far)):
                ref[at : at + z.half, 0 : z.ch] = work[pl.ds(half, z.half), :].astype(BF16)
                ref[at : at + z.half, z.ch : LANES] = jnp.zeros((z.half, z.extra), BF16)
        grown[...] = jnp.zeros_like(grown)
        fill_inner(z, grown, tile_data)
        start = jnp.broadcast_to(bias[...], (z.side * 8, z.ch))

        @pl.loop(0, z.side)
        def _(row):
            total = conv_row(z, grown, taps, row, start, False)
            out[pl.ds(pl.multiple_of(row * z.side * 8, 8), z.side * 8), :] = total

    rows = shaped((2 * z.half, LANES), BF16)
    return call(
        body,
        (rows, rows, shaped((z.pixels * 8, z.ch), F32), shaped(slots.shape, jnp.int32)),
        [slots, tile_data, cotangent, taps, conv_bias],
        1,
        scratch=[pixel_major(z), field(z)],
        out_specs=tuple(
            pl.BlockSpec(memory_space=space) for space in [pltpu.VMEM] * 3 + [pltpu.SMEM]
        ),
        flops=2 * 49 * z.rows * z.ch,
    )


def rim_conv(z, slots, tissue, inbox, inner, taps, after):
    def body(slots, tissue, inbox, inner, taps, own, far, box, flat, grown, whole):
        core = lax.axis_index("sub")
        box[...] = inbox[...].astype(F32)
        assemble(z, box, z.box1, 0, slots, tissue, flat, grown)
        for row in range(z.side):
            start = inner[row * z.side * 8 : (row + 1) * z.side * 8, :]
            for col, piece in enumerate(rim_row(z, grown, taps, row, start, False)):
                at = (row * z.side + col) * z.tiles
                whole[at : at + z.tiles, :] = piece[0 : z.tiles]
        for out, half in ((own, core), (far, 1 - core)):
            out[:, 0 : z.ch] = whole[pl.ds(pl.multiple_of(half * z.half, 8), z.half), :]
            out[:, z.ch : LANES] = jnp.zeros((z.half, z.extra), F32)

    out = shaped((z.half, LANES), F32)
    return call(
        body,
        (out, out),
        [slots, tissue, inbox, inner, taps],
        2,
        [boxes(z, z.box1), flat_strips(z), field(z), pixel_major(z)],
        after=after,
    )


ACROSS = (((1,), (1,)), ((), ()))
DOWN = (((0,), (0,)), ((), ()))


def arrange_weights(z, w_in, w_out):
    hid = z.hidden

    def body(w_in, w_out, in_mine, out_mine, in_theirs, out_theirs):
        first = lax.axis_index("sub") == 0
        for w, mine, theirs in ((w_in, in_mine, in_theirs), (w_out, out_mine, out_theirs)):
            low, high = w[0 : z.ch, :], w[z.ch : 2 * z.ch, :]
            own = jnp.where(first, low, high).astype(BF16)
            far = jnp.where(first, high, low).astype(BF16)
            empty = jnp.zeros((z.extra, hid), BF16)
            for out, blocks in ((mine, (own, far)), (theirs, (far, own))):
                for place, block in enumerate(blocks):
                    at = place * LANES
                    out[at : at + z.ch, :] = block
                    out[at + z.ch : at + LANES, :] = empty

    return call(body, (shaped((2 * LANES, hid), BF16),) * 4, [w_in, w_out])


def block_pass(z, spatial, rows, w_in, w_out, vectors):
    hid = z.hidden
    wide = 2 * LANES
    every = 2 * z.ch

    def body(sp_own, sp_far, row_own, row_far, wi_own, wi_far, wo_own, wo_far, v_own, v_far,
             g_own, block_own, block_far, keep, send, normed_s, branch_s, pre_s, gact_s, act_s,
             gpre_s, xhat_s, inv_s):
        def vector(index):
            at = index * z.ch
            empty = jnp.zeros((1, z.extra), F32)
            own, far = v_own[:, at : at + z.ch], v_far[:, at : at + z.ch]
            return jnp.concatenate([own, empty, far, empty], axis=1)

        gain, shift, b_out, layer_scale = [vector(index) for index in range(4)]
        lanes = lax.broadcasted_iota(jnp.int32, (1, wide), 1)
        flat = jnp.concatenate([sp_own[...], sp_far[...]], axis=1)
        centre = flat - jnp.sum(flat, axis=1, keepdims=True) * (1.0 / every)
        centre = jnp.where(lanes % LANES < z.ch, centre, 0.0)
        var = jnp.sum(centre * centre, axis=1, keepdims=True) * (1.0 / every)
        inverse = lax.rsqrt(var + eps_norm)
        xhat = centre * inverse
        xhat_s[...] = xhat
        inv_s[...] = inverse
        normed_s[...] = (xhat * gain + shift).astype(BF16)
        normed = normed_s[...]
        cot = jnp.concatenate([row_own[z.half :, :], row_far[z.half :, :]], axis=1)
        branch_s[...] = (layer_scale * cot.astype(F32)).astype(BF16)
        g_branch = branch_s[...]
        for side, (wi, wo, vec) in enumerate(((wi_own, wo_own, v_own), (wi_far, wo_far, v_far))):
            at = side * hid
            b_in = vec[:, 4 * z.ch : 4 * z.ch + hid]
            pre_s[:, at : at + hid] = jnp.dot(normed, wi[...], preferred_element_type=F32) + b_in
            gact_s[:, at : at + hid] = jnp.dot(g_branch, wo[...], preferred_element_type=F32)

        @pl.loop(0, z.half // 48, unroll=1)
        def _(step):
            spot = pl.ds(pl.multiple_of(step * 48, 48), 48)
            for low in range(0, 2 * hid, 256):
                part = slice(low, low + 256)
                pre = pre_s[spot, part]
                cdf = 0.5 * (1.0 + lax.erf(pre * root_half))
                act_s[spot, part] = (pre * cdf).astype(BF16)
                slope = cdf + pre * jnp.exp(-0.5 * pre * pre) * inv_root_tau
                gpre_s[spot, part] = (gact_s[spot, part] * slope).astype(BF16)

        g_normed = lax.dot_general(
            gpre_s[:, 0:hid], wi_own[...], ACROSS, preferred_element_type=F32
        ) + lax.dot_general(gpre_s[:, hid:], wi_far[...], ACROSS, preferred_element_type=F32)
        xhat = xhat_s[...]
        leading = g_normed * gain
        mean_h = jnp.sum(leading, axis=1, keepdims=True) * (1.0 / every)
        mean_hx = jnp.sum(leading * xhat, axis=1, keepdims=True) * (1.0 / every)
        g_rows = (inv_s[...] * (leading - mean_h - xhat * mean_hx)).astype(BF16)
        g_own[...] = g_rows[:, 0:LANES]
        send[0 : z.half, :] = g_rows[:, LANES:]
        branch = layer_scale * (
            lax.dot_general(act_s[:, 0:hid], wo_own[...], ACROSS, preferred_element_type=F32)
            + lax.dot_general(act_s[:, hid:], wo_far[...], ACROSS, preferred_element_type=F32)
            + b_out
        )
        block_own[...] = (row_own[0 : z.half, :].astype(F32) + branch[:, 0:LANES]).astype(BF16)
        block_far[...] = (row_far[0 : z.half, :].astype(F32) + branch[:, LANES:]).astype(BF16)
        for side in range(2):
            at = side * hid
            ref, low = (keep, 0) if side == 0 else (send, z.half)
            for left, right in ((normed, gpre_s), (g_branch, act_s)):
                grad = lax.dot_general(
                    left, right[:, at : at + hid], DOWN, preferred_element_type=F32
                )
                for group in range(hid // LANES):
                    part = slice(group * LANES, (group + 1) * LANES)
                    for place in (0, LANES) if side == 0 else (LANES, 0):
                        ref[low : low + z.ch, :] = grad[place : place + z.ch, part].astype(ref.dtype)
                        low += z.ch

    rows_out = shaped((z.half, LANES), BF16)
    return call(
        body,
        (
            rows_out,
            rows_out,
            rows_out,
            shaped((z.weight_rows, LANES), F32),
            shaped((z.half + z.weight_rows, LANES), BF16),
        ),
        [*spatial, *rows, *w_in, *w_out, *vectors],
        0,
        [
            pltpu.VMEM((z.half, wide), BF16),
            pltpu.VMEM((z.half, wide), BF16),
            pltpu.VMEM((z.half, 2 * hid), F32),
            pltpu.VMEM((z.half, 2 * hid), F32),
            pltpu.VMEM((z.half, 2 * hid), BF16),
            pltpu.VMEM((z.half, 2 * hid), BF16),
            pltpu.VMEM((z.half, wide), F32),
            pltpu.VMEM((z.half, 1), F32),
        ],
        flops=12 * z.half * wide * 2 * hid,
    )


def both_halves(z, work, own, far):
    core = lax.axis_index("sub")
    work[pl.ds(pl.multiple_of(core * z.half, 16), z.half), :] = own.astype(F32)
    work[pl.ds(pl.multiple_of((1 - core) * z.half, 16), z.half), :] = far.astype(F32)


def second_strips(z, slots, g_own, keep, received):
    def body(slots, g_own, keep, received, out, plain, strips, box):
        both_halves(z, plain, g_own[:, 0 : z.ch], received[0 : z.half, 0 : z.ch])
        for owner in range(z.owners):
            at = owner * z.share
            low = z.half + at
            box[owner * z.box2 : owner * z.box2 + z.share, :] = keep[
                at : at + z.share, :
            ] + received[low : low + z.share, :].astype(F32)

        def load_row(tile, row):
            return plain[pl.ds(row * z.side * z.tiles + tile, z.side, stride=z.tiles), :]

        def load_col(tile, col):
            return plain[pl.ds(col * z.tiles + tile, z.side, stride=z.side * z.tiles), :]

        pack_strips(z, load_row, load_col, slots, strips, box, z.box2, z.halo_at)
        out[...] = box[...].astype(BF16)

    return call(
        body,
        shaped((z.owners * z.box2, LANES), BF16),
        [slots, g_own, keep, received],
        1,
        [pixel_major(z), packed_strips(z), boxes(z, z.box2)],
    )


def filter_gradient(z, slots, tissue, inbox, tile_data, g_own, received, scale):
    def body(slots, tissue, inbox, tile_data, g_own, received, taps, box, flat, grown, plain,
             g_field, sums):
        box[...] = inbox[...].astype(F32)
        assemble(z, box, z.box1, 0, slots, tissue, flat, grown)
        fill_inner(z, grown, tile_data)
        empty = jnp.zeros((z.wide * z.wide, z.ch), F32)
        for tile in range(z.tiles, 8):
            grown[pl.ds(tile, z.wide * z.wide, stride=8), :] = empty
        both_halves(z, plain, g_own[:, 0 : z.ch], received[0 : z.half, 0 : z.ch])
        g_field[...] = jnp.zeros_like(g_field)
        for tile in range(z.tiles):
            g_field[pl.ds(tile, z.pixels, stride=8), :] = plain[
                pl.ds(tile, z.pixels, stride=z.tiles), :
            ]
        sums[...] = jnp.zeros_like(sums)
        line = z.wide * 8

        @pl.loop(0, z.side)
        def _(row):
            g_row = g_field[pl.ds(pl.multiple_of(row * z.side * 8, 8), z.side * 8), :]
            for a in range(7):
                band = grown[pl.ds(pl.multiple_of((row + a) * line, 8), line), :]
                for b in range(7):
                    product = band[b * 8 : (b + z.side) * 8] * g_row
                    total = product[0:8]
                    for col in range(1, z.side):
                        total = total + product[col * 8 : (col + 1) * 8]
                    at = (a * 7 + b) * 8
                    sums[at : at + 8, :] += total

        for a in range(7):
            rows = sums[a * 56 : (a + 1) * 56, :].reshape(7, 8, z.ch)
            taps[a] = jnp.sum(rows, axis=1) * scale

    return call(
        body,
        shaped((7, 7, z.ch), F32),
        [slots, tissue, inbox, tile_data, g_own, received],
        2,
        [
            boxes(z, z.box1),
            flat_strips(z),
            field(z),
            pixel_major(z),
            pltpu.VMEM((z.pixels * 8 + 64, z.ch), F32),
            pltpu.VMEM((49 * 8, z.ch), F32),
        ],
        flops=2 * 49 * z.rows * z.ch,
    )


def sum_shares(z, inbox, after):
    def body(inbox, out):
        total = inbox[0 : z.share, :].astype(F32)
        for owner in range(1, z.owners):
            at = owner * z.box2
            total = total + inbox[at : at + z.share, :].astype(F32)
        share = total.astype(BF16)
        for owner in range(z.owners):
            at = owner * z.box3
            out[at : at + z.share, :] = share

    return call(body, shaped((z.owners * z.box3, LANES), BF16), [inbox], after=after)


def second_inner(z, g_own, received, block, cotangent, taps):
    def body(g_own, received, block_own, block_far, cotangent, taps, out, block_out, plain, grown, cot):
        both_halves(z, plain, block_own[:, 0 : z.ch], block_far[:, 0 : z.ch])
        for tile in range(z.tiles):
            for row in range(z.side):
                spot = pl.ds(row * z.side * z.tiles + tile, z.side, stride=z.tiles)
                block_out[tile, row] = plain[spot, :].astype(BF16)
        both_halves(z, plain, g_own[:, 0 : z.ch], received[0 : z.half, 0 : z.ch])
        grown[...] = jnp.zeros_like(grown)
        for tile in range(z.tiles):
            for row in range(z.side):
                spot = pl.ds(row * z.side * z.tiles + tile, z.side, stride=z.tiles)
                grown[inner_spot(z, tile, row), :] = plain[spot, :]
                spot = pl.ds(row * z.side * 8 + tile, z.side, stride=8)
                cot[spot, :] = cotangent[tile, row].astype(F32)

        @pl.loop(0, z.side)
        def _(row):
            spot = pl.ds(pl.multiple_of(row * z.side * 8, 8), z.side * 8)
            out[spot, :] = conv_row(z, grown, taps, row, cot[spot, :], True)

    return call(
        body,
        (
            shaped((z.pixels * 8, z.ch), F32),
            shaped((z.tiles, z.side, z.side, z.ch), BF16),
        ),
        [g_own, received, *block, cotangent, taps],
        0,
        [pixel_major(z), field(z), pltpu.VMEM((z.pixels * 8 + 64, z.ch), F32)],
        flops=2 * 49 * z.rows * z.ch,
    )


def second_rim(z, slots, tissue, inbox, inner, taps, messages, after):
    count = len(messages)

    def body(slots, tissue, inbox, inner, taps, *refs):
        messages, (out, *refs) = refs[:count], refs[count:]
        if count:
            grad_taps, box, flat, grown, totals, work = refs
            line = lax.axis_index("tiles") // 2
            for step, message in enumerate(messages):
                at = pl.multiple_of(jnp.bitwise_xor(line, step) * 56, 8)
                packed = message[z.taps_at : z.taps_at + 40, :].astype(F32)
                work[pl.ds(at, 37), :] = packed[0:37, 0 : z.ch]
                for group in range(z.groups):
                    lanes = slice(group * z.extra, (group + 1) * z.extra)
                    work[pl.ds(at + 37, 12), lanes] = packed[
                        group * 12 : (group + 1) * 12, z.ch : LANES
                    ]
            for a in range(7):
                total = work[a * 7 : a * 7 + 7, :]
                for place in range(1, count):
                    low = place * 56 + a * 7
                    total = total + work[low : low + 7, :]
                grad_taps[a] = total
        else:
            box, flat, grown, totals = refs
        box[...] = inbox[...].astype(F32)
        assemble(z, box, z.box2, z.halo_at, slots, tissue, flat, grown)
        for row in range(z.side):
            start = inner[row * z.side * 8 : (row + 1) * z.side * 8, :]
            for col, piece in enumerate(rim_row(z, grown, taps, row, start, True)):
                at = (row * z.side + col) * 8
                totals[at : at + 8, :] = piece
            for tile in range(z.tiles):
                spot = pl.ds(row * z.side * 8 + tile, z.side, stride=8)
                out[tile, row] = totals[spot, :].astype(BF16)

    outs = (shaped((z.tiles, z.side, z.side, z.ch), BF16), shaped((7, 7, z.ch), F32))
    scratch = [
        boxes(z, z.box2),
        flat_strips(z),
        field(z),
        pltpu.VMEM((z.pixels * 8 + 64, z.ch), F32),
        pltpu.VMEM((count * 56 + 16, z.ch), F32),
    ]
    if not count:
        outs, scratch = outs[0], scratch[:-1]
    return call(
        body, outs, [slots, tissue, inbox, inner, taps, *messages], 2, scratch, after=after
    )


def share_message(z, inbox, taps, after):
    def body(inbox, taps_own, taps_far, out, work):
        total = inbox[0 : z.share, :].astype(F32)
        for owner in range(1, z.owners):
            at = owner * z.box2
            total = total + inbox[at : at + z.share, :].astype(F32)
        out[0 : z.share, :] = total.astype(BF16)
        rows = jnp.concatenate([taps_own[a] + taps_far[a] for a in range(7)], axis=0)
        work[...] = jnp.zeros_like(work)
        work[0:37, 0 : z.ch] = rows[0:37]
        for group in range(z.groups):
            lanes = slice(group * z.extra, (group + 1) * z.extra)
            work[group * 12 : (group + 1) * 12, z.ch : LANES] = rows[37:49, lanes]
        out[z.taps_at : z.taps_at + 40, :] = work[0:40, :].astype(BF16)

    return call(body, shaped((z.message, LANES), BF16), [inbox, *taps], scratch=[pltpu.VMEM((48, LANES), F32)], after=after)


def column(z, messages):
    count = len(messages)

    def body(*refs):
        messages, (out,) = refs[:count], refs[count:]
        line = lax.axis_index("tiles") // 2
        for step, message in enumerate(messages):
            at = pl.multiple_of(jnp.bitwise_xor(line, step) * z.share, 16)
            out[pl.ds(at, z.share), :] = message[0 : z.share, :]

    return call(body, shaped((count * z.share, LANES), BF16), messages)


def finish_share(z, grads, owner, share):
    core = lax.axis_index("sub")
    wide = 2 * z.ch
    groups = z.hidden // LANES
    row, stop = owner * z.share, (owner + 1) * z.share
    while row < stop:
        group, place = divmod(row, wide)
        side, place = divmod(place, z.ch)
        count = min(stop - row, z.ch - place)
        at = row - owner * z.share
        block = core if side == 0 else 1 - core
        spot = pl.ds(pl.multiple_of(block * z.ch, 8) + place, count)
        low = group % groups * LANES
        grads[group // groups][spot, low : low + LANES] = share(at, count)
        row += count


def finish(z, inbox, taps, scale):
    groups = z.hidden // LANES

    def body(inbox, taps_own, taps_far, grad_in, grad_out, grad_taps, work):
        grad_taps[...] = taps_own[...] + taps_far[...]
        for owner in range(z.owners):
            at = owner * z.box3
            work[owner * z.share : (owner + 1) * z.share, :] = (
                inbox[at : at + z.share, :].astype(F32) * scale
            )
        core = lax.axis_index("sub")
        for index, grad in enumerate((grad_in, grad_out)):
            for group in range(groups):
                for side, block in enumerate((core, 1 - core)):
                    low = ((index * groups + group) * 2 + side) * z.ch
                    spot = pl.ds(pl.multiple_of(block * z.ch, 8), z.ch)
                    lanes = slice(group * LANES, (group + 1) * LANES)
                    grad[spot, lanes] = work[low : low + z.ch, :]

    out = shaped((2 * z.ch, z.hidden), F32)
    return call(
        body,
        (out, out, shaped((7, 7, z.ch), F32)),
        [inbox, *taps],
        scratch=[pltpu.VMEM((z.weight_rows, LANES), F32)],
    )


def finish_columns(z, own, far, scale):
    def body(own, far, grad_in, grad_out):
        first = lax.axis_index("tiles") % 2 == 0
        for owner in range(z.owners):

            def share(at, count, owner=owner):
                low = owner // 2 * z.share + at
                mine = own[low : low + count, :].astype(F32)
                other = far[low : low + count, :].astype(F32)
                pair = (mine, other) if owner % 2 == 0 else (other, mine)
                return jnp.where(first, *pair) * scale

            finish_share(z, (grad_in, grad_out), owner, share)

    out = shaped((2 * z.ch, z.hidden), F32)
    return call(body, (out, out), [own, far])


def exchange_tiles(z, box):
    boxes = box.reshape(z.owners, -1, LANES)
    return lax.all_to_all(boxes, "tiles", split_axis=0, concat_axis=0, tiled=True).reshape(box.shape)


def swap_sub(piece):
    return lax.ppermute(piece, "sub", [(0, 1), (1, 0)])


def swap_tiles(z, piece, step):
    pairs = [(owner, owner ^ step) for owner in range(z.owners)]
    return lax.ppermute(piece, "tiles", pairs)


def sum_tiles(z, part):
    step = 1
    while True:
        other = swap_tiles(z, part, step)
        step *= 2
        if step == z.owners:
            return part, other
        part = part + other


def local(
    tile_data,
    cotangent,
    neighbour,
    tissue,
    kernel,
    conv_bias,
    layer_norm_gain,
    layer_norm_bias,
    w_in,
    b_in,
    w_out,
    b_out,
    layer_scale,
):
    z = Sizes(tile_data.shape, w_in.shape[1], lax.axis_size("tiles"))
    scale = 1.0 / math.sqrt(z.owners * z.rows)

    outbox, slots = first_strips(z, neighbour, tile_data)
    inbox = exchange_tiles(z, outbox)

    in_mine, out_mine, in_theirs, out_theirs = arrange_weights(z, w_in, w_out.T)
    vectors = jnp.concatenate([layer_norm_gain, layer_norm_bias, b_out, layer_scale, b_in])
    vectors = vectors.reshape(1, -1)
    rows_keep, rows_send, inner, slots = local_part(
        z, slots, tile_data, cotangent, kernel, conv_bias.reshape(1, z.ch)
    )
    w_in_both = (in_mine, swap_sub(in_theirs))
    w_out_both = (out_mine, swap_sub(out_theirs))
    v_both = (vectors, swap_sub(vectors))
    rows_both = (rows_keep, swap_sub(rows_send))
    ready = (rows_both[1], w_in_both[1], w_out_both[1], v_both[1])
    sp_own, sp_far = rim_conv(z, slots, tissue, inbox, inner, kernel, ready)
    g_own, block_own, block_far, keep, send = block_pass(
        z, (sp_own, swap_sub(sp_far)), rows_both, w_in_both, w_out_both, v_both
    )
    received = swap_sub(send)
    inbox2 = exchange_tiles(z, second_strips(z, slots, g_own, keep, received))
    taps = filter_gradient(z, slots, tissue, inbox, tile_data, g_own, received, scale)
    inner2, block_out = second_inner(
        z, g_own, received, (block_own, swap_sub(block_far)), cotangent, kernel
    )
    if z.paired:
        taps_both = (taps, swap_tiles(z, taps, 1))
        message = share_message(z, inbox2, taps_both, (inner2,))
        steps = range(2, z.owners, 2)
        messages = [message] + [swap_tiles(z, message, step) for step in steps]
        own = column(z, messages)
        far = swap_tiles(z, own, 1)
        tile_grad, grad_kernel = second_rim(
            z, slots, tissue, inbox2, inner2, kernel, messages, (own,)
        )
        grad_in, grad_out = finish_columns(z, own, far, scale)
    else:
        taps_own, taps_far = sum_tiles(z, taps)
        inbox3 = exchange_tiles(z, sum_shares(z, inbox2, (taps_own, inner2)))
        tile_grad = second_rim(z, slots, tissue, inbox2, inner2, kernel, (), ())
        grad_in, grad_out, grad_kernel = finish(z, inbox3, (taps_own, taps_far), scale)
    return block_out, tile_grad, grad_in, grad_out.T, grad_kernel


def solution(mesh):
    placed = (
        P(("slides", "tiles"), None, None, "sub"),
        P(("slides", "tiles"), None, None, "sub"),
        P(("slides", "tiles"), None),
        P(("slides", "tiles"), None),
        P(None, None, "sub"),
        P("sub"),
        P("sub"),
        P("sub"),
        P(None, "sub"),
        P("sub"),
        P("sub", None),
        P("sub"),
        P("sub"),
    )
    return jax.shard_map(
        local,
        mesh=mesh,
        in_specs=placed,
        out_specs=(
            P(("slides", "tiles"), None, None, "sub"),
            P(("slides", "tiles"), None, None, "sub"),
            P("slides", "sub"),
            P(("slides", "sub"), None),
            P("slides", None, "sub"),
        ),
        check_vma=False,
    )
```
